32 devices in a mesh: grp: 4 (over z), grid: 8 (over y, x, core).
Axes of the slice: x: 2, y: 2, z: 4, core: 2. Of those that a mesh axis runs over, the one named last changes fastest.
Arguments:
- vectors: float32 [4, 3, 2, 32, 256, 256], P('grp', None, None, 'grid'), may hold values from -6 to 6
- potential: float32 [32, 256, 256], P('grid'), may hold values from 0.1 to 2
- added_field: float32 [4, 32, 256, 256], P('grp', 'grid'), may hold values from -3 to 3
- qp_states: bfloat16 [32, 32, 256, 256], P(None, 'grid'), may hold values from -0.00390625 to 0.00390625
Outputs:
- elements: float32 [4, 32, 6], P('grp', 'grid')
The draws below stay inside these ranges and needn't reach their ends.
All inputs are finite; a program needn't handle non-finite values.
Results may differ from the reference program's by a relative error of at most 0.0033.
Values sent between devices are 32-bit elements; how exact they have to be, the bound alone decides.
No kernel may reach another device: no remote copies, remote signals or barrier semaphores. Data moves between devices by JAX's collectives and lax.ppermute only.
A program may use at most 256 MiB of HBM per device.

```python
import math
import jax
import jax.numpy as jnp
from jax import lax

NY = 256
NZ = 256
NV = 3
NQ = 32
ORDER = 4
NX = 32
N_GRP = 4


def shard_levels(stream_key, shape, cuts, low, largest):
    loudness, own = 1.0, jax.random.fold_in(stream_key, 6)
    for position, blocks in cuts:
        draws = jnp.exp(jax.random.uniform(jax.random.fold_in(own, position), (blocks,), jnp.float32, low / len(cuts), largest / len(cuts)))
        loudness = loudness * jnp.repeat(draws, shape[position] // blocks).reshape([-1 if axis == position else 1 for axis in range(len(shape))])
    return loudness


def noise(rng, shape, spread, reach, pieces=(), kind=jnp.bfloat16):
    factor_of = shard_levels(rng, shape, pieces, -0.22, 0.18) if pieces else 1.0
    entries = jax.random.normal(rng, shape, jnp.float32) * spread * factor_of
    return jnp.minimum(jnp.maximum(entries, -reach), reach).astype(kind)


def setup_inputs(seed: int = 0) -> dict:
    key_list = jax.random.split(jax.random.key(seed), 5)
    vectors = noise(key_list[0], (N_GRP, NV, 2, NX, NY, NZ), 1.0, 6.0, ((0, 4), (3, 8)), jnp.float32)
    potential = jnp.clip(jnp.exp(math.log(2.0) - 2.9957323 * jax.random.uniform(key_list[1], (NX, NY, NZ), jnp.float32) ** shard_levels(key_list[1], (NX, NY, NZ), ((0, 8),), -0.2, 0.2)), 0.1, 2.0)
    added_field = noise(key_list[2], (N_GRP, NX, NY, NZ), 0.5, 3.0, ((0, 4), (1, 8)), jnp.float32)
    qp_states = noise(key_list[3], (NQ, NX, NY, NZ), (NX * NY * NZ) ** -0.5, 0.00390625, ((1, 8),))
    return dict(vectors=vectors, potential=potential, added_field=added_field, qp_states=qp_states)


time_step = 0.2
four_pi = 12.566370614359172

def sine_table(length):
    indices = jnp.arange(length, dtype=jnp.int32) + 1
    products = indices[:, None] * indices[None, :] % (2 * (length + 1))
    return jnp.sqrt(2.0 / (length + 1)) * jnp.sin(jnp.pi * products.astype(jnp.float32) / (length + 1))

def eigenvalues(length):
    indices = jnp.arange(length, dtype=jnp.int32) + 1
    return 2.0 - 2.0 * jnp.cos(jnp.pi * indices.astype(jnp.float32) / (length + 1))

def laplace_inner(field):
    centre = field[..., 1:-1, :, :]
    result = field[..., 2:, :, :] + field[..., :-2, :, :]
    widths = [(0, 0)] * (centre.ndim - 2)
    along_y = jnp.pad(centre, widths + [(1, 1), (0, 0)])
    result = result + along_y[..., 2:, :] + along_y[..., :-2, :]
    along_z = jnp.pad(centre, widths + [(0, 0), (1, 1)])
    result = result + along_z[..., 2:] + along_z[..., :-2]
    return result - 6.0 * centre

def taylor_term(applied, power):
    factor = time_step / power
    return jnp.stack([factor * applied[:, :, 1], -factor * applied[:, :, 0]], axis=2)

def propagate(initial, potential, added):
    state = jnp.stack([initial, initial])
    fields = jnp.stack([potential, potential + added])
    summed = state
    current = state
    for power in range(1, ORDER + 1):
        padded = jnp.pad(current, [(0, 0)] * 3 + [(1, 1), (0, 0), (0, 0)])
        applied = -0.5 * laplace_inner(padded) + fields[:, None, None] * current
        current = taylor_term(applied, power)
        summed = summed + current
    return summed

def poisson(density):
    highest = lax.Precision.HIGHEST
    table_x = sine_table(NX)
    table_y = sine_table(NY)
    table_z = sine_table(NZ)
    field = jnp.einsum('xyz,zl->xyl', density, table_z, precision=highest)
    field = jnp.einsum('xyl,yk->xkl', field, table_y, precision=highest)
    field = jnp.einsum('xkl,xm->mkl', field, table_x, precision=highest)
    spectrum = eigenvalues(NX)[:, None, None] + eigenvalues(NY)[None, :, None] + eigenvalues(NZ)[None, None, :]
    field = field * (four_pi / spectrum)
    field = jnp.einsum('mkl,mx->xkl', field, table_x, precision=highest)
    field = jnp.einsum('xkl,ky->xyl', field, table_y, precision=highest)
    return jnp.einsum('xyl,lz->xyz', field, table_z, precision=highest)

def reference(vectors, potential, added_field, qp_states):
    half = N_GRP // 2
    induced = []
    blocks = []
    flat_states = qp_states.reshape(NQ, -1)
    for group in range(N_GRP):
        summed = propagate(vectors[group], potential, added_field[group])
        if group < half:
            density = lax.optimization_barrier(jnp.sum(summed[1] * summed[1] - summed[0] * summed[0], axis=(0, 1)))
            induced.append(poisson(density))
            received = jnp.zeros_like(potential)
        else:
            received = induced[group - half]
        weighted = ((received + added_field[group]) * summed[1]).astype(jnp.bfloat16)
        blocks.append(jnp.dot(flat_states, weighted.reshape(2 * NV, -1).T, preferred_element_type=jnp.float32))
    return jnp.stack(blocks)
```

```python
import functools

import jax
import jax.numpy as jnp
from jax import lax
from jax.experimental import pallas as pl
from jax.experimental.pallas import tpu as pltpu
from jax.sharding import PartitionSpec as P

ORDER = 4
LANES = 128
SUBS = 8
SHARES = (1, 1, 1, 1)

time_step = 0.2
four_pi = 12.566370614359172
highest = lax.Precision.HIGHEST


def neighbour_pairs(count):
    forward = [(i, i + 1) for i in range(count - 1)]
    backward = [(i + 1, i) for i in range(count - 1)]
    return forward, backward


def sine_table(length):
    indices = jnp.arange(length, dtype=jnp.int32) + 1
    products = indices[:, None] * indices[None, :] % (2 * (length + 1))
    return jnp.sqrt(2.0 / (length + 1)) * jnp.sin(
        jnp.pi * products.astype(jnp.float32) / (length + 1)
    )


def eigenvalues(length):
    indices = jnp.arange(length, dtype=jnp.int32) + 1
    return 2.0 - 2.0 * jnp.cos(jnp.pi * indices.astype(jnp.float32) / (length + 1))


def edge_rows(first, last):
    sub = lax.broadcasted_iota(jnp.int32, first.shape, 0)
    before = jnp.where(sub == 0, 0.0, pltpu.roll(last, 1, 0))
    after = jnp.where(sub == SUBS - 1, 0.0, pltpu.roll(first, SUBS - 1, 0))
    return before, after


def across_lanes(tiles):
    shape = tiles[0].shape
    lane = lax.broadcasted_iota(jnp.int32, shape, len(shape) - 1)
    up = [pltpu.roll(t, 1, len(shape) - 1) for t in tiles]
    down = [pltpu.roll(t, LANES - 1, len(shape) - 1) for t in tiles]
    sums = []
    for m in range(len(tiles)):
        low = up[m - 1] if m > 0 else 0.0
        high = down[m + 1] if m < len(tiles) - 1 else 0.0
        sums.append(
            jnp.where(lane == 0, low, up[m]) + jnp.where(lane == LANES - 1, high, down[m])
        )
    return sums


def neighbour_sum(ref, lead, p, r0, n):
    block = ref[lead + (p, pl.ds(r0, n + 2))]
    x_low = ref[lead + (p - 1, pl.ds(r0 + 1, n))]
    x_high = ref[lead + (p + 1, pl.ds(r0 + 1, n))]
    centre = block[1:-1]
    plain = (block[2:] + block[:-2]) + (x_low + x_high)
    tiles = block.shape[-1] // LANES
    cut = lambda a, m: a[..., m * LANES : (m + 1) * LANES]
    z_sums = across_lanes([cut(centre, m) for m in range(tiles)])
    total = jnp.concatenate([cut(plain, m) + z_sums[m] for m in range(tiles)], axis=-1)
    return centre, total


def spans(size_y, shares):
    edges = [0]
    for share in shares:
        edges.append(edges[-1] + share * size_y // sum(shares))
    found, low = [], 0
    for o0, o1 in zip(edges[:-1], edges[1:]):
        high = min(o1 + SUBS, size_y)
        found.append(((o0, o1), (low, high), (max(o0 - SUBS, 0), high)))
        low = high
    return found


def pieces(rows):
    count = -(-rows // 5)
    sizes = [rows // count + (1 if j < rows % count else 0) for j in range(count)]
    starts = [sum(sizes[:j]) for j in range(count)]
    return list(zip(starts, sizes))


def taylor_kernel(span, sources, planes, first_call, flag_ref, mask_ref, own_ref, pot_ref, add_ref, *refs):
    out_rows, _, window = span
    n_msgs = sum(len(names) for names, _, _ in sources)
    flat, refs = refs[:n_msgs], refs[n_msgs:]
    msgs, at = [], 0
    for names, _, _ in sources:
        msgs.append(dict(zip(names, flat[at : at + len(names)])))
        at += len(names)
    if not first_call:
        refs = refs[1:]
    b_ref, rho_out, x_in, f_in, b_out, r_out, u0, u1, u2, u3, w, even, odd, acc, sems = refs
    s = 0.5 * time_step
    halo = ORDER
    tiles, n_fields = x_in.shape[:2]
    height = window[1] - window[0]
    rows = height // SUBS
    reach = [planes + 2 * (halo - k) for k in range(ORDER + 1)]
    lanes = lambda m: pl.ds(m * LANES, LANES)
    used = [0]
    waits = {"f": [], "x": []}

    def sem():
        used[0] += 1
        return sems.at[used[0] - 1]

    def fetch_own(kind, source, target):
        for m in range(tiles):
            copy = pltpu.make_async_copy(
                source.at[:, pl.ds(window[0], height), lanes(m)], target(m), sem()
            )
            copy.start()
            waits[kind].append(copy)

    def fetch_halo(kind, side, p0, n, target):
        for names, (start, size), to in sources:
            msg = msgs[sources.index((names, (start, size), to))]
            for m in range(tiles):
                own = sem()
                goal = target(m, pl.ds(to, size))
                part = lambda ref, p: pltpu.make_async_copy(
                    ref.at[pl.ds(p, n), pl.ds(start, size), lanes(m)], goal, own
                )
                plain = part(msg[side], p0)
                if "direct" in msg:
                    split = msg["direct"].shape[0]
                    other = (
                        part(msg["direct"], p0) if p0 < split else part(msg["relay"], p0 - split)
                    )
                    flag = flag_ref[0 if side == "low" else 1]
                    pl.when(flag == 0)(plain.start)
                    pl.when(flag == 1)(other.start)
                else:
                    plain.start()
                waits[kind].append(plain)

    for which, ref in enumerate((pot_ref, add_ref)):
        p0 = n_fields * planes + which * (halo - 1)
        for side, to in (("low", 0), ("high", halo - 1 + planes)):
            fetch_halo(
                "f", side, p0, halo - 1,
                lambda m, at, to=to, which=which: f_in.at[m, which, pl.ds(to, halo - 1), at],
            )
        fetch_own("f", ref, lambda m: f_in.at[m, which, pl.ds(halo - 1, planes)])
    for j in range(n_fields):
        for side, to in (("low", 0), ("high", halo + planes)):
            fetch_halo(
                "x", side, j * planes, halo,
                lambda m, at, to=to, j=j: x_in.at[m, j, pl.ds(to, halo), at],
            )
        fetch_own("x", own_ref.at[j], lambda m: x_in.at[m, j, pl.ds(halo, planes)])

    def gather(ref, lead, r):
        at = pl.ds(r, SUBS, stride=rows)
        return jnp.concatenate([ref[(m,) + lead + (at, slice(None))] for m in range(tiles)], axis=1)

    def scatter(ref, lead, r, value):
        at = pl.ds(r, SUBS, stride=rows)
        for m in range(tiles):
            ref[(m,) + lead + (at, slice(None))] = value[:, m * LANES : (m + 1) * LANES]

    for copy in waits["f"]:
        copy.wait()

    def load_w(q, carry):
        for r in range(rows):
            pot = 2.0 * gather(f_in, (0, q), r) + 6.0
            w[0, q, r] = pot
            w[1, q, r] = pot + 2.0 * gather(f_in, (1, q), r)
        return carry

    lax.fori_loop(0, reach[1], load_w, 0)
    acc[...] = jnp.zeros_like(acc)
    for copy in waits["x"]:
        copy.wait()

    def finish(ref, lead):
        before, after = edge_rows(ref[lead + (1,)], ref[lead + (rows,)])
        ref[lead + (0,)] = before
        ref[lead + (rows + 1,)] = after

    def inside(p, k):
        side = halo - k
        low = jnp.where(p < side, mask_ref[0], 1.0)
        return jnp.where(p >= side + planes, mask_ref[1], low)

    def run_part(i, part):
        def load_field(q, carry):
            for r in range(rows):
                u0[q, r + 1] = gather(x_in, (2 * i + part, q), r)
            finish(u0, (q,))
            return carry

        lax.fori_loop(0, reach[0], load_field, 0)

        def order_1(p, carry):
            keep = inside(p, 1)
            for r0, n in pieces(rows):
                centre, total = neighbour_sum(u0, (), p + 1, r0, n)
                for stack in range(2):
                    u1[stack, p, pl.ds(r0 + 1, n)] = keep * (
                        total - w[stack, p, pl.ds(r0, n)] * centre
                    )
            for stack in range(2):
                finish(u1, (stack, p))
            return carry

        lax.fori_loop(0, reach[1], order_1, 0)
        for k, source, target in ((2, u1, u2), (3, u2, u3)):

            def order_k(p, carry, k=k, source=source, target=target):
                keep = inside(p, k)
                for stack in range(2):
                    for r0, n in pieces(rows):
                        centre, total = neighbour_sum(source, (stack,), p + 1, r0, n)
                        target[stack, p, pl.ds(r0 + 1, n)] = keep * (
                            total - w[stack, p + k - 1, pl.ds(r0, n)] * centre
                        )
                    finish(target, (stack, p))
                return carry

            lax.fori_loop(0, reach[k], order_k, 0)

        def last(p, carry):
            for r0, n in pieces(rows):
                at = pl.ds(r0 + 1, n)
                plain = pl.ds(r0, n)
                first = u0[p + 4, at]
                found = []
                for stack in range(2):
                    centre, total = neighbour_sum(u3, (stack,), p + 1, r0, n)
                    fourth = total - w[stack, p + 3, plain] * centre
                    ev = first - (s**2 / 2) * u2[stack, p + 2, at] + (s**4 / 24) * fourth
                    od = s * u1[stack, p + 3, at] - (s**3 / 6) * centre
                    if part == 0:
                        even[stack, p, plain] = ev
                        odd[stack, p, plain] = od
                    else:
                        found.append((even[stack, p, plain] - od, odd[stack, p, plain] + ev))
                if part == 1:
                    (ar, ai), (br, bi) = found
                    acc[p, plain] += (br * br + bi * bi) - (ar * ar + ai * ai)
                    for j in range(n):
                        scatter(b_out, (2 * i, p), r0 + j, br[j])
                        scatter(b_out, (2 * i + 1, p), r0 + j, bi[j])
            return carry

        lax.fori_loop(0, planes, last, 0)

    def vector(i, carry):
        run_part(i, 0)
        run_part(i, 1)
        return carry

    lax.fori_loop(0, n_fields // 2, vector, 0)

    def spread(p, carry):
        for r in range(rows):
            scatter(r_out, (p,), r, acc[p, r])
        return carry

    lax.fori_loop(0, planes, spread, 0)
    out = []
    count = out_rows[1] - out_rows[0]
    inner = pl.ds(out_rows[0] - window[0], count)
    for m in range(tiles):
        out.append(
            pltpu.make_async_copy(
                b_out.at[m, :, :, inner],
                b_ref.at[:, :, pl.ds(out_rows[0], count), lanes(m)],
                sem(),
            )
        )
        out.append(
            pltpu.make_async_copy(r_out.at[m, :, inner], rho_out.at[:, :, lanes(m)], sem())
        )
    for copy in out:
        copy.start()
    for copy in out:
        copy.wait()


def taylor(span, flags, mask, own, potential, added, sources, b):
    n_fields, planes, size_y, size_z = own.shape
    out_rows, _, window = span
    height = window[1] - window[0]
    rows = height // SUBS
    tiles = size_z // LANES
    held = lambda *lead: pltpu.VMEM(lead + (rows + 2, SUBS, size_z), jnp.float32)
    plain = lambda *lead: pltpu.VMEM(lead + (rows, SUBS, size_z), jnp.float32)
    natural = lambda *lead: pltpu.VMEM((tiles,) + lead + (height, LANES), jnp.float32)
    hbm = pl.BlockSpec(memory_space=pl.ANY)
    smem = pl.BlockSpec(memory_space=pltpu.SMEM)
    shape = [(tuple(msgs), piece, to) for msgs, piece, to in sources]
    operands = [own, potential, added] + [m for msgs, _, _ in sources for m in msgs.values()]
    aliases = {}
    if b is not None:
        operands.append(b)
        aliases = {2 + len(operands) - 1: 0}
    n_sems = tiles * (8 + 16 * len(sources) + 2 * (n_fields - 6) + 2)
    return pl.pallas_call(
        functools.partial(taylor_kernel, span, shape, planes, b is None),
        out_shape=(
            jax.ShapeDtypeStruct(own.shape, jnp.float32),
            jax.ShapeDtypeStruct((planes, out_rows[1] - out_rows[0], size_z), jnp.float32),
        ),
        in_specs=[smem, smem] + [hbm] * len(operands),
        out_specs=(hbm, hbm),
        input_output_aliases=aliases,
        scratch_shapes=[
            natural(n_fields, planes + 8),
            natural(2, planes + 6),
            natural(n_fields, planes),
            natural(planes),
            held(planes + 8),
            held(2, planes + 6),
            held(2, planes + 4),
            held(2, planes + 2),
            plain(2, planes + 6),
            plain(2, planes),
            plain(2, planes),
            plain(planes),
            pltpu.SemaphoreType.DMA((n_sems + 8,)),
        ],
        name="taylor",
    )(flags, mask, *operands)


def elements_kernel(n_states, parts, last_step, rec_ref, add_ref, b_ref, q_ref, out_ref, acc):
    step = pl.program_id(0) * pl.num_programs(1) + pl.program_id(1)

    @pl.when(step == 0)
    def _():
        acc[...] = jnp.zeros_like(acc)

    field = rec_ref[0] + add_ref[0]
    group = 16
    total = acc[...]
    for g in range(field.shape[0] // group):
        at = slice(g * group, (g + 1) * group)
        weighted = [field[at] * b_ref[j, 0, at] for j in range(parts)]
        weighted = jnp.concatenate(weighted, axis=0).astype(jnp.bfloat16)
        states = q_ref[:, 0, at].reshape(n_states * group, field.shape[-1])
        total += lax.dot_general(
            states, weighted, (((1,), (1,)), ((), ())), preferred_element_type=jnp.float32
        )
    acc[...] = total

    @pl.when(step == last_step)
    def _():
        found = acc[...].reshape(n_states, group, parts * group)
        row = lax.broadcasted_iota(jnp.int32, found.shape, 1)
        col = lax.broadcasted_iota(jnp.int32, found.shape, 2)
        own = jnp.sum(jnp.where(row == col % group, found, 0.0), axis=1)
        fold_r = lax.broadcasted_iota(jnp.int32, (parts * group, parts), 0)
        fold_c = lax.broadcasted_iota(jnp.int32, (parts * group, parts), 1)
        fold = jnp.where(fold_r // group == fold_c, 1.0, 0.0)
        out_ref[...] = jnp.dot(own, fold, precision=highest, preferred_element_type=jnp.float32)


def elements(received, added, b, states):
    n_states, planes, size_y, size_z = states.shape
    block = 64
    parts = b.shape[0]
    grid = (planes, size_y // block)
    field = pl.BlockSpec((1, block, size_z), lambda p, y: (p, y, 0))
    vec = pl.BlockSpec((parts, 1, block, size_z), lambda p, y: (0, p, y, 0))
    return pl.pallas_call(
        functools.partial(elements_kernel, n_states, parts, planes * (size_y // block) - 1),
        grid=grid,
        out_shape=jax.ShapeDtypeStruct((n_states, parts), jnp.float32),
        in_specs=[field, field]
        + [vec]
        + [pl.BlockSpec((n_states, 1, block, size_z), lambda p, y: (0, p, y, 0))],
        out_specs=pl.BlockSpec((n_states, parts), lambda p, y: (0, 0)),
        scratch_shapes=[pltpu.VMEM((n_states * 16, parts * 16), jnp.float32)],
        name="elements",
    )(received, added, b, states)


def forward_yz(chunks, table_y, table_z):
    total, at = 0.0, 0
    for piece in chunks:
        count = piece.shape[1]
        field = jnp.einsum("xyz,zl->xyl", piece, table_z, precision=highest)
        total += jnp.einsum("xyl,yk->xkl", field, table_y[at : at + count], precision=highest)
        at += count
    return total


def poisson_block(chunks):
    planes, _, size_z = chunks[0].shape
    size_y = sum(piece.shape[1] for piece in chunks)
    full_x = planes * lax.axis_size("grid")
    table_x = sine_table(full_x)
    table_y = sine_table(size_y)
    table_z = sine_table(size_z)
    field = forward_yz(chunks, table_y, table_z)
    columns = lax.all_to_all(field, "grid", split_axis=1, concat_axis=0, tiled=True)
    row_count = columns.shape[1]
    own_rows = lax.dynamic_slice_in_dim(
        eigenvalues(size_y), lax.axis_index("grid") * row_count, row_count
    )
    field = jnp.einsum("xkl,xm->mkl", columns, table_x, precision=highest)
    spectrum = (
        eigenvalues(full_x)[:, None, None]
        + own_rows[None, :, None]
        + eigenvalues(size_z)[None, None, :]
    )
    field = field * (four_pi / spectrum)
    field = jnp.einsum("mkl,mx->xkl", field, table_x, precision=highest)
    returned = lax.all_to_all(field, "grid", split_axis=0, concat_axis=1, tiled=True)
    field = jnp.einsum("xkl,ky->xyl", returned, table_y, precision=highest)
    return jnp.einsum("xyl,lz->xyz", field, table_z, precision=highest)


def scatter_sum(value, axis):
    count = lax.axis_size(axis)
    place = lax.axis_index(axis)
    step = count // 2
    while step:
        half = value.shape[0] // 2
        upper = (place // step) % 2 == 1
        low, high = value[:half], value[half:]
        pairs = [(i, i ^ step) for i in range(count)]
        sent = lax.ppermute(jnp.where(upper, low, high), axis, pairs)
        value = jnp.where(upper, high, low) + sent
        step //= 2
    return value


def on_device(vectors, potential, added_field, qp_states):
    own = vectors.reshape((-1,) + vectors.shape[3:])
    added = added_field[0]
    count = lax.axis_size("grid")
    groups = lax.axis_size("grp")
    place = lax.axis_index("grid")
    n_fields, planes, size_y, size_z = own.shape
    assert planes == ORDER and n_fields == 6
    mask = jnp.stack([place > 0, place < count - 1]).astype(jnp.float32)
    relayed = count == 8
    middle = count // 2
    left, right = middle - 1, middle
    flags = jnp.stack([place == right, place == left]).astype(jnp.int32)
    keep = lambda pairs: [p for p in pairs if set(p) != {left, right}]
    forward, backward = neighbour_pairs(count)
    layout = spans(size_y, SHARES)

    fields = (potential, added)
    messages, previous = [], None
    for c, (_, (lo, hi), _) in enumerate(layout):
        parts = [own, *fields]
        if previous is not None:
            parts, _ = lax.optimization_barrier((parts, previous))
        block = parts[0][:, :, lo:hi].reshape(-1, hi - lo, size_z)
        upper = [f[1:, lo:hi] for f in parts[1:]]
        lower = [f[:-1, lo:hi] for f in parts[1:]]
        to_right = jnp.concatenate([block] + upper)
        to_left = jnp.concatenate([block] + lower)
        msg = {}
        if relayed:
            split = 4 * planes
            free = own[4:, :, lo:hi].reshape(-1, hi - lo, size_z)
            ends = [jnp.where(place == left, f[1:, lo:hi], f[:-1, lo:hi]) for f in fields]
            rest = jnp.concatenate([free] + ends)
            first_leg = [(left, count - 1), (right, 0)]
            second_leg = [(count - 1, right), (0, left)]
            hop = lax.ppermute(rest, "grid", first_leg)
            msg["low"] = lax.ppermute(to_right, "grid", keep(forward))
            msg["high"] = lax.ppermute(to_left, "grid", keep(backward))
            msg["direct"] = lax.ppermute(block[:split], "grid", [(left, right), (right, left)])
            msg["relay"] = lax.ppermute(hop, "grid", second_leg)
        else:
            msg["low"] = lax.ppermute(to_right, "grid", forward)
            msg["high"] = lax.ppermute(to_left, "grid", backward)
        messages.append(msg)
        previous = msg
    pairs = [(g, g + groups // 2) for g in range(groups // 2)]
    b, arrived = None, []
    for c, span in enumerate(layout):
        _, (lo, hi), window = span
        sources = []
        if c:
            before = layout[c - 1][1]
            sources.append(
                (messages[c - 1], (window[0] - before[0], lo - window[0]), 0)
            )
        sources.append((messages[c], (0, hi - lo), lo - window[0]))
        b, rho = taylor(span, flags, mask, own, potential, added, sources, b)
        arrived.append(lax.ppermute(rho, "grp", pairs))
    received = poisson_block(arrived)
    partial = elements(received, added, b, qp_states)
    return scatter_sum(partial, "grid")[None]


def solution(mesh):
    in_specs = (
        P("grp", None, None, "grid", None, None),
        P("grid", None, None),
        P("grp", "grid", None, None),
        P(None, "grid", None, None),
    )
    out_specs = P("grp", "grid", None)
    return jax.shard_map(
        on_device, mesh=mesh, in_specs=in_specs, out_specs=out_specs, check_vma=False
    )
```

```python
import functools

import jax
import jax.numpy as jnp
from jax import lax
from jax.experimental import pallas as pl
from jax.experimental.pallas import tpu as pltpu
from jax.sharding import PartitionSpec as P

ORDER = 4
LANES = 128
SUBS = 8
SHARES = (1, 1, 1, 1)

time_step = 0.2
four_pi = 12.566370614359172
highest = lax.Precision.HIGHEST


def neighbour_pairs(count):
    forward = [(i, i + 1) for i in range(count - 1)]
    backward = [(i + 1, i) for i in range(count - 1)]
    return forward, backward


def sine_table(length):
    indices = jnp.arange(length, dtype=jnp.int32) + 1
    products = indices[:, None] * indices[None, :] % (2 * (length + 1))
    return jnp.sqrt(2.0 / (length + 1)) * jnp.sin(
        jnp.pi * products.astype(jnp.float32) / (length + 1)
    )


def eigenvalues(length):
    indices = jnp.arange(length, dtype=jnp.int32) + 1
    return 2.0 - 2.0 * jnp.cos(jnp.pi * indices.astype(jnp.float32) / (length + 1))


def edge_rows(first, last):
    sub = lax.broadcasted_iota(jnp.int32, first.shape, 0)
    before = jnp.where(sub == 0, 0.0, pltpu.roll(last, 1, 0))
    after = jnp.where(sub == SUBS - 1, 0.0, pltpu.roll(first, SUBS - 1, 0))
    return before, after


def across_lanes(tiles):
    shape = tiles[0].shape
    lane = lax.broadcasted_iota(jnp.int32, shape, len(shape) - 1)
    up = [pltpu.roll(t, 1, len(shape) - 1) for t in tiles]
    down = [pltpu.roll(t, LANES - 1, len(shape) - 1) for t in tiles]
    sums = []
    for m in range(len(tiles)):
        low = up[m - 1] if m > 0 else 0.0
        high = down[m + 1] if m < len(tiles) - 1 else 0.0
        sums.append(
            jnp.where(lane == 0, low, up[m]) + jnp.where(lane == LANES - 1, high, down[m])
        )
    return sums


def neighbour_sum(ref, lead, p, r0, n):
    block = ref[lead + (p, pl.ds(r0, n + 2))]
    x_low = ref[lead + (p - 1, pl.ds(r0 + 1, n))]
    x_high = ref[lead + (p + 1, pl.ds(r0 + 1, n))]
    centre = block[1:-1]
    plain = (block[2:] + block[:-2]) + (x_low + x_high)
    tiles = block.shape[-1] // LANES
    cut = lambda a, m: a[..., m * LANES : (m + 1) * LANES]
    z_sums = across_lanes([cut(centre, m) for m in range(tiles)])
    total = jnp.concatenate([cut(plain, m) + z_sums[m] for m in range(tiles)], axis=-1)
    return centre, total


def spans(size_y, shares):
    edges = [0]
    for share in shares:
        edges.append(edges[-1] + share * size_y // sum(shares))
    found, low = [], 0
    for o0, o1 in zip(edges[:-1], edges[1:]):
        high = min(o1 + SUBS, size_y)
        found.append(((o0, o1), (low, high), (max(o0 - SUBS, 0), high)))
        low = high
    return found


def pieces(rows):
    count = -(-rows // 5)
    sizes = [rows // count + (1 if j < rows % count else 0) for j in range(count)]
    starts = [sum(sizes[:j]) for j in range(count)]
    return list(zip(starts, sizes))


def taylor_kernel(span, sources, planes, first_call, flag_ref, mask_ref, own_ref, pot_ref, add_ref, *refs):
    out_rows, _, window = span
    n_msgs = sum(len(names) for names, _, _ in sources)
    flat, refs = refs[:n_msgs], refs[n_msgs:]
    msgs, at = [], 0
    for names, _, _ in sources:
        msgs.append(dict(zip(names, flat[at : at + len(names)])))
        at += len(names)
    if not first_call:
        refs = refs[1:]
    b_ref, rho_out, x_in, f_in, b_out, r_out, u0, u1, u2, u3, w, even, odd, acc, sems = refs
    s = 0.5 * time_step
    halo = ORDER
    tiles, n_fields = x_in.shape[:2]
    height = window[1] - window[0]
    rows = height // SUBS
    reach = [planes + 2 * (halo - k) for k in range(ORDER + 1)]
    lanes = lambda m: pl.ds(m * LANES, LANES)
    used = [0]
    waits = {"f": [], "x": []}

    def sem():
        used[0] += 1
        return sems.at[used[0] - 1]

    def fetch_own(kind, source, target):
        for m in range(tiles):
            copy = pltpu.make_async_copy(
                source.at[:, pl.ds(window[0], height), lanes(m)], target(m), sem()
            )
            copy.start()
            waits[kind].append(copy)

    def fetch_halo(kind, side, p0, n, target):
        for names, (start, size), to in sources:
            msg = msgs[sources.index((names, (start, size), to))]
            for m in range(tiles):
                own = sem()
                goal = target(m, pl.ds(to, size))
                part = lambda ref, p: pltpu.make_async_copy(
                    ref.at[pl.ds(p, n), pl.ds(start, size), lanes(m)], goal, own
                )
                plain = part(msg[side], p0)
                if "direct" in msg:
                    split = msg["direct"].shape[0]
                    other = (
                        part(msg["direct"], p0) if p0 < split else part(msg["relay"], p0 - split)
                    )
                    flag = flag_ref[0 if side == "low" else 1]
                    pl.when(flag == 0)(plain.start)
                    pl.when(flag == 1)(other.start)
                else:
                    plain.start()
                waits[kind].append(plain)

    for which, ref in enumerate((pot_ref, add_ref)):
        p0 = n_fields * planes + which * (halo - 1)
        for side, to in (("low", 0), ("high", halo - 1 + planes)):
            fetch_halo(
                "f", side, p0, halo - 1,
                lambda m, at, to=to, which=which: f_in.at[m, which, pl.ds(to, halo - 1), at],
            )
        fetch_own("f", ref, lambda m: f_in.at[m, which, pl.ds(halo - 1, planes)])
    for j in range(n_fields):
        for side, to in (("low", 0), ("high", halo + planes)):
            fetch_halo(
                "x", side, j * planes, halo,
                lambda m, at, to=to, j=j: x_in.at[m, j, pl.ds(to, halo), at],
            )
        fetch_own("x", own_ref.at[j], lambda m: x_in.at[m, j, pl.ds(halo, planes)])

    def gather(ref, lead, r):
        at = pl.ds(r, SUBS, stride=rows)
        return jnp.concatenate([ref[(m,) + lead + (at, slice(None))] for m in range(tiles)], axis=1)

    def scatter(ref, lead, r, value):
        at = pl.ds(r, SUBS, stride=rows)
        for m in range(tiles):
            ref[(m,) + lead + (at, slice(None))] = value[:, m * LANES : (m + 1) * LANES]

    for copy in waits["f"]:
        copy.wait()

    def load_w(q, carry):
        for r in range(rows):
            pot = 2.0 * gather(f_in, (0, q), r) + 6.0
            w[0, q, r] = pot
            w[1, q, r] = pot + 2.0 * gather(f_in, (1, q), r)
        return carry

    lax.fori_loop(0, reach[1], load_w, 0)
    acc[...] = jnp.zeros_like(acc)
    for copy in waits["x"]:
        copy.wait()

    def finish(ref, lead):
        before, after = edge_rows(ref[lead + (1,)], ref[lead + (rows,)])
        ref[lead + (0,)] = before
        ref[lead + (rows + 1,)] = after

    def inside(p, k):
        side = halo - k
        low = jnp.where(p < side, mask_ref[0], 1.0)
        return jnp.where(p >= side + planes, mask_ref[1], low)

    def run_part(i, part):
        def load_field(q, carry):
            for r in range(rows):
                u0[q, r + 1] = gather(x_in, (2 * i + part, q), r)
            finish(u0, (q,))
            return carry

        lax.fori_loop(0, reach[0], load_field, 0)

        def order_1(p, carry):
            keep = inside(p, 1)
            for r0, n in pieces(rows):
                centre, total = neighbour_sum(u0, (), p + 1, r0, n)
                for stack in range(2):
                    u1[stack, p, pl.ds(r0 + 1, n)] = keep * (
                        total - w[stack, p, pl.ds(r0, n)] * centre
                    )
            for stack in range(2):
                finish(u1, (stack, p))
            return carry

        lax.fori_loop(0, reach[1], order_1, 0)
        for k, source, target in ((2, u1, u2), (3, u2, u3)):

            def order_k(p, carry, k=k, source=source, target=target):
                keep = inside(p, k)
                for stack in range(2):
                    for r0, n in pieces(rows):
                        centre, total = neighbour_sum(source, (stack,), p + 1, r0, n)
                        target[stack, p, pl.ds(r0 + 1, n)] = keep * (
                            total - w[stack, p + k - 1, pl.ds(r0, n)] * centre
                        )
                    finish(target, (stack, p))
                return carry

            lax.fori_loop(0, reach[k], order_k, 0)

        def last(p, carry):
            for r0, n in pieces(rows):
                at = pl.ds(r0 + 1, n)
                plain = pl.ds(r0, n)
                first = u0[p + 4, at]
                found = []
                for stack in range(2):
                    centre, total = neighbour_sum(u3, (stack,), p + 1, r0, n)
                    fourth = total - w[stack, p + 3, plain] * centre
                    ev = first - (s**2 / 2) * u2[stack, p + 2, at] + (s**4 / 24) * fourth
                    od = s * u1[stack, p + 3, at] - (s**3 / 6) * centre
                    if part == 0:
                        even[stack, p, plain] = ev
                        odd[stack, p, plain] = od
                    else:
                        found.append((even[stack, p, plain] - od, odd[stack, p, plain] + ev))
                if part == 1:
                    (ar, ai), (br, bi) = found
                    acc[p, plain] += (br * br + bi * bi) - (ar * ar + ai * ai)
                    for j in range(n):
                        scatter(b_out, (2 * i, p), r0 + j, br[j])
                        scatter(b_out, (2 * i + 1, p), r0 + j, bi[j])
            return carry

        lax.fori_loop(0, planes, last, 0)

    def vector(i, carry):
        run_part(i, 0)
        run_part(i, 1)
        return carry

    lax.fori_loop(0, n_fields // 2, vector, 0)

    def spread(p, carry):
        for r in range(rows):
            scatter(r_out, (p,), r, acc[p, r])
        return carry

    lax.fori_loop(0, planes, spread, 0)
    out = []
    count = out_rows[1] - out_rows[0]
    inner = pl.ds(out_rows[0] - window[0], count)
    for m in range(tiles):
        out.append(
            pltpu.make_async_copy(
                b_out.at[m, :, :, inner],
                b_ref.at[:, :, pl.ds(out_rows[0], count), lanes(m)],
                sem(),
            )
        )
        out.append(
            pltpu.make_async_copy(r_out.at[m, :, inner], rho_out.at[:, :, lanes(m)], sem())
        )
    for copy in out:
        copy.start()
    for copy in out:
        copy.wait()


def taylor(span, flags, mask, own, potential, added, sources, b):
    n_fields, planes, size_y, size_z = own.shape
    out_rows, _, window = span
    height = window[1] - window[0]
    rows = height // SUBS
    tiles = size_z // LANES
    held = lambda *lead: pltpu.VMEM(lead + (rows + 2, SUBS, size_z), jnp.float32)
    plain = lambda *lead: pltpu.VMEM(lead + (rows, SUBS, size_z), jnp.float32)
    natural = lambda *lead: pltpu.VMEM((tiles,) + lead + (height, LANES), jnp.float32)
    hbm = pl.BlockSpec(memory_space=pl.ANY)
    smem = pl.BlockSpec(memory_space=pltpu.SMEM)
    shape = [(tuple(msgs), piece, to) for msgs, piece, to in sources]
    operands = [own, potential, added] + [m for msgs, _, _ in sources for m in msgs.values()]
    aliases = {}
    if b is not None:
        operands.append(b)
        aliases = {2 + len(operands) - 1: 0}
    n_sems = tiles * (8 + 16 * len(sources) + 2 * (n_fields - 6) + 2)
    return pl.pallas_call(
        functools.partial(taylor_kernel, span, shape, planes, b is None),
        out_shape=(
            jax.ShapeDtypeStruct(own.shape, jnp.float32),
            jax.ShapeDtypeStruct((planes, out_rows[1] - out_rows[0], size_z), jnp.float32),
        ),
        in_specs=[smem, smem] + [hbm] * len(operands),
        out_specs=(hbm, hbm),
        input_output_aliases=aliases,
        scratch_shapes=[
            natural(n_fields, planes + 8),
            natural(2, planes + 6),
            natural(n_fields, planes),
            natural(planes),
            held(planes + 8),
            held(2, planes + 6),
            held(2, planes + 4),
            held(2, planes + 2),
            plain(2, planes + 6),
            plain(2, planes),
            plain(2, planes),
            plain(planes),
            pltpu.SemaphoreType.DMA((n_sems + 8,)),
        ],
        cost_estimate=pl.CostEstimate(
            flops=rows * SUBS * size_z * planes * 120000, transcendentals=0, bytes_accessed=20 << 20
        ),
        name="taylor",
    )(flags, mask, *operands)


def elements_kernel(n_states, parts, last_step, rec_ref, add_ref, b_ref, q_ref, out_ref, acc):
    step = pl.program_id(0) * pl.num_programs(1) + pl.program_id(1)

    @pl.when(step == 0)
    def _():
        acc[...] = jnp.zeros_like(acc)

    field = rec_ref[0] + add_ref[0]
    group = 16
    total = acc[...]
    for g in range(field.shape[0] // group):
        at = slice(g * group, (g + 1) * group)
        weighted = [field[at] * b_ref[j, 0, at] for j in range(parts)]
        weighted = jnp.concatenate(weighted, axis=0).astype(jnp.bfloat16)
        states = q_ref[:, 0, at].reshape(n_states * group, field.shape[-1])
        total += lax.dot_general(
            states, weighted, (((1,), (1,)), ((), ())), preferred_element_type=jnp.float32
        )
    acc[...] = total

    @pl.when(step == last_step)
    def _():
        found = acc[...].reshape(n_states, group, parts * group)
        row = lax.broadcasted_iota(jnp.int32, found.shape, 1)
        col = lax.broadcasted_iota(jnp.int32, found.shape, 2)
        own = jnp.sum(jnp.where(row == col % group, found, 0.0), axis=1)
        fold_r = lax.broadcasted_iota(jnp.int32, (parts * group, parts), 0)
        fold_c = lax.broadcasted_iota(jnp.int32, (parts * group, parts), 1)
        fold = jnp.where(fold_r // group == fold_c, 1.0, 0.0)
        out_ref[...] = jnp.dot(own, fold, precision=highest, preferred_element_type=jnp.float32)


def elements(received, added, b, states):
    n_states, planes, size_y, size_z = states.shape
    block = 64
    parts = b.shape[0]
    grid = (planes, size_y // block)
    field = pl.BlockSpec((1, block, size_z), lambda p, y: (p, y, 0))
    vec = pl.BlockSpec((parts, 1, block, size_z), lambda p, y: (0, p, y, 0))
    return pl.pallas_call(
        functools.partial(elements_kernel, n_states, parts, planes * (size_y // block) - 1),
        grid=grid,
        out_shape=jax.ShapeDtypeStruct((n_states, parts), jnp.float32),
        in_specs=[field, field]
        + [vec]
        + [pl.BlockSpec((n_states, 1, block, size_z), lambda p, y: (0, p, y, 0))],
        out_specs=pl.BlockSpec((n_states, parts), lambda p, y: (0, 0)),
        scratch_shapes=[pltpu.VMEM((n_states * 16, parts * 16), jnp.float32)],
        name="elements",
    )(received, added, b, states)


def forward_yz(chunks, table_y, table_z):
    total, at = 0.0, 0
    for piece in chunks:
        count = piece.shape[1]
        field = jnp.einsum("xyz,zl->xyl", piece, table_z, precision=highest)
        total += jnp.einsum("xyl,yk->xkl", field, table_y[at : at + count], precision=highest)
        at += count
    return total


def poisson_block(chunks):
    planes, _, size_z = chunks[0].shape
    size_y = sum(piece.shape[1] for piece in chunks)
    full_x = planes * lax.axis_size("grid")
    table_x = sine_table(full_x)
    table_y = sine_table(size_y)
    table_z = sine_table(size_z)
    field = forward_yz(chunks, table_y, table_z)
    columns = lax.all_to_all(field, "grid", split_axis=1, concat_axis=0, tiled=True)
    row_count = columns.shape[1]
    own_rows = lax.dynamic_slice_in_dim(
        eigenvalues(size_y), lax.axis_index("grid") * row_count, row_count
    )
    field = jnp.einsum("xkl,xm->mkl", columns, table_x, precision=highest)
    spectrum = (
        eigenvalues(full_x)[:, None, None]
        + own_rows[None, :, None]
        + eigenvalues(size_z)[None, None, :]
    )
    field = field * (four_pi / spectrum)
    field = jnp.einsum("mkl,mx->xkl", field, table_x, precision=highest)
    returned = lax.all_to_all(field, "grid", split_axis=0, concat_axis=1, tiled=True)
    field = jnp.einsum("xkl,ky->xyl", returned, table_y, precision=highest)
    return jnp.einsum("xyl,lz->xyz", field, table_z, precision=highest)


def scatter_sum(value, axis):
    count = lax.axis_size(axis)
    place = lax.axis_index(axis)
    step = count // 2
    while step:
        half = value.shape[0] // 2
        upper = (place // step) % 2 == 1
        low, high = value[:half], value[half:]
        pairs = [(i, i ^ step) for i in range(count)]
        sent = lax.ppermute(jnp.where(upper, low, high), axis, pairs)
        value = jnp.where(upper, high, low) + sent
        step //= 2
    return value


def on_device(vectors, potential, added_field, qp_states):
    own = vectors.reshape((-1,) + vectors.shape[3:])
    added = added_field[0]
    count = lax.axis_size("grid")
    groups = lax.axis_size("grp")
    place = lax.axis_index("grid")
    n_fields, planes, size_y, size_z = own.shape
    assert planes == ORDER and n_fields == 6
    mask = jnp.stack([place > 0, place < count - 1]).astype(jnp.float32)
    relayed = count == 8
    middle = count // 2
    left, right = middle - 1, middle
    flags = jnp.stack([place == right, place == left]).astype(jnp.int32)
    keep = lambda pairs: [p for p in pairs if set(p) != {left, right}]
    forward, backward = neighbour_pairs(count)
    layout = spans(size_y, SHARES)

    fields = (potential, added)
    messages = []
    for c, (_, (lo, hi), _) in enumerate(layout):
        parts = [own, *fields]
        block = parts[0][:, :, lo:hi].reshape(-1, hi - lo, size_z)
        upper = [f[1:, lo:hi] for f in parts[1:]]
        lower = [f[:-1, lo:hi] for f in parts[1:]]
        to_right = jnp.concatenate([block] + upper)
        to_left = jnp.concatenate([block] + lower)
        msg = {}
        if relayed:
            split = 4 * planes
            free = own[4:, :, lo:hi].reshape(-1, hi - lo, size_z)
            ends = [jnp.where(place == left, f[1:, lo:hi], f[:-1, lo:hi]) for f in fields]
            rest = jnp.concatenate([free] + ends)
            first_leg = [(left, count - 1), (right, 0)]
            second_leg = [(count - 1, right), (0, left)]
            hop = lax.ppermute(rest, "grid", first_leg)
            msg["low"] = lax.ppermute(to_right, "grid", keep(forward))
            msg["high"] = lax.ppermute(to_left, "grid", keep(backward))
            msg["direct"] = lax.ppermute(block[:split], "grid", [(left, right), (right, left)])
            msg["relay"] = lax.ppermute(hop, "grid", second_leg)
        else:
            msg["low"] = lax.ppermute(to_right, "grid", forward)
            msg["high"] = lax.ppermute(to_left, "grid", backward)
        messages.append(msg)
    pairs = [(g, g + groups // 2) for g in range(groups // 2)]
    b, arrived = None, []
    for c, span in enumerate(layout):
        _, (lo, hi), window = span
        sources = []
        if c:
            before = layout[c - 1][1]
            sources.append(
                (messages[c - 1], (window[0] - before[0], lo - window[0]), 0)
            )
        sources.append((messages[c], (0, hi - lo), lo - window[0]))
        if c >= 2:
            b, arrived[c - 2] = lax.optimization_barrier((b, arrived[c - 2]))
        b, rho = taylor(span, flags, mask, own, potential, added, sources, b)
        arrived.append(lax.ppermute(rho, "grp", pairs))
    received = poisson_block(arrived)
    partial = elements(received, added, b, qp_states)
    return scatter_sum(partial, "grid")[None]


def solution(mesh):
    in_specs = (
        P("grp", None, None, "grid", None, None),
        P("grid", None, None),
        P("grp", "grid", None, None),
        P(None, "grid", None, None),
    )
    out_specs = P("grp", "grid", None)
    return jax.shard_map(
        on_device, mesh=mesh, in_specs=in_specs, out_specs=out_specs, check_vma=False
    )
```

```python
import functools

import jax
import jax.numpy as jnp
from jax import lax
from jax.experimental import pallas as pl
from jax.experimental.pallas import tpu as pltpu
from jax.sharding import PartitionSpec as P

ORDER = 4
LANES = 128
SUBS = 8
SHARES = (10, 10, 8, 4)

time_step = 0.2
four_pi = 12.566370614359172
highest = lax.Precision.HIGHEST


def neighbour_pairs(count):
    forward = [(i, i + 1) for i in range(count - 1)]
    backward = [(i + 1, i) for i in range(count - 1)]
    return forward, backward


def sine_table(length):
    indices = jnp.arange(length, dtype=jnp.int32) + 1
    products = indices[:, None] * indices[None, :] % (2 * (length + 1))
    return jnp.sqrt(2.0 / (length + 1)) * jnp.sin(
        jnp.pi * products.astype(jnp.float32) / (length + 1)
    )


def eigenvalues(length):
    indices = jnp.arange(length, dtype=jnp.int32) + 1
    return 2.0 - 2.0 * jnp.cos(jnp.pi * indices.astype(jnp.float32) / (length + 1))


def edge_rows(first, last):
    sub = lax.broadcasted_iota(jnp.int32, first.shape, 0)
    before = jnp.where(sub == 0, 0.0, pltpu.roll(last, 1, 0))
    after = jnp.where(sub == SUBS - 1, 0.0, pltpu.roll(first, SUBS - 1, 0))
    return before, after


def across_lanes(tiles):
    shape = tiles[0].shape
    lane = lax.broadcasted_iota(jnp.int32, shape, len(shape) - 1)
    up = [pltpu.roll(t, 1, len(shape) - 1) for t in tiles]
    down = [pltpu.roll(t, LANES - 1, len(shape) - 1) for t in tiles]
    sums = []
    for m in range(len(tiles)):
        low = up[m - 1] if m > 0 else 0.0
        high = down[m + 1] if m < len(tiles) - 1 else 0.0
        sums.append(
            jnp.where(lane == 0, low, up[m]) + jnp.where(lane == LANES - 1, high, down[m])
        )
    return sums


def neighbour_sum(ref, lead, p, r0, n):
    block = ref[lead + (p, pl.ds(r0, n + 2))]
    x_low = ref[lead + (p - 1, pl.ds(r0 + 1, n))]
    x_high = ref[lead + (p + 1, pl.ds(r0 + 1, n))]
    centre = block[1:-1]
    plain = (block[2:] + block[:-2]) + (x_low + x_high)
    tiles = block.shape[-1] // LANES
    cut = lambda a, m: a[..., m * LANES : (m + 1) * LANES]
    z_sums = across_lanes([cut(centre, m) for m in range(tiles)])
    total = jnp.concatenate([cut(plain, m) + z_sums[m] for m in range(tiles)], axis=-1)
    return centre, total


def spans(size_y, shares):
    edges = [0]
    for share in shares:
        edges.append(edges[-1] + share * size_y // sum(shares))
    found, low = [], 0
    for o0, o1 in zip(edges[:-1], edges[1:]):
        high = min(o1 + SUBS, size_y)
        found.append(((o0, o1), (low, high), (max(o0 - SUBS, 0), high)))
        low = high
    return found


def pieces(rows):
    count = -(-rows // 5)
    sizes = [rows // count + (1 if j < rows % count else 0) for j in range(count)]
    starts = [sum(sizes[:j]) for j in range(count)]
    return list(zip(starts, sizes))


def taylor_kernel(span, sources, planes, first_call, flag_ref, mask_ref, own_ref, pot_ref, add_ref, *refs):
    out_rows, _, window = span
    n_msgs = sum(len(names) for names, _, _ in sources)
    flat, refs = refs[:n_msgs], refs[n_msgs:]
    msgs, at = [], 0
    for names, _, _ in sources:
        msgs.append(dict(zip(names, flat[at : at + len(names)])))
        at += len(names)
    if not first_call:
        refs = refs[1:]
    b_ref, rho_out, x_in, f_in, b_out, r_out, u0, u1, u2, u3, w, acc, f_sems, x_sems, o_sems = refs
    s = 0.5 * time_step
    halo = ORDER
    tiles, n_fields = x_in.shape[:2]
    n_vectors = n_fields // 2
    height = window[1] - window[0]
    rows = height // SUBS
    reach = [planes + 2 * (halo - k) for k in range(ORDER + 1)]
    lanes = lambda m: pl.ds(m * LANES, LANES)

    def own_copies(source, target, sem):
        at = pl.ds(window[0], height)
        return [
            (pltpu.make_async_copy(source.at[:, at, lanes(m)], target(m, pl.ds(0, height)), sem()), None, None)
            for m in range(tiles)
        ]

    def halo_copies(side, p0, n, target, sem, starting):
        found = []
        for msg, (_, (start, size), to) in zip(msgs, sources):
            for m in range(tiles):
                part = lambda ref, p, done: pltpu.make_async_copy(
                    ref.at[pl.ds(p, n), pl.ds(start, size), lanes(m)], target(m, pl.ds(to, size)), done
                )
                done, other, flag = sem(), None, None
                if starting and "direct" in msg:
                    split = msg["direct"].shape[0]
                    other = (
                        part(msg["direct"], p0, done)
                        if p0 < split
                        else part(msg["relay"], p0 - split, done)
                    )
                    flag = flag_ref[0 if side == "low" else 1]
                found.append((part(msg[side], p0, done), other, flag))
        return found

    def counter(sems, first=0):
        used = [0]

        def sem():
            used[0] += 1
            return sems.at[first + used[0] - 1]

        return sem

    def field_copies(starting):
        sem, found = counter(f_sems), []
        for which, ref in enumerate((pot_ref, add_ref)):
            p0 = n_fields * planes + which * (halo - 1)
            for side, to in (("low", 0), ("high", halo - 1 + planes)):
                goal = lambda m, at, to=to: f_in.at[m, which, pl.ds(to, halo - 1), at]
                found += halo_copies(side, p0, halo - 1, goal, sem, starting)
            goal = lambda m, at: f_in.at[m, which, pl.ds(halo - 1, planes), at]
            found += own_copies(ref, goal, sem)
        return found

    per_vector = x_sems.shape[0] // n_vectors

    def vector_copies(i, starting):
        sem, found = counter(x_sems, i * per_vector), []
        for part in range(2):
            j = 2 * i + part
            for side, to in (("low", 0), ("high", halo + planes)):
                goal = lambda m, at, to=to: x_in.at[m, j, pl.ds(to, halo), at]
                found += halo_copies(side, j * planes, halo, goal, sem, starting)
            goal = lambda m, at: x_in.at[m, j, pl.ds(halo, planes), at]
            found += own_copies(own_ref.at[j], goal, sem)
        return found

    def start(copies):
        for plain, other, flag in copies:
            if other is None:
                plain.start()
            else:
                pl.when(flag == 0)(plain.start)
                pl.when(flag == 1)(other.start)

    def wait(copies):
        for plain, _, _ in copies:
            plain.wait()

    start(field_copies(True))
    for i in range(n_vectors):
        start(vector_copies(i, True))

    def gather(ref, lead, r):
        at = pl.ds(r, SUBS, stride=rows)
        return jnp.concatenate([ref[(m,) + lead + (at, slice(None))] for m in range(tiles)], axis=1)

    def scatter(ref, lead, r, value):
        at = pl.ds(r, SUBS, stride=rows)
        for m in range(tiles):
            ref[(m,) + lead + (at, slice(None))] = value[:, m * LANES : (m + 1) * LANES]

    wait(field_copies(False))

    def load_w(q, carry):
        for r in range(rows):
            pot = 2.0 * gather(f_in, (0, q), r) + 6.0
            w[0, q, r] = pot
            w[1, q, r] = pot + 2.0 * gather(f_in, (1, q), r)
        return carry

    lax.fori_loop(0, reach[1], load_w, 0)
    acc[...] = jnp.zeros_like(acc)

    def finish(ref, lead):
        before, after = edge_rows(ref[lead + (1,)], ref[lead + (rows,)])
        ref[lead + (0,)] = before
        ref[lead + (rows + 1,)] = after

    def inside(p, k):
        side = halo - k
        low = jnp.where(p < side, mask_ref[0], 1.0)
        return jnp.where(p >= side + planes, mask_ref[1], low)

    out_count = out_rows[1] - out_rows[0]
    inner = pl.ds(out_rows[0] - window[0], out_count)

    def b_copies(i):
        return [
            pltpu.make_async_copy(
                b_out.at[m, pl.ds(2 * i, 2), :, inner],
                b_ref.at[pl.ds(2 * i, 2), :, pl.ds(out_rows[0], out_count), lanes(m)],
                o_sems.at[i * tiles + m],
            )
            for m in range(tiles)
        ]

    def vector(i, carry):
        wait(vector_copies(i, False))

        def load_field(q, carry):
            for part in range(2):
                for r in range(rows):
                    u0[part, q, r + 1] = gather(x_in, (2 * i + part, q), r)
                finish(u0, (part, q))
            return carry

        lax.fori_loop(0, reach[0], load_field, 0)

        def order_1(p, carry):
            keep = inside(p, 1)
            for part in range(2):
                for r0, n in pieces(rows):
                    centre, total = neighbour_sum(u0, (part,), p + 1, r0, n)
                    for stack in range(2):
                        u1[2 * stack + part, p, pl.ds(r0 + 1, n)] = keep * (
                            total - w[stack, p, pl.ds(r0, n)] * centre
                        )
            for chain in range(4):
                finish(u1, (chain, p))
            return carry

        lax.fori_loop(0, reach[1], order_1, 0)
        for k, source, target in ((2, u1, u2), (3, u2, u3)):

            def order_k(p, carry, k=k, source=source, target=target):
                keep = inside(p, k)
                for chain in range(4):
                    for r0, n in pieces(rows):
                        centre, total = neighbour_sum(source, (chain,), p + 1, r0, n)
                        target[chain, p, pl.ds(r0 + 1, n)] = keep * (
                            total - w[chain // 2, p + k - 1, pl.ds(r0, n)] * centre
                        )
                    finish(target, (chain, p))
                return carry

            lax.fori_loop(0, reach[k], order_k, 0)

        def last(p, carry):
            for r0, n in pieces(rows):
                at = pl.ds(r0 + 1, n)
                plain = pl.ds(r0, n)
                rho = acc[p, plain]
                for stack in range(2):
                    ev, od = [], []
                    for part in range(2):
                        chain = 2 * stack + part
                        centre, total = neighbour_sum(u3, (chain,), p + 1, r0, n)
                        fourth = total - w[stack, p + 3, plain] * centre
                        ev.append(
                            u0[part, p + 4, at]
                            - (s**2 / 2) * u2[chain, p + 2, at]
                            + (s**4 / 24) * fourth
                        )
                        od.append(s * u1[chain, p + 3, at] - (s**3 / 6) * centre)
                    real, imag = ev[0] - od[1], od[0] + ev[1]
                    size = real * real + imag * imag
                    rho = rho + size if stack else rho - size
                acc[p, plain] = rho
                for j in range(n):
                    scatter(b_out, (2 * i, p), r0 + j, real[j])
                    scatter(b_out, (2 * i + 1, p), r0 + j, imag[j])
            return carry

        lax.fori_loop(0, planes, last, 0)
        for copy in b_copies(i):
            copy.start()
        return carry

    lax.fori_loop(0, n_vectors, vector, 0)

    def spread(p, carry):
        for r in range(rows):
            scatter(r_out, (p,), r, acc[p, r])
        return carry

    lax.fori_loop(0, planes, spread, 0)
    out = [
        pltpu.make_async_copy(
            r_out.at[m, :, inner], rho_out.at[:, :, lanes(m)], o_sems.at[n_vectors * tiles + m]
        )
        for m in range(tiles)
    ]
    for copy in out:
        copy.start()
    for i in range(n_vectors):
        out += b_copies(i)
    for copy in out:
        copy.wait()


def taylor(span, flags, mask, own, potential, added, sources, b):
    n_fields, planes, size_y, size_z = own.shape
    out_rows, _, window = span
    height = window[1] - window[0]
    rows = height // SUBS
    tiles = size_z // LANES
    held = lambda *lead: pltpu.VMEM(lead + (rows + 2, SUBS, size_z), jnp.float32)
    plain = lambda *lead: pltpu.VMEM(lead + (rows, SUBS, size_z), jnp.float32)
    natural = lambda *lead: pltpu.VMEM((tiles,) + lead + (height, LANES), jnp.float32)
    hbm = pl.BlockSpec(memory_space=pl.ANY)
    smem = pl.BlockSpec(memory_space=pltpu.SMEM)
    shape = [(tuple(msgs), piece, to) for msgs, piece, to in sources]
    operands = [own, potential, added] + [m for msgs, _, _ in sources for m in msgs.values()]
    aliases = {}
    if b is not None:
        operands.append(b)
        aliases = {2 + len(operands) - 1: 0}
    return pl.pallas_call(
        functools.partial(taylor_kernel, span, shape, planes, b is None),
        out_shape=(
            jax.ShapeDtypeStruct(own.shape, jnp.float32),
            jax.ShapeDtypeStruct((planes, out_rows[1] - out_rows[0], size_z), jnp.float32),
        ),
        in_specs=[smem, smem] + [hbm] * len(operands),
        out_specs=(hbm, hbm),
        input_output_aliases=aliases,
        scratch_shapes=[
            natural(n_fields, planes + 8),
            natural(2, planes + 6),
            natural(n_fields, planes),
            natural(planes),
            held(2, planes + 8),
            held(4, planes + 6),
            held(4, planes + 4),
            held(4, planes + 2),
            plain(2, planes + 6),
            plain(planes),
            pltpu.SemaphoreType.DMA((tiles * (2 + 4 * len(sources)),)),
            pltpu.SemaphoreType.DMA((tiles * n_fields * (1 + 2 * len(sources)),)),
            pltpu.SemaphoreType.DMA((tiles * (n_fields // 2 + 1),)),
        ],
        cost_estimate=pl.CostEstimate(
            flops=rows * SUBS * size_z * planes * 120000, transcendentals=0, bytes_accessed=20 << 20
        ),
        name="taylor",
    )(flags, mask, *operands)


def elements_kernel(n_states, parts, last_step, rec_ref, add_ref, b_ref, q_ref, out_ref, acc):
    step = pl.program_id(0) * pl.num_programs(1) + pl.program_id(1)

    @pl.when(step == 0)
    def _():
        acc[...] = jnp.zeros_like(acc)

    field = rec_ref[0] + add_ref[0]
    group = 16
    total = acc[...]
    for g in range(field.shape[0] // group):
        at = slice(g * group, (g + 1) * group)
        weighted = [field[at] * b_ref[j, 0, at] for j in range(parts)]
        weighted = jnp.concatenate(weighted, axis=0).astype(jnp.bfloat16)
        states = q_ref[:, 0, at].reshape(n_states * group, field.shape[-1])
        total += lax.dot_general(
            states, weighted, (((1,), (1,)), ((), ())), preferred_element_type=jnp.float32
        )
    acc[...] = total

    @pl.when(step == last_step)
    def _():
        found = acc[...].reshape(n_states, group, parts * group)
        row = lax.broadcasted_iota(jnp.int32, found.shape, 1)
        col = lax.broadcasted_iota(jnp.int32, found.shape, 2)
        own = jnp.sum(jnp.where(row == col % group, found, 0.0), axis=1)
        fold_r = lax.broadcasted_iota(jnp.int32, (parts * group, parts), 0)
        fold_c = lax.broadcasted_iota(jnp.int32, (parts * group, parts), 1)
        fold = jnp.where(fold_r // group == fold_c, 1.0, 0.0)
        out_ref[...] = jnp.dot(own, fold, precision=highest, preferred_element_type=jnp.float32)


def elements(received, added, b, states):
    n_states, planes, size_y, size_z = states.shape
    block = 64
    parts = b.shape[0]
    grid = (planes, size_y // block)
    field = pl.BlockSpec((1, block, size_z), lambda p, y: (p, y, 0))
    vec = pl.BlockSpec((parts, 1, block, size_z), lambda p, y: (0, p, y, 0))
    return pl.pallas_call(
        functools.partial(elements_kernel, n_states, parts, planes * (size_y // block) - 1),
        grid=grid,
        out_shape=jax.ShapeDtypeStruct((n_states, parts), jnp.float32),
        in_specs=[field, field]
        + [vec]
        + [pl.BlockSpec((n_states, 1, block, size_z), lambda p, y: (0, p, y, 0))],
        out_specs=pl.BlockSpec((n_states, parts), lambda p, y: (0, 0)),
        scratch_shapes=[pltpu.VMEM((n_states * 16, parts * 16), jnp.float32)],
        name="elements",
    )(received, added, b, states)


def forward_yz(chunks, table_y, table_z):
    total, at = 0.0, 0
    for piece in chunks:
        count = piece.shape[1]
        field = jnp.einsum("xyz,zl->xyl", piece, table_z, precision=highest)
        total += jnp.einsum("xyl,yk->xkl", field, table_y[at : at + count], precision=highest)
        at += count
    return total


def poisson_block(chunks):
    planes, _, size_z = chunks[0].shape
    size_y = sum(piece.shape[1] for piece in chunks)
    full_x = planes * lax.axis_size("grid")
    table_x = sine_table(full_x)
    table_y = sine_table(size_y)
    table_z = sine_table(size_z)
    field = forward_yz(chunks, table_y, table_z)
    columns = lax.all_to_all(field, "grid", split_axis=1, concat_axis=0, tiled=True)
    row_count = columns.shape[1]
    own_rows = lax.dynamic_slice_in_dim(
        eigenvalues(size_y), lax.axis_index("grid") * row_count, row_count
    )
    field = jnp.einsum("xkl,xm->mkl", columns, table_x, precision=highest)
    spectrum = (
        eigenvalues(full_x)[:, None, None]
        + own_rows[None, :, None]
        + eigenvalues(size_z)[None, None, :]
    )
    field = field * (four_pi / spectrum)
    field = jnp.einsum("mkl,mx->xkl", field, table_x, precision=highest)
    returned = lax.all_to_all(field, "grid", split_axis=0, concat_axis=1, tiled=True)
    field = jnp.einsum("xkl,ky->xyl", returned, table_y, precision=highest)
    return jnp.einsum("xyl,lz->xyz", field, table_z, precision=highest)


def scatter_sum(value, axis):
    count = lax.axis_size(axis)
    place = lax.axis_index(axis)
    step = count // 2
    while step:
        half = value.shape[0] // 2
        upper = (place // step) % 2 == 1
        low, high = value[:half], value[half:]
        pairs = [(i, i ^ step) for i in range(count)]
        sent = lax.ppermute(jnp.where(upper, low, high), axis, pairs)
        value = jnp.where(upper, high, low) + sent
        step //= 2
    return value


def on_device(vectors, potential, added_field, qp_states):
    own = vectors.reshape((-1,) + vectors.shape[3:])
    added = added_field[0]
    count = lax.axis_size("grid")
    groups = lax.axis_size("grp")
    place = lax.axis_index("grid")
    n_fields, planes, size_y, size_z = own.shape
    assert planes == ORDER and n_fields == 6
    mask = jnp.stack([place > 0, place < count - 1]).astype(jnp.float32)
    relayed = count == 8
    middle = count // 2
    left, right = middle - 1, middle
    flags = jnp.stack([place == right, place == left]).astype(jnp.int32)
    keep = lambda pairs: [p for p in pairs if set(p) != {left, right}]
    forward, backward = neighbour_pairs(count)
    layout = spans(size_y, SHARES)

    fields = (potential, added)
    def exchange(c, after):
        _, (lo, hi), _ = layout[c]
        block, *parts = own, *fields
        if after is not None:
            (block, *parts), _ = lax.optimization_barrier(((own, *fields), after))
        block = block[:, :, lo:hi].reshape(-1, hi - lo, size_z)
        to_right = jnp.concatenate([block] + [f[1:, lo:hi] for f in parts])
        to_left = jnp.concatenate([block] + [f[:-1, lo:hi] for f in parts])
        if not relayed:
            return dict(
                low=lax.ppermute(to_right, "grid", forward),
                high=lax.ppermute(to_left, "grid", backward),
            )
        split = 4 * planes
        rest = jnp.where(place == left, to_right[split:], to_left[split:])
        first_leg = [(left, count - 1), (right, 0)]
        second_leg = [(count - 1, right), (0, left)]
        hop = lax.ppermute(rest, "grid", first_leg)
        return dict(
            low=lax.ppermute(to_right, "grid", keep(forward)),
            high=lax.ppermute(to_left, "grid", keep(backward)),
            direct=lax.ppermute(block[:split], "grid", [(left, right), (right, left)]),
            relay=lax.ppermute(hop, "grid", second_leg),
        )

    pairs = [(g, g + groups // 2) for g in range(groups // 2)]
    ahead = 3
    messages = [exchange(c, None) for c in range(min(ahead, len(layout)))]
    b, arrived = None, []
    for c, span in enumerate(layout):
        _, (lo, hi), window = span
        sources = []
        if c:
            before = layout[c - 1][1]
            sources.append(
                (messages[c - 1], (window[0] - before[0], lo - window[0]), 0)
            )
        sources.append((messages[c], (0, hi - lo), lo - window[0]))
        if c >= 2:
            b, arrived[c - 2] = lax.optimization_barrier((b, arrived[c - 2]))
        if c == len(layout) - 1:
            b, arrived[c - 1] = lax.optimization_barrier((b, arrived[c - 1]))
        b, rho = taylor(span, flags, mask, own, potential, added, sources, b)
        arrived.append(lax.ppermute(rho, "grp", pairs))
        if c + ahead < len(layout):
            messages.append(exchange(c + ahead, rho))
    received = poisson_block(arrived)
    partial = elements(received, added, b, qp_states)
    return scatter_sum(partial, "grid")[None]


def solution(mesh):
    in_specs = (
        P("grp", None, None, "grid", None, None),
        P("grid", None, None),
        P("grp", "grid", None, None),
        P(None, "grid", None, None),
    )
    out_specs = P("grp", "grid", None)
    return jax.shard_map(
        on_device, mesh=mesh, in_specs=in_specs, out_specs=out_specs, check_vma=False
    )
```

```python
import functools

import jax
import jax.numpy as jnp
from jax import lax
from jax.experimental import pallas as pl
from jax.experimental.pallas import tpu as pltpu
from jax.sharding import PartitionSpec as P

ORDER = 4
LANES = 128
SUBS = 8
SHARES = (10, 10, 8, 4)

time_step = 0.2
four_pi = 12.566370614359172
highest = lax.Precision.HIGHEST


def neighbour_pairs(count):
    forward = [(i, i + 1) for i in range(count - 1)]
    backward = [(i + 1, i) for i in range(count - 1)]
    return forward, backward


def sine_table(length):
    indices = jnp.arange(length, dtype=jnp.int32) + 1
    products = indices[:, None] * indices[None, :] % (2 * (length + 1))
    return jnp.sqrt(2.0 / (length + 1)) * jnp.sin(
        jnp.pi * products.astype(jnp.float32) / (length + 1)
    )


def eigenvalues(length):
    indices = jnp.arange(length, dtype=jnp.int32) + 1
    return 2.0 - 2.0 * jnp.cos(jnp.pi * indices.astype(jnp.float32) / (length + 1))


def edge_rows(first, last):
    sub = lax.broadcasted_iota(jnp.int32, first.shape, 0)
    before = jnp.where(sub == 0, 0.0, pltpu.roll(last, 1, 0))
    after = jnp.where(sub == SUBS - 1, 0.0, pltpu.roll(first, SUBS - 1, 0))
    return before, after


def across_lanes(tiles):
    shape = tiles[0].shape
    lane = lax.broadcasted_iota(jnp.int32, shape, len(shape) - 1)
    up = [pltpu.roll(t, 1, len(shape) - 1) for t in tiles]
    down = [pltpu.roll(t, LANES - 1, len(shape) - 1) for t in tiles]
    sums = []
    for m in range(len(tiles)):
        low = up[m - 1] if m > 0 else 0.0
        high = down[m + 1] if m < len(tiles) - 1 else 0.0
        sums.append(
            jnp.where(lane == 0, low, up[m]) + jnp.where(lane == LANES - 1, high, down[m])
        )
    return sums


def neighbour_sum(ref, lead, p, r0, n):
    block = ref[lead + (p, pl.ds(r0, n + 2))]
    x_low = ref[lead + (p - 1, pl.ds(r0 + 1, n))]
    x_high = ref[lead + (p + 1, pl.ds(r0 + 1, n))]
    centre = block[1:-1]
    plain = (block[2:] + block[:-2]) + (x_low + x_high)
    tiles = block.shape[-1] // LANES
    cut = lambda a, m: a[..., m * LANES : (m + 1) * LANES]
    z_sums = across_lanes([cut(centre, m) for m in range(tiles)])
    total = jnp.concatenate([cut(plain, m) + z_sums[m] for m in range(tiles)], axis=-1)
    return centre, total


def spans(size_y, shares):
    edges = [0]
    for share in shares:
        edges.append(edges[-1] + share * size_y // sum(shares))
    found, low = [], 0
    for o0, o1 in zip(edges[:-1], edges[1:]):
        high = min(o1 + SUBS, size_y)
        found.append(((o0, o1), (low, high), (max(o0 - SUBS, 0), high)))
        low = high
    return found


def pieces(rows):
    count = -(-rows // 5)
    sizes = [rows // count + (1 if j < rows % count else 0) for j in range(count)]
    starts = [sum(sizes[:j]) for j in range(count)]
    return list(zip(starts, sizes))


def taylor_kernel(
    span, sources, planes, first_call, flag_ref, mask_ref, own_ref, pot_ref, add_ref, mate_ref,
    mate_pot, mate_add, *refs
):
    out_rows, _, window = span
    msgs, refs = refs[: 2 * len(sources)], refs[2 * len(sources) :]
    if not first_call:
        refs = refs[1:]
    b_ref, rho_out, x_in, f_in, b_out, r_out, u0, u1, u2, u3, w, acc, f_sems, x_sems, o_sems = refs
    s = 0.5 * time_step
    halo = ORDER
    tiles, n_fields = x_in.shape[:2]
    n_vectors = n_fields // 2
    height = window[1] - window[0]
    rows = height // SUBS
    reach = [planes + 2 * (halo - k) for k in range(ORDER + 1)]
    lanes = lambda m: pl.ds(m * LANES, LANES)

    def own_copies(source, target, sem):
        at = pl.ds(window[0], height)
        return [
            (pltpu.make_async_copy(source.at[:, at, lanes(m)], target(m, pl.ds(0, height)), sem()), None, None)
            for m in range(tiles)
        ]

    def halo_copies(side, p0, n, mate, target, sem):
        found = []
        for j, ((start, size), to) in enumerate(sources):
            ref, p = msgs[2 * j], p0
            if not isinstance(p0, int):
                ref, p = msgs[2 * j + 1], 0
            elif p0 >= ref.shape[0]:
                ref, p = msgs[2 * j + 1], p0 - ref.shape[0]
            first = mate.shape[0] - n if side == "low" else 0
            for m in range(tiles):
                goal, done = target(m, pl.ds(to, size)), sem()
                near = pltpu.make_async_copy(
                    mate.at[pl.ds(first, n), pl.ds(window[0] + to, size), lanes(m)], goal, done
                )
                far = pltpu.make_async_copy(
                    ref.at[pl.ds(p, n), pl.ds(start, size), lanes(m)], goal, done
                )
                found.append((near, far, flag_ref[0 if side == "low" else 1]))
        return found

    def counter(sems, first=0):
        used = [0]

        def sem():
            used[0] += 1
            return sems.at[first + used[0] - 1]

        return sem

    def field_copies():
        sem, found = counter(f_sems), []
        for which, (ref, mate) in enumerate(((pot_ref, mate_pot), (add_ref, mate_add))):
            p0 = n_fields * planes + which * (halo - 1)
            for side, to in (("low", 0), ("high", halo - 1 + planes)):
                goal = lambda m, at, to=to: f_in.at[m, which, pl.ds(to, halo - 1), at]
                found += halo_copies(side, p0, halo - 1, mate, goal, sem)
            goal = lambda m, at: f_in.at[m, which, pl.ds(halo - 1, planes), at]
            found += own_copies(ref, goal, sem)
        return found

    per_vector = x_sems.shape[0] // n_vectors

    def vector_copies(i):
        sem, found = counter(x_sems, i * per_vector), []
        for part in range(2):
            j = 2 * i + part
            for side, to in (("low", 0), ("high", halo + planes)):
                goal = lambda m, at, to=to: x_in.at[m, j, pl.ds(to, halo), at]
                found += halo_copies(side, j * planes, halo, mate_ref.at[j], goal, sem)
            goal = lambda m, at: x_in.at[m, j, pl.ds(halo, planes), at]
            found += own_copies(own_ref.at[j], goal, sem)
        return found

    def start(copies):
        for near, far, flag in copies:
            if far is None:
                near.start()
            else:
                pl.when(flag == 0)(near.start)
                pl.when(flag == 1)(far.start)

    def wait(copies):
        for near, _, _ in copies:
            near.wait()

    start(field_copies())
    for i in range(n_vectors):
        start(vector_copies(i))

    def gather(ref, lead, r):
        at = pl.ds(r, SUBS, stride=rows)
        return jnp.concatenate([ref[(m,) + lead + (at, slice(None))] for m in range(tiles)], axis=1)

    def scatter(ref, lead, r, value):
        at = pl.ds(r, SUBS, stride=rows)
        for m in range(tiles):
            ref[(m,) + lead + (at, slice(None))] = value[:, m * LANES : (m + 1) * LANES]

    wait(field_copies())

    def load_w(q, carry):
        for r in range(rows):
            pot = 2.0 * gather(f_in, (0, q), r) + 6.0
            w[0, q, r] = pot
            w[1, q, r] = pot + 2.0 * gather(f_in, (1, q), r)
        return carry

    lax.fori_loop(0, reach[1], load_w, 0)
    acc[...] = jnp.zeros_like(acc)

    def finish(ref, lead):
        before, after = edge_rows(ref[lead + (1,)], ref[lead + (rows,)])
        ref[lead + (0,)] = before
        ref[lead + (rows + 1,)] = after

    def inside(p, k):
        side = halo - k
        low = jnp.where(p < side, mask_ref[0], 1.0)
        return jnp.where(p >= side + planes, mask_ref[1], low)

    out_count = out_rows[1] - out_rows[0]
    inner = pl.ds(out_rows[0] - window[0], out_count)

    def b_copies(i):
        return [
            pltpu.make_async_copy(
                b_out.at[m, pl.ds(2 * i, 2), :, inner],
                b_ref.at[pl.ds(2 * i, 2), :, pl.ds(out_rows[0], out_count), lanes(m)],
                o_sems.at[i * tiles + m],
            )
            for m in range(tiles)
        ]

    def vector(i, carry):
        wait(vector_copies(i))

        def load_field(q, carry):
            for part in range(2):
                for r in range(rows):
                    u0[part, q, r + 1] = gather(x_in, (2 * i + part, q), r)
                finish(u0, (part, q))
            return carry

        lax.fori_loop(0, reach[0], load_field, 0)

        def order_1(p, carry):
            keep = inside(p, 1)
            for part in range(2):
                for r0, n in pieces(rows):
                    centre, total = neighbour_sum(u0, (part,), p + 1, r0, n)
                    for stack in range(2):
                        u1[2 * stack + part, p, pl.ds(r0 + 1, n)] = keep * (
                            total - w[stack, p, pl.ds(r0, n)] * centre
                        )
            for chain in range(4):
                finish(u1, (chain, p))
            return carry

        lax.fori_loop(0, reach[1], order_1, 0)
        for k, source, target in ((2, u1, u2), (3, u2, u3)):

            def order_k(p, carry, k=k, source=source, target=target):
                keep = inside(p, k)
                for chain in range(4):
                    for r0, n in pieces(rows):
                        centre, total = neighbour_sum(source, (chain,), p + 1, r0, n)
                        target[chain, p, pl.ds(r0 + 1, n)] = keep * (
                            total - w[chain // 2, p + k - 1, pl.ds(r0, n)] * centre
                        )
                    finish(target, (chain, p))
                return carry

            lax.fori_loop(0, reach[k], order_k, 0)

        def last(p, carry):
            for r0, n in pieces(rows):
                at = pl.ds(r0 + 1, n)
                plain = pl.ds(r0, n)
                rho = acc[p, plain]
                for stack in range(2):
                    ev, od = [], []
                    for part in range(2):
                        chain = 2 * stack + part
                        centre, total = neighbour_sum(u3, (chain,), p + 1, r0, n)
                        fourth = total - w[stack, p + 3, plain] * centre
                        ev.append(
                            u0[part, p + 4, at]
                            - (s**2 / 2) * u2[chain, p + 2, at]
                            + (s**4 / 24) * fourth
                        )
                        od.append(s * u1[chain, p + 3, at] - (s**3 / 6) * centre)
                    real, imag = ev[0] - od[1], od[0] + ev[1]
                    size = real * real + imag * imag
                    rho = rho + size if stack else rho - size
                acc[p, plain] = rho
                for j in range(n):
                    scatter(b_out, (2 * i, p), r0 + j, real[j])
                    scatter(b_out, (2 * i + 1, p), r0 + j, imag[j])
            return carry

        lax.fori_loop(0, planes, last, 0)
        for copy in b_copies(i):
            copy.start()
        return carry

    lax.fori_loop(0, n_vectors, vector, 0)

    def spread(p, carry):
        for r in range(rows):
            scatter(r_out, (p,), r, acc[p, r])
        return carry

    lax.fori_loop(0, planes, spread, 0)
    out = [
        pltpu.make_async_copy(
            r_out.at[m, :, inner], rho_out.at[:, :, lanes(m)], o_sems.at[n_vectors * tiles + m]
        )
        for m in range(tiles)
    ]
    for copy in out:
        copy.start()
    for i in range(n_vectors):
        out += b_copies(i)
    for copy in out:
        copy.wait()


def taylor(span, flags, mask, own, potential, added, mates, sources, b):
    n_fields, planes, size_y, size_z = own.shape
    out_rows, _, window = span
    height = window[1] - window[0]
    rows = height // SUBS
    tiles = size_z // LANES
    held = lambda *lead: pltpu.VMEM(lead + (rows + 2, SUBS, size_z), jnp.float32)
    plain = lambda *lead: pltpu.VMEM(lead + (rows, SUBS, size_z), jnp.float32)
    natural = lambda *lead: pltpu.VMEM((tiles,) + lead + (height, LANES), jnp.float32)
    hbm = pl.BlockSpec(memory_space=pl.ANY)
    smem = pl.BlockSpec(memory_space=pltpu.SMEM)
    shape = [(piece, to) for _, piece, to in sources]
    operands = [own, potential, added, *mates] + [m for msgs, _, _ in sources for m in msgs]
    aliases = {}
    if b is not None:
        operands.append(b)
        aliases = {2 + len(operands) - 1: 0}
    return pl.pallas_call(
        functools.partial(taylor_kernel, span, shape, planes, b is None),
        out_shape=(
            jax.ShapeDtypeStruct(own.shape, jnp.float32),
            jax.ShapeDtypeStruct((planes, out_rows[1] - out_rows[0], size_z), jnp.float32),
        ),
        in_specs=[smem, smem] + [hbm] * len(operands),
        out_specs=(hbm, hbm),
        input_output_aliases=aliases,
        scratch_shapes=[
            natural(n_fields, planes + 8),
            natural(2, planes + 6),
            natural(n_fields, planes),
            natural(planes),
            held(2, planes + 8),
            held(4, planes + 6),
            held(4, planes + 4),
            held(4, planes + 2),
            plain(2, planes + 6),
            plain(planes),
            pltpu.SemaphoreType.DMA((tiles * (2 + 4 * len(sources)),)),
            pltpu.SemaphoreType.DMA((tiles * n_fields * (1 + 2 * len(sources)),)),
            pltpu.SemaphoreType.DMA((tiles * (n_fields // 2 + 1),)),
        ],
        cost_estimate=pl.CostEstimate(
            flops=rows * SUBS * size_z * planes * 120000, transcendentals=0, bytes_accessed=20 << 20
        ),
        name="taylor",
    )(flags, mask, *operands)


def elements_kernel(n_states, parts, last_step, rec_ref, add_ref, b_ref, q_ref, out_ref, acc):
    step = pl.program_id(0) * pl.num_programs(1) + pl.program_id(1)

    @pl.when(step == 0)
    def _():
        acc[...] = jnp.zeros_like(acc)

    field = rec_ref[0] + add_ref[0]
    group = 16
    total = acc[...]
    for g in range(field.shape[0] // group):
        at = slice(g * group, (g + 1) * group)
        weighted = [field[at] * b_ref[j, 0, at] for j in range(parts)]
        weighted = jnp.concatenate(weighted, axis=0).astype(jnp.bfloat16)
        states = q_ref[:, 0, at].reshape(n_states * group, field.shape[-1])
        total += lax.dot_general(
            states, weighted, (((1,), (1,)), ((), ())), preferred_element_type=jnp.float32
        )
    acc[...] = total

    @pl.when(step == last_step)
    def _():
        found = acc[...].reshape(n_states, group, parts * group)
        row = lax.broadcasted_iota(jnp.int32, found.shape, 1)
        col = lax.broadcasted_iota(jnp.int32, found.shape, 2)
        own = jnp.sum(jnp.where(row == col % group, found, 0.0), axis=1)
        fold_r = lax.broadcasted_iota(jnp.int32, (parts * group, parts), 0)
        fold_c = lax.broadcasted_iota(jnp.int32, (parts * group, parts), 1)
        fold = jnp.where(fold_r // group == fold_c, 1.0, 0.0)
        out_ref[...] = jnp.dot(own, fold, precision=highest, preferred_element_type=jnp.float32)


def elements(received, added, b, states):
    n_states, planes, size_y, size_z = states.shape
    block = 64
    parts = b.shape[0]
    grid = (planes, size_y // block)
    field = pl.BlockSpec((1, block, size_z), lambda p, y: (p, y, 0))
    vec = pl.BlockSpec((parts, 1, block, size_z), lambda p, y: (0, p, y, 0))
    return pl.pallas_call(
        functools.partial(elements_kernel, n_states, parts, planes * (size_y // block) - 1),
        grid=grid,
        out_shape=jax.ShapeDtypeStruct((n_states, parts), jnp.float32),
        in_specs=[field, field]
        + [vec]
        + [pl.BlockSpec((n_states, 1, block, size_z), lambda p, y: (0, p, y, 0))],
        out_specs=pl.BlockSpec((n_states, parts), lambda p, y: (0, 0)),
        scratch_shapes=[pltpu.VMEM((n_states * 16, parts * 16), jnp.float32)],
        name="elements",
    )(received, added, b, states)


def moments_kernel(f_ref, low_ref, high_ref, r_ref, to_right, to_left):
    planes = f_ref.shape[0]

    def step(q, carry):
        at = pl.ds(pl.multiple_of(q * SUBS, SUBS), SUBS)
        r = r_ref[at, :]
        up = low_ref[0, at, :] * f_ref[0, at, :]
        for j in range(1, planes):
            up = r * up + low_ref[j, at, :] * f_ref[j, at, :]
        down = high_ref[planes - 1, at, :] * f_ref[planes - 1, at, :]
        for j in range(planes - 2, -1, -1):
            down = r * down + high_ref[j, at, :] * f_ref[j, at, :]
        to_right[at, :] = up
        to_left[at, :] = down
        return carry

    lax.fori_loop(0, f_ref.shape[1] // SUBS, step, 0, unroll=4)


def solve_kernel(n_far, side_ref, f_ref, low_ref, high_ref, r_ref, scale_ref, *refs):
    far, decay, out = refs[:n_far], refs[n_far : 2 * n_far], refs[2 * n_far]
    planes = f_ref.shape[0]

    def step(q, carry):
        at = pl.ds(pl.multiple_of(q * SUBS, SUBS), SUBS)
        r = r_ref[at, :]
        up, down = jnp.zeros_like(r), jnp.zeros_like(r)
        for k in range(n_far):
            value = decay[k][at, :] * far[k][at, :]
            up = up + side_ref[k] * value
            down = down + (1.0 - side_ref[k]) * value
        below = []
        for j in range(planes):
            up = r * up + low_ref[j, at, :] * f_ref[j, at, :]
            below.append(up)
        for j in range(planes - 1, -1, -1):
            down = r * down
            out[j, at, :] = scale_ref[at, :] * (
                high_ref[j, at, :] * below[j] + low_ref[j, at, :] * down
            )
            down = down + high_ref[j, at, :] * f_ref[j, at, :]
        return carry

    lax.fori_loop(0, f_ref.shape[1] // SUBS, step, 0, unroll=2)


class Poisson:
    def __init__(self, planes, size_y, size_z):
        self.count = lax.axis_size("grid")
        self.place = lax.axis_index("grid")
        self.chip, self.core = self.place // 2, self.place % 2
        self.first = self.core == 0
        self.planes, self.half = planes, size_z // 2
        self.table_y, self.table_z = sine_table(size_y), sine_table(size_z)
        full_x = planes * self.count
        sine_half = lambda n: jnp.sin(
            (0.5 * jnp.pi / (n + 1)) * (jnp.arange(n, dtype=jnp.int32) + 1).astype(jnp.float32)
        )
        of_y = 4.0 * sine_half(size_y) ** 2
        of_z = self.pick(4.0 * sine_half(size_z) ** 2, True)
        mu = of_y[:, None] + of_z[None, :]
        root = jnp.sqrt(mu + 0.25 * mu * mu)
        theta = jnp.log1p(0.5 * mu + root)
        self.r = jnp.exp(-theta)
        x = (2 * planes * self.chip + jnp.arange(2 * planes)).astype(jnp.float32)[:, None, None]
        self.low = -jnp.expm1(-2.0 * theta * (x + 1.0))
        self.high = -jnp.expm1(-2.0 * theta * (full_x - x))
        self.scale = four_pi / (-2.0 * root * jnp.expm1(-2.0 * (full_x + 1) * theta))
        self.hops = list(range(1, self.count // 2))
        other = [self.chip ^ k for k in self.hops]
        self.side = jnp.stack([o < self.chip for o in other]).astype(jnp.float32)
        self.decay = [
            jnp.exp(-(2.0 * planes) * theta * (jnp.abs(o - self.chip) - 1).astype(jnp.float32))
            for o in other
        ]
        self.total = 0.0

    def pick(self, array, mine):
        take = self.first if mine else jnp.logical_not(self.first)
        return jnp.where(take, array[..., : self.half], array[..., self.half :])

    def swap(self, array):
        return lax.ppermute(array, "grid", [(i, i ^ 1) for i in range(self.count)])

    def transform_z(self, density):
        return jnp.einsum("xyz,zl->xyl", density, self.table_z, precision=highest)

    def add(self, piece, at):
        mine, got = self.pick(piece, True), self.swap(self.pick(piece, False))
        both = jnp.where(
            self.first, jnp.concatenate([mine, got]), jnp.concatenate([got, mine])
        )
        rows = self.table_y[at : at + piece.shape[1]]
        self.total += jnp.einsum("xyl,yk->xkl", both, rows, precision=highest)

    def solve(self):
        shape = jax.ShapeDtypeStruct(self.r.shape, jnp.float32)
        vmem = pl.BlockSpec(memory_space=pltpu.VMEM)
        to_right, to_left = pl.pallas_call(
            moments_kernel,
            out_shape=(shape, shape),
            in_specs=[vmem] * 4,
            out_specs=(vmem, vmem),
            name="moments",
        )(self.total, self.low, self.high, self.r)
        far = []
        for k in self.hops:
            sent = jnp.where((self.chip ^ k) > self.chip, to_right, to_left)
            far.append(
                lax.ppermute(sent, "grid", [(i, i ^ (2 * k)) for i in range(self.count)])
            )
        field = pl.pallas_call(
            functools.partial(solve_kernel, len(far)),
            out_shape=jax.ShapeDtypeStruct(self.total.shape, jnp.float32),
            in_specs=[pl.BlockSpec(memory_space=pltpu.SMEM)] + [vmem] * (5 + 2 * len(far)),
            out_specs=vmem,
            name="solve",
        )(self.side, self.total, self.low, self.high, self.r, self.scale, *far, *self.decay)
        field = jnp.einsum("xkl,ky->xyl", field, self.table_y, precision=highest)
        lower, upper = field[: self.planes], field[self.planes :]
        mine = jnp.where(self.first, lower, upper)
        got = self.swap(jnp.where(self.first, upper, lower))
        flip = lambda mine: self.pick(self.table_z.T, mine).T
        back = lambda part, table: jnp.einsum("xyl,lz->xyz", part, table, precision=highest)
        return back(mine, flip(True)) + back(got, flip(False))


def scatter_sum(value, axis):
    count = lax.axis_size(axis)
    place = lax.axis_index(axis)
    step = count // 2
    while step:
        half = value.shape[0] // 2
        upper = (place // step) % 2 == 1
        low, high = value[:half], value[half:]
        pairs = [(i, i ^ step) for i in range(count)]
        sent = lax.ppermute(jnp.where(upper, low, high), axis, pairs)
        value = jnp.where(upper, high, low) + sent
        step //= 2
    return value


def on_device(vectors, potential, added_field, qp_states):
    own = vectors.reshape((-1,) + vectors.shape[3:])
    added = added_field[0]
    count = lax.axis_size("grid")
    groups = lax.axis_size("grp")
    place = lax.axis_index("grid")
    n_fields, planes, size_y, size_z = own.shape
    assert planes == ORDER and n_fields == 6
    assert count % 2 == 0
    mask = jnp.stack([place > 0, place < count - 1]).astype(jnp.float32)
    even = place % 2 == 0
    flags = jnp.stack([even, jnp.logical_not(even)]).astype(jnp.int32)
    mate_pairs = [(i, i ^ 1) for i in range(count)]
    chip_pairs = []
    for i in range(1, count - 1, 2):
        chip_pairs += [(i, i + 1), (i + 1, i)]
    relayed = count == 8
    left, right = count // 2 - 1, count // 2
    first_leg = [(left, count - 1), (right, 0)]
    second_leg = [(count - 1, right), (0, left)]
    layout = spans(size_y, SHARES)
    split = 4

    def message(lo, hi):
        edge = lambda f: jnp.where(even, f[:-1, lo:hi], f[1:, lo:hi])
        parts = [own[split:, :, lo:hi].reshape(-1, hi - lo, size_z), edge(potential), edge(added)]
        return jnp.concatenate(parts)

    cut = layout[0][1][1]
    hops = [None] * len(layout)
    if relayed:
        hops[0] = lax.ppermute(message(0, cut), "grid", first_leg)
    messages = []
    mates = None
    for c, (_, (lo, hi), _) in enumerate(layout):
        block = own[:split, :, lo:hi].reshape(-1, hi - lo, size_z)
        direct = lax.ppermute(block, "grid", chip_pairs)
        rest, pairs = message(lo, hi), chip_pairs
        if mates is None:
            mates = [lax.ppermute(f, "grid", mate_pairs) for f in (own, potential, added)]
        if relayed:
            if c == 1:
                late = lax.ppermute(message(cut, size_y), "grid", first_leg)
                hops[1:] = [late[:, l - cut : h - cut] for _, (l, h), _ in layout[1:]]
            ends = jnp.logical_or(place == 0, place == count - 1)
            rest = jnp.where(ends, hops[c], rest)
            pairs = [p for p in chip_pairs if set(p) != {left, right}] + second_leg
        messages.append((direct, lax.ppermute(rest, "grid", pairs)))

    poisson = Poisson(planes, size_y, size_z)
    group_pairs = [(g, g + groups // 2) for g in range(groups // 2)]
    b, arrived = None, []
    for c, span in enumerate(layout):
        _, (lo, hi), window = span
        sources = []
        if c:
            before = layout[c - 1][1]
            sources.append((messages[c - 1], (window[0] - before[0], lo - window[0]), 0))
        sources.append((messages[c], (0, hi - lo), lo - window[0]))
        if c >= 2:
            b, arrived[c - 2] = lax.optimization_barrier((b, arrived[c - 2]))
        if c == len(layout) - 1:
            b, arrived[c - 1] = lax.optimization_barrier((b, arrived[c - 1]))
        b, rho = taylor(span, flags, mask, own, potential, added, mates, sources, b)
        arrived.append(lax.ppermute(poisson.transform_z(rho), "grp", group_pairs))
    for c, ((o0, _), _, _) in enumerate(layout):
        poisson.add(arrived[c], o0)
    received = poisson.solve()
    partial = elements(received, added, b, qp_states)
    return scatter_sum(partial, "grid")[None]


def solution(mesh):
    in_specs = (
        P("grp", None, None, "grid", None, None),
        P("grid", None, None),
        P("grp", "grid", None, None),
        P(None, "grid", None, None),
    )
    out_specs = P("grp", "grid", None)
    return jax.shard_map(
        on_device, mesh=mesh, in_specs=in_specs, out_specs=out_specs, check_vma=False
    )
```

```python
import functools

import jax
import jax.numpy as jnp
from jax import lax
from jax.experimental import pallas as pl
from jax.experimental.pallas import tpu as pltpu
from jax.sharding import PartitionSpec as P


ORDER = 4
LANES = 128
SUBS = 8
SHARES = (6, 10, 10, 6)

time_step = 0.2
four_pi = 12.566370614359172
highest = lax.Precision.HIGHEST


def sine_table(length):
    indices = jnp.arange(length, dtype=jnp.int32) + 1
    products = indices[:, None] * indices[None, :] % (2 * (length + 1))
    return jnp.sqrt(2.0 / (length + 1)) * jnp.sin(
        jnp.pi * products.astype(jnp.float32) / (length + 1)
    )


def edge_rows(first, last):
    sub = lax.broadcasted_iota(jnp.int32, first.shape, 0)
    before = jnp.where(sub == 0, 0.0, pltpu.roll(last, 1, 0))
    after = jnp.where(sub == SUBS - 1, 0.0, pltpu.roll(first, SUBS - 1, 0))
    return before, after


def across_lanes(tiles):
    shape = tiles[0].shape
    lane = lax.broadcasted_iota(jnp.int32, shape, len(shape) - 1)
    up = [pltpu.roll(t, 1, len(shape) - 1) for t in tiles]
    down = [pltpu.roll(t, LANES - 1, len(shape) - 1) for t in tiles]
    sums = []
    for m in range(len(tiles)):
        low = up[m - 1] if m > 0 else 0.0
        high = down[m + 1] if m < len(tiles) - 1 else 0.0
        sums.append(
            jnp.where(lane == 0, low, up[m]) + jnp.where(lane == LANES - 1, high, down[m])
        )
    return sums


def neighbour_sum(ref, lead, p, r0, n):
    block = ref[lead + (p, pl.ds(r0, n + 2))]
    x_low = ref[lead + (p - 1, pl.ds(r0 + 1, n))]
    x_high = ref[lead + (p + 1, pl.ds(r0 + 1, n))]
    centre = block[1:-1]
    plain = (block[2:] + block[:-2]) + (x_low + x_high)
    tiles = block.shape[-1] // LANES
    cut = lambda a, m: a[..., m * LANES : (m + 1) * LANES]
    z_sums = across_lanes([cut(centre, m) for m in range(tiles)])
    total = jnp.concatenate([cut(plain, m) + z_sums[m] for m in range(tiles)], axis=-1)
    return centre, total


def spans(size_y, shares):
    edges = [0]
    for share in shares:
        edges.append(edges[-1] + share * size_y // sum(shares))
    found, low = [], 0
    for o0, o1 in zip(edges[:-1], edges[1:]):
        high = min(o1 + SUBS, size_y)
        found.append(((o0, o1), (low, high), (max(o0 - SUBS, 0), high)))
        low = high
    return found


def pieces(rows):
    count = -(-rows // 5)
    sizes = [rows // count + (1 if j < rows % count else 0) for j in range(count)]
    starts = [sum(sizes[:j]) for j in range(count)]
    return list(zip(starts, sizes))


def taylor_kernel(
    span, sources, planes, first_call, flag_ref, mask_ref, own_ref, pot_ref, add_ref, mate_ref,
    mate_pot, mate_add, *refs
):
    out_rows, _, window = span
    msgs, refs = refs[: 2 * len(sources)], refs[2 * len(sources) :]
    if not first_call:
        refs = refs[1:]
    b_ref, rho_out, x_in, f_in, b_out, r_out, u0, u1, u2, u3, w, acc, f_sems, x_sems, o_sems = refs
    s = 0.5 * time_step
    halo = ORDER
    tiles, n_fields = x_in.shape[:2]
    n_vectors = n_fields // 2
    height = window[1] - window[0]
    rows = height // SUBS
    reach = [planes + 2 * (halo - k) for k in range(ORDER + 1)]
    lanes = lambda m: pl.ds(m * LANES, LANES)

    def own_copies(source, target, sem):
        at = pl.ds(window[0], height)
        return [
            (pltpu.make_async_copy(source.at[:, at, lanes(m)], target(m, pl.ds(0, height)), sem()), None, None)
            for m in range(tiles)
        ]

    def halo_copies(side, p0, n, mate, target, sem):
        found = []
        for j, ((start, size), to) in enumerate(sources):
            ref, p = msgs[2 * j], p0
            if not isinstance(p0, int):
                ref, p = msgs[2 * j + 1], 0
            elif p0 >= ref.shape[0]:
                ref, p = msgs[2 * j + 1], p0 - ref.shape[0]
            first = mate.shape[0] - n if side == "low" else 0
            for m in range(tiles):
                goal, done = target(m, pl.ds(to, size)), sem()
                near = pltpu.make_async_copy(
                    mate.at[pl.ds(first, n), pl.ds(window[0] + to, size), lanes(m)], goal, done
                )
                far = pltpu.make_async_copy(
                    ref.at[pl.ds(p, n), pl.ds(start, size), lanes(m)], goal, done
                )
                found.append((near, far, flag_ref[0 if side == "low" else 1]))
        return found

    def counter(sems, first=0):
        used = [0]

        def sem():
            used[0] += 1
            return sems.at[first + used[0] - 1]

        return sem

    def field_copies():
        sem, found = counter(f_sems), []
        for which, (ref, mate) in enumerate(((pot_ref, mate_pot), (add_ref, mate_add))):
            p0 = n_fields * planes + which * (halo - 1)
            for side, to in (("low", 0), ("high", halo - 1 + planes)):
                goal = lambda m, at, to=to: f_in.at[m, which, pl.ds(to, halo - 1), at]
                found += halo_copies(side, p0, halo - 1, mate, goal, sem)
            goal = lambda m, at: f_in.at[m, which, pl.ds(halo - 1, planes), at]
            found += own_copies(ref, goal, sem)
        return found

    per_vector = x_sems.shape[0] // n_vectors

    def vector_copies(i):
        sem, found = counter(x_sems, i * per_vector), []
        for part in range(2):
            j = 2 * i + part
            for side, to in (("low", 0), ("high", halo + planes)):
                goal = lambda m, at, to=to: x_in.at[m, j, pl.ds(to, halo), at]
                found += halo_copies(side, j * planes, halo, mate_ref.at[j], goal, sem)
            goal = lambda m, at: x_in.at[m, j, pl.ds(halo, planes), at]
            found += own_copies(own_ref.at[j], goal, sem)
        return found

    def start(copies):
        for near, far, flag in copies:
            if far is None:
                near.start()
            else:
                pl.when(flag == 0)(near.start)
                pl.when(flag == 1)(far.start)

    def wait(copies):
        for near, _, _ in copies:
            near.wait()

    start(field_copies())
    for i in range(n_vectors):
        start(vector_copies(i))

    def gather(ref, lead, r):
        at = pl.ds(r, SUBS, stride=rows)
        return jnp.concatenate([ref[(m,) + lead + (at, slice(None))] for m in range(tiles)], axis=1)

    def scatter(ref, lead, r, value):
        at = pl.ds(r, SUBS, stride=rows)
        for m in range(tiles):
            ref[(m,) + lead + (at, slice(None))] = value[:, m * LANES : (m + 1) * LANES]

    wait(field_copies())

    def load_w(q, carry):
        for r in range(rows):
            pot = 2.0 * gather(f_in, (0, q), r) + 6.0
            w[0, q, r] = pot
            w[1, q, r] = pot + 2.0 * gather(f_in, (1, q), r)
        return carry

    lax.fori_loop(0, reach[1], load_w, 0)
    acc[...] = jnp.zeros_like(acc)

    def finish(ref, lead):
        before, after = edge_rows(ref[lead + (1,)], ref[lead + (rows,)])
        ref[lead + (0,)] = before
        ref[lead + (rows + 1,)] = after

    def inside(p, k):
        side = halo - k
        low = jnp.where(p < side, mask_ref[0], 1.0)
        return jnp.where(p >= side + planes, mask_ref[1], low)

    out_count = out_rows[1] - out_rows[0]
    inner = pl.ds(out_rows[0] - window[0], out_count)

    def b_copies(i):
        return [
            pltpu.make_async_copy(
                b_out.at[m, pl.ds(2 * i, 2), :, inner],
                b_ref.at[pl.ds(2 * i, 2), :, pl.ds(out_rows[0], out_count), lanes(m)],
                o_sems.at[i * tiles + m],
            )
            for m in range(tiles)
        ]

    def vector(i, carry):
        wait(vector_copies(i))

        def load_field(q, carry):
            for part in range(2):
                for r in range(rows):
                    u0[part, q, r + 1] = gather(x_in, (2 * i + part, q), r)
                finish(u0, (part, q))
            return carry

        lax.fori_loop(0, reach[0], load_field, 0)

        def order_1(p, carry):
            keep = inside(p, 1)
            for part in range(2):
                for r0, n in pieces(rows):
                    centre, total = neighbour_sum(u0, (part,), p + 1, r0, n)
                    for stack in range(2):
                        u1[2 * stack + part, p, pl.ds(r0 + 1, n)] = keep * (
                            total - w[stack, p, pl.ds(r0, n)] * centre
                        )
            for chain in range(4):
                finish(u1, (chain, p))
            return carry

        lax.fori_loop(0, reach[1], order_1, 0)
        for k, source, target in ((2, u1, u2), (3, u2, u3)):

            def order_k(p, carry, k=k, source=source, target=target):
                keep = inside(p, k)
                for chain in range(4):
                    for r0, n in pieces(rows):
                        centre, total = neighbour_sum(source, (chain,), p + 1, r0, n)
                        target[chain, p, pl.ds(r0 + 1, n)] = keep * (
                            total - w[chain // 2, p + k - 1, pl.ds(r0, n)] * centre
                        )
                    finish(target, (chain, p))
                return carry

            lax.fori_loop(0, reach[k], order_k, 0)

        def last(p, carry):
            for r0, n in pieces(rows):
                at = pl.ds(r0 + 1, n)
                plain = pl.ds(r0, n)
                rho = acc[p, plain]
                for stack in range(2):
                    ev, od = [], []
                    for part in range(2):
                        chain = 2 * stack + part
                        centre, total = neighbour_sum(u3, (chain,), p + 1, r0, n)
                        fourth = total - w[stack, p + 3, plain] * centre
                        ev.append(
                            u0[part, p + 4, at]
                            - (s**2 / 2) * u2[chain, p + 2, at]
                            + (s**4 / 24) * fourth
                        )
                        od.append(s * u1[chain, p + 3, at] - (s**3 / 6) * centre)
                    real, imag = ev[0] - od[1], od[0] + ev[1]
                    size = real * real + imag * imag
                    rho = rho + size if stack else rho - size
                acc[p, plain] = rho
                for j in range(n):
                    scatter(b_out, (2 * i, p), r0 + j, real[j])
                    scatter(b_out, (2 * i + 1, p), r0 + j, imag[j])
            return carry

        lax.fori_loop(0, planes, last, 0)
        for copy in b_copies(i):
            copy.start()
        return carry

    lax.fori_loop(0, n_vectors, vector, 0)

    def spread(p, carry):
        for r in range(rows):
            scatter(r_out, (p,), r, acc[p, r])
        return carry

    lax.fori_loop(0, planes, spread, 0)
    out = [
        pltpu.make_async_copy(
            r_out.at[m, :, inner], rho_out.at[:, :, lanes(m)], o_sems.at[n_vectors * tiles + m]
        )
        for m in range(tiles)
    ]
    for copy in out:
        copy.start()
    for i in range(n_vectors):
        out += b_copies(i)
    for copy in out:
        copy.wait()


def taylor(span, flags, mask, own, potential, added, mates, sources, b):
    n_fields, planes, _, size_z = own.shape
    out_rows, _, window = span
    height = window[1] - window[0]
    rows = height // SUBS
    tiles = size_z // LANES
    held = lambda *lead: pltpu.VMEM(lead + (rows + 2, SUBS, size_z), jnp.float32)
    plain = lambda *lead: pltpu.VMEM(lead + (rows, SUBS, size_z), jnp.float32)
    natural = lambda *lead: pltpu.VMEM((tiles,) + lead + (height, LANES), jnp.float32)
    hbm = pl.BlockSpec(memory_space=pl.ANY)
    smem = pl.BlockSpec(memory_space=pltpu.SMEM)
    shape = [(piece, to) for _, piece, to in sources]
    operands = [own, potential, added, *mates] + [m for msgs, _, _ in sources for m in msgs]
    aliases = {}
    if b is not None:
        operands.append(b)
        aliases = {2 + len(operands) - 1: 0}
    return pl.pallas_call(
        functools.partial(taylor_kernel, span, shape, planes, b is None),
        out_shape=(
            jax.ShapeDtypeStruct(own.shape, jnp.float32),
            jax.ShapeDtypeStruct((planes, out_rows[1] - out_rows[0], size_z), jnp.float32),
        ),
        in_specs=[smem, smem] + [hbm] * len(operands),
        out_specs=(hbm, hbm),
        input_output_aliases=aliases,
        scratch_shapes=[
            natural(n_fields, planes + 8),
            natural(2, planes + 6),
            natural(n_fields, planes),
            natural(planes),
            held(2, planes + 8),
            held(4, planes + 6),
            held(4, planes + 4),
            held(4, planes + 2),
            plain(2, planes + 6),
            plain(planes),
            pltpu.SemaphoreType.DMA((tiles * (2 + 4 * len(sources)),)),
            pltpu.SemaphoreType.DMA((tiles * n_fields * (1 + 2 * len(sources)),)),
            pltpu.SemaphoreType.DMA((tiles * (n_fields // 2 + 1),)),
        ],
        cost_estimate=pl.CostEstimate(
            flops=rows * SUBS * size_z * planes * 120000, transcendentals=0, bytes_accessed=20 << 20
        ),
        name="taylor",
    )(flags, mask, *operands)


def elements_kernel(n_states, parts, last_step, rec_ref, add_ref, b_ref, q_ref, out_ref, acc):
    step = pl.program_id(0) * pl.num_programs(1) + pl.program_id(1)

    @pl.when(step == 0)
    def _():
        acc[...] = jnp.zeros_like(acc)

    field = rec_ref[0] + add_ref[0]
    group = 16
    total = acc[...]
    for g in range(field.shape[0] // group):
        at = slice(g * group, (g + 1) * group)
        weighted = [field[at] * b_ref[j, 0, at] for j in range(parts)]
        weighted = jnp.concatenate(weighted, axis=0).astype(jnp.bfloat16)
        states = q_ref[:, 0, at].reshape(n_states * group, field.shape[-1])
        total += lax.dot_general(
            states, weighted, (((1,), (1,)), ((), ())), preferred_element_type=jnp.float32
        )
    acc[...] = total

    @pl.when(step == last_step)
    def _():
        found = acc[...].reshape(n_states, group, parts * group)
        row = lax.broadcasted_iota(jnp.int32, found.shape, 1)
        col = lax.broadcasted_iota(jnp.int32, found.shape, 2)
        own = jnp.sum(jnp.where(row == col % group, found, 0.0), axis=1)
        fold_r = lax.broadcasted_iota(jnp.int32, (parts * group, parts), 0)
        fold_c = lax.broadcasted_iota(jnp.int32, (parts * group, parts), 1)
        fold = jnp.where(fold_r // group == fold_c, 1.0, 0.0)
        out_ref[...] = jnp.dot(own, fold, precision=highest, preferred_element_type=jnp.float32)


def elements(received, added, b, states):
    n_states, planes, size_y, size_z = states.shape
    block = 64
    parts = b.shape[0]
    grid = (planes, size_y // block)
    field = pl.BlockSpec((1, block, size_z), lambda p, y: (p, y, 0))
    vec = pl.BlockSpec((parts, 1, block, size_z), lambda p, y: (0, p, y, 0))
    return pl.pallas_call(
        functools.partial(elements_kernel, n_states, parts, planes * (size_y // block) - 1),
        grid=grid,
        out_shape=jax.ShapeDtypeStruct((n_states, parts), jnp.float32),
        in_specs=[field, field]
        + [vec]
        + [pl.BlockSpec((n_states, 1, block, size_z), lambda p, y: (0, p, y, 0))],
        out_specs=pl.BlockSpec((n_states, parts), lambda p, y: (0, 0)),
        scratch_shapes=[pltpu.VMEM((n_states * 16, parts * 16), jnp.float32)],
        name="elements",
    )(received, added, b, states)


def moments_kernel(f_ref, low_ref, high_ref, r_ref, to_right, to_left):
    planes = f_ref.shape[0]

    def step(q, carry):
        at = pl.ds(pl.multiple_of(q * SUBS, SUBS), SUBS)
        r = r_ref[at, :]
        up = low_ref[0, at, :] * f_ref[0, at, :]
        for j in range(1, planes):
            up = r * up + low_ref[j, at, :] * f_ref[j, at, :]
        down = high_ref[planes - 1, at, :] * f_ref[planes - 1, at, :]
        for j in range(planes - 2, -1, -1):
            down = r * down + high_ref[j, at, :] * f_ref[j, at, :]
        to_right[at, :] = up
        to_left[at, :] = down
        return carry

    lax.fori_loop(0, f_ref.shape[1] // SUBS, step, 0, unroll=4)


def solve_kernel(n_far, side_ref, f_ref, low_ref, high_ref, r_ref, scale_ref, *refs):
    far, decay, out = refs[:n_far], refs[n_far : 2 * n_far], refs[2 * n_far]
    planes = f_ref.shape[0]

    def step(q, carry):
        at = pl.ds(pl.multiple_of(q * SUBS, SUBS), SUBS)
        r = r_ref[at, :]
        up, down = jnp.zeros_like(r), jnp.zeros_like(r)
        for k in range(n_far):
            value = decay[k][at, :] * far[k][at, :]
            up = up + side_ref[k] * value
            down = down + (1.0 - side_ref[k]) * value
        below = []
        for j in range(planes):
            up = r * up + low_ref[j, at, :] * f_ref[j, at, :]
            below.append(up)
        for j in range(planes - 1, -1, -1):
            down = r * down
            out[j, at, :] = scale_ref[at, :] * (
                high_ref[j, at, :] * below[j] + low_ref[j, at, :] * down
            )
            down = down + high_ref[j, at, :] * f_ref[j, at, :]
        return carry

    lax.fori_loop(0, f_ref.shape[1] // SUBS, step, 0, unroll=2)


class Poisson:
    def __init__(self, planes, size_y, size_z):
        self.count = lax.axis_size("grid")
        self.place = lax.axis_index("grid")
        self.chip, self.core = self.place // 2, self.place % 2
        self.first = self.core == 0
        self.planes, self.half = planes, size_z // 2
        self.table_y, self.table_z = sine_table(size_y), sine_table(size_z)
        full_x = planes * self.count
        sine_half = lambda n: jnp.sin(
            (0.5 * jnp.pi / (n + 1)) * (jnp.arange(n, dtype=jnp.int32) + 1).astype(jnp.float32)
        )
        of_y = 4.0 * sine_half(size_y) ** 2
        of_z = self.pick(4.0 * sine_half(size_z) ** 2, True)
        mu = of_y[:, None] + of_z[None, :]
        root = jnp.sqrt(mu + 0.25 * mu * mu)
        theta = jnp.log1p(0.5 * mu + root)
        self.r = jnp.exp(-theta)
        x = (2 * planes * self.chip + jnp.arange(2 * planes)).astype(jnp.float32)[:, None, None]
        self.low = -jnp.expm1(-2.0 * theta * (x + 1.0))
        self.high = -jnp.expm1(-2.0 * theta * (full_x - x))
        self.scale = four_pi / (-2.0 * root * jnp.expm1(-2.0 * (full_x + 1) * theta))
        self.hops = list(range(1, self.count // 2))
        other = [self.chip ^ k for k in self.hops]
        self.side = jnp.stack([o < self.chip for o in other]).astype(jnp.float32)
        self.decay = [
            jnp.exp(-(2.0 * planes) * theta * (jnp.abs(o - self.chip) - 1).astype(jnp.float32))
            for o in other
        ]
        self.total = 0.0

    def pick(self, array, mine):
        take = self.first if mine else jnp.logical_not(self.first)
        return jnp.where(take, array[..., : self.half], array[..., self.half :])

    def swap(self, array):
        return lax.ppermute(array, "grid", [(i, i ^ 1) for i in range(self.count)])

    def transform_z(self, density):
        return jnp.einsum("xyz,zl->xyl", density, self.table_z, precision=highest)

    def add(self, piece, at):
        mine, got = self.pick(piece, True), self.swap(self.pick(piece, False))
        both = jnp.where(
            self.first, jnp.concatenate([mine, got]), jnp.concatenate([got, mine])
        )
        rows = self.table_y[at : at + piece.shape[1]]
        self.total += jnp.einsum("xyl,yk->xkl", both, rows, precision=highest)

    def solve(self):
        shape = jax.ShapeDtypeStruct(self.r.shape, jnp.float32)
        vmem = pl.BlockSpec(memory_space=pltpu.VMEM)
        to_right, to_left = pl.pallas_call(
            moments_kernel,
            out_shape=(shape, shape),
            in_specs=[vmem] * 4,
            out_specs=(vmem, vmem),
            name="moments",
        )(self.total, self.low, self.high, self.r)
        far = []
        for k in self.hops:
            sent = jnp.where((self.chip ^ k) > self.chip, to_right, to_left)
            far.append(
                lax.ppermute(sent, "grid", [(i, i ^ (2 * k)) for i in range(self.count)])
            )
        field = pl.pallas_call(
            functools.partial(solve_kernel, len(far)),
            out_shape=jax.ShapeDtypeStruct(self.total.shape, jnp.float32),
            in_specs=[pl.BlockSpec(memory_space=pltpu.SMEM)] + [vmem] * (5 + 2 * len(far)),
            out_specs=vmem,
            name="solve",
        )(self.side, self.total, self.low, self.high, self.r, self.scale, *far, *self.decay)
        field = jnp.einsum("xkl,ky->xyl", field, self.table_y, precision=highest)
        lower, upper = field[: self.planes], field[self.planes :]
        mine = jnp.where(self.first, lower, upper)
        got = self.swap(jnp.where(self.first, upper, lower))
        flip = lambda mine: self.pick(self.table_z.T, mine).T
        back = lambda part, table: jnp.einsum("xyl,lz->xyz", part, table, precision=highest)
        return back(mine, flip(True)) + back(got, flip(False))


def scatter_sum(value, axis):
    count = lax.axis_size(axis)
    place = lax.axis_index(axis)
    step = count // 2
    while step:
        half = value.shape[0] // 2
        upper = (place // step) % 2 == 1
        low, high = value[:half], value[half:]
        pairs = [(i, i ^ step) for i in range(count)]
        sent = lax.ppermute(jnp.where(upper, low, high), axis, pairs)
        value = jnp.where(upper, high, low) + sent
        step //= 2
    return value


def on_device(vectors, potential, added_field, qp_states):
    own = vectors.reshape((-1,) + vectors.shape[3:])
    added = added_field[0]
    count = lax.axis_size("grid")
    groups = lax.axis_size("grp")
    place = lax.axis_index("grid")
    n_fields, planes, size_y, size_z = own.shape
    assert planes == ORDER and n_fields == 6
    assert count % 2 == 0
    mask = jnp.stack([place > 0, place < count - 1]).astype(jnp.float32)
    even = place % 2 == 0
    flags = jnp.stack([even, jnp.logical_not(even)]).astype(jnp.int32)
    mate_pairs = [(i, i ^ 1) for i in range(count)]
    chip_pairs = []
    for i in range(1, count - 1, 2):
        chip_pairs += [(i, i + 1), (i + 1, i)]
    relayed = count == 8
    left, right = count // 2 - 1, count // 2
    first_leg = [(left, count - 1), (right, 0)]
    second_leg = [(count - 1, right), (0, left)]
    layout = spans(size_y, SHARES)
    split = 4

    def message(lo, hi):
        edge = lambda f: jnp.where(even, f[:-1, lo:hi], f[1:, lo:hi])
        parts = [own[split:, :, lo:hi].reshape(-1, hi - lo, size_z), edge(potential), edge(added)]
        return jnp.concatenate(parts)

    cut = layout[0][1][1]
    hops = [None] * len(layout)
    if relayed:
        hops[0] = lax.ppermute(message(0, cut), "grid", first_leg)
    messages = []
    mates = None
    for c, (_, (lo, hi), _) in enumerate(layout):
        block = own[:split, :, lo:hi].reshape(-1, hi - lo, size_z)
        direct = lax.ppermute(block, "grid", chip_pairs)
        rest, pairs = message(lo, hi), chip_pairs
        if mates is None:
            mates = [lax.ppermute(f, "grid", mate_pairs) for f in (own, potential, added)]
        if relayed:
            if c == 1:
                late = lax.ppermute(message(cut, size_y), "grid", first_leg)
                hops[1:] = [late[:, l - cut : h - cut] for _, (l, h), _ in layout[1:]]
            ends = jnp.logical_or(place == 0, place == count - 1)
            rest = jnp.where(ends, hops[c], rest)
            pairs = [p for p in chip_pairs if set(p) != {left, right}] + second_leg
        messages.append((direct, lax.ppermute(rest, "grid", pairs)))

    poisson = Poisson(planes, size_y, size_z)
    group_pairs = [(g, g + groups // 2) for g in range(groups // 2)]
    b, arrived = None, []
    for c, span in enumerate(layout):
        _, (lo, hi), window = span
        sources = []
        if c:
            before = layout[c - 1][1]
            sources.append((messages[c - 1], (window[0] - before[0], lo - window[0]), 0))
        sources.append((messages[c], (0, hi - lo), lo - window[0]))
        if c >= 2:
            b, arrived[c - 2] = lax.optimization_barrier((b, arrived[c - 2]))
        if c == len(layout) - 1:
            b, arrived[c - 1] = lax.optimization_barrier((b, arrived[c - 1]))
        b, rho = taylor(span, flags, mask, own, potential, added, mates, sources, b)
        arrived.append(lax.ppermute(poisson.transform_z(rho), "grp", group_pairs))
    for c, ((o0, _), _, _) in enumerate(layout):
        poisson.add(arrived[c], o0)
    received = poisson.solve()
    partial = elements(received, added, b, qp_states)
    return scatter_sum(partial, "grid")[None]


def solution(mesh):
    in_specs = (
        P("grp", None, None, "grid", None, None),
        P("grid", None, None),
        P("grp", "grid", None, None),
        P(None, "grid", None, None),
    )
    out_specs = P("grp", "grid", None)
    return jax.shard_map(
        on_device, mesh=mesh, in_specs=in_specs, out_specs=out_specs, check_vma=False
    )
```

```python
import functools

import jax
import jax.numpy as jnp
from jax import lax
from jax.experimental import pallas as pl
from jax.experimental.pallas import tpu as pltpu
from jax.sharding import PartitionSpec as P


ORDER = 4
LANES = 128
SUBS = 8
SHARES = (6, 10, 10, 6)

time_step = 0.2
four_pi = 12.566370614359172
highest = lax.Precision.HIGHEST


def sine_table(length, rows=None):
    indices = jnp.arange(length, dtype=jnp.int32) + 1
    rows = indices if rows is None else rows + 1
    products = rows[:, None] * indices[None, :] % (2 * (length + 1))
    return jnp.sqrt(2.0 / (length + 1)) * jnp.sin(
        jnp.pi * products.astype(jnp.float32) / (length + 1)
    )


def edge_rows(first, last):
    sub = lax.broadcasted_iota(jnp.int32, first.shape, 0)
    before = jnp.where(sub == 0, 0.0, pltpu.roll(last, 1, 0))
    after = jnp.where(sub == SUBS - 1, 0.0, pltpu.roll(first, SUBS - 1, 0))
    return before, after


def z_of(position, tiles):
    return tiles * (position % LANES) + position // LANES


def across_lanes(tiles):
    shape = tiles[0].shape
    axis = len(shape) - 1
    lane = lax.broadcasted_iota(jnp.int32, shape, axis)
    before = jnp.where(lane == 0, 0.0, pltpu.roll(tiles[-1], 1, axis))
    after = jnp.where(lane == LANES - 1, 0.0, pltpu.roll(tiles[0], LANES - 1, axis))
    line = [before] + tiles + [after]
    return [line[m] + line[m + 2] for m in range(len(tiles))]


def reorder_table(size_z, back=False):
    row = lax.broadcasted_iota(jnp.int32, (size_z, size_z), 0)
    col = lax.broadcasted_iota(jnp.int32, (size_z, size_z), 1)
    z, position = (col, row) if back else (row, col)
    return jnp.where(z == z_of(position, size_z // LANES), 1.0, 0.0).astype(jnp.bfloat16)


def reorder_kernel(own_ref, pot_ref, add_ref, own_out, pot_out, add_out, table):
    @pl.when(pl.program_id(0) == 0)
    def _():
        table[...] = reorder_table(table.shape[0])

    def reorder(value):
        total = None
        for _ in range(3):
            part = value.astype(jnp.bfloat16)
            value = value - part.astype(jnp.float32)
            moved = jnp.dot(part, table[...], preferred_element_type=jnp.float32)
            total = moved if total is None else total + moved
        return total

    for j in range(own_ref.shape[0]):
        own_out[j, 0] = reorder(own_ref[j, 0])
    pot_out[0] = reorder(pot_ref[0])
    add_out[0] = reorder(add_ref[0])


def reorder(own, potential, added, rows):
    n_fields, planes, _, size_z = own.shape
    full = pl.BlockSpec((n_fields, 1, rows, size_z), lambda p: (0, p, 0, 0))
    field = pl.BlockSpec((1, rows, size_z), lambda p: (p, 0, 0))
    shape = lambda *lead: jax.ShapeDtypeStruct(lead + (planes, rows, size_z), jnp.float32)
    return pl.pallas_call(
        reorder_kernel,
        grid=(planes,),
        out_shape=(shape(n_fields), shape(), shape()),
        in_specs=[full, field, field],
        out_specs=(full, field, field),
        scratch_shapes=[pltpu.VMEM((size_z, size_z), jnp.bfloat16)],
        name="reorder",
    )(own, potential, added)


def neighbour_sum(ref, lead, p, r0, n):
    block = ref[lead + (p, pl.ds(r0, n + 2))]
    x_low = ref[lead + (p - 1, pl.ds(r0 + 1, n))]
    x_high = ref[lead + (p + 1, pl.ds(r0 + 1, n))]
    centre = block[1:-1]
    plain = (block[2:] + block[:-2]) + (x_low + x_high)
    tiles = block.shape[-1] // LANES
    cut = lambda a, m: a[..., m * LANES : (m + 1) * LANES]
    z_sums = across_lanes([cut(centre, m) for m in range(tiles)])
    total = jnp.concatenate([cut(plain, m) + z_sums[m] for m in range(tiles)], axis=-1)
    return centre, total


def spans(size_y, shares):
    edges = [0]
    for share in shares:
        edges.append(edges[-1] + share * size_y // sum(shares))
    found, low = [], 0
    for o0, o1 in zip(edges[:-1], edges[1:]):
        high = min(o1 + SUBS, size_y)
        found.append(((o0, o1), (low, high), (max(o0 - SUBS, 0), high)))
        low = high
    return found


def pieces(rows):
    count = -(-rows // 5)
    sizes = [rows // count + (1 if j < rows % count else 0) for j in range(count)]
    starts = [sum(sizes[:j]) for j in range(count)]
    return list(zip(starts, sizes))


def taylor_kernel(
    span, sources, planes, first_call, flag_ref, mask_ref, own_ref, pot_ref, add_ref, mate_ref,
    mate_pot, mate_add, table_ref, *refs
):
    out_rows, _, window = span
    msgs, refs = refs[: 2 * len(sources)], refs[2 * len(sources) :]
    if not first_call:
        refs = refs[1:]
    b_ref, rho_out, x_in, f_in, b_out, r_out, u0, u1, u2, u3, w, acc, f_sems, x_sems, o_sems = refs
    s = 0.5 * time_step
    halo = ORDER
    tiles, n_fields = x_in.shape[:2]
    n_vectors = n_fields // 2
    height = window[1] - window[0]
    rows = height // SUBS
    reach = [planes + 2 * (halo - k) for k in range(ORDER + 1)]
    lanes = lambda m: pl.ds(m * LANES, LANES)

    def own_copies(source, target, sem):
        at = pl.ds(window[0], height)
        return [
            (pltpu.make_async_copy(source.at[:, at, lanes(m)], target(m, pl.ds(0, height)), sem()), None, None)
            for m in range(tiles)
        ]

    def halo_copies(side, p0, n, mate, target, sem):
        found = []
        for j, ((start, size), to) in enumerate(sources):
            ref, p = msgs[2 * j], p0
            if not isinstance(p0, int):
                ref, p = msgs[2 * j + 1], 0
            elif p0 >= ref.shape[0]:
                ref, p = msgs[2 * j + 1], p0 - ref.shape[0]
            first = mate.shape[0] - n if side == "low" else 0
            for m in range(tiles):
                goal, done = target(m, pl.ds(to, size)), sem()
                near = pltpu.make_async_copy(
                    mate.at[pl.ds(first, n), pl.ds(window[0] + to, size), lanes(m)], goal, done
                )
                far = pltpu.make_async_copy(
                    ref.at[pl.ds(p, n), pl.ds(start, size), lanes(m)], goal, done
                )
                found.append((near, far, flag_ref[0 if side == "low" else 1]))
        return found

    def counter(sems, first=0):
        used = [0]

        def sem():
            used[0] += 1
            return sems.at[first + used[0] - 1]

        return sem

    def field_copies():
        sem, found = counter(f_sems), []
        for which, (ref, mate) in enumerate(((pot_ref, mate_pot), (add_ref, mate_add))):
            p0 = n_fields * planes + which * (halo - 1)
            for side, to in (("low", 0), ("high", halo - 1 + planes)):
                goal = lambda m, at, to=to: f_in.at[m, which, pl.ds(to, halo - 1), at]
                found += halo_copies(side, p0, halo - 1, mate, goal, sem)
            goal = lambda m, at: f_in.at[m, which, pl.ds(halo - 1, planes), at]
            found += own_copies(ref, goal, sem)
        return found

    per_vector = x_sems.shape[0] // n_vectors

    def vector_copies(i):
        sem, found = counter(x_sems, i * per_vector), []
        for part in range(2):
            j = 2 * i + part
            for side, to in (("low", 0), ("high", halo + planes)):
                goal = lambda m, at, to=to: x_in.at[m, j, pl.ds(to, halo), at]
                found += halo_copies(side, j * planes, halo, mate_ref.at[j], goal, sem)
            goal = lambda m, at: x_in.at[m, j, pl.ds(halo, planes), at]
            found += own_copies(own_ref.at[j], goal, sem)
        return found

    def start(copies):
        for near, far, flag in copies:
            if far is None:
                near.start()
            else:
                pl.when(flag == 0)(near.start)
                pl.when(flag == 1)(far.start)

    def wait(copies):
        for near, _, _ in copies:
            near.wait()

    start(field_copies())
    for i in range(n_vectors):
        start(vector_copies(i))

    def gather(ref, lead, r):
        at = pl.ds(r, SUBS, stride=rows)
        return jnp.concatenate([ref[(m,) + lead + (at, slice(None))] for m in range(tiles)], axis=1)

    def scatter(ref, lead, r, value):
        at = pl.ds(r, SUBS, stride=rows)
        for m in range(tiles):
            ref[(m,) + lead + (at, slice(None))] = value[:, m * LANES : (m + 1) * LANES]

    wait(field_copies())

    def load_w(q, carry):
        for r in range(rows):
            pot = 2.0 * gather(f_in, (0, q), r) + 6.0
            w[0, q, r] = pot
            w[1, q, r] = pot + 2.0 * gather(f_in, (1, q), r)
        return carry

    lax.fori_loop(0, reach[1], load_w, 0)
    acc[...] = jnp.zeros_like(acc)

    def finish(ref, lead):
        before, after = edge_rows(ref[lead + (1,)], ref[lead + (rows,)])
        ref[lead + (0,)] = before
        ref[lead + (rows + 1,)] = after

    def inside(p, k):
        side = halo - k
        low = jnp.where(p < side, mask_ref[0], 1.0)
        return jnp.where(p >= side + planes, mask_ref[1], low)

    out_count = out_rows[1] - out_rows[0]
    inner = pl.ds(out_rows[0] - window[0], out_count)

    def b_copies(i):
        return [
            pltpu.make_async_copy(
                b_out.at[m, pl.ds(2 * i, 2), :, inner],
                b_ref.at[pl.ds(2 * i, 2), :, pl.ds(out_rows[0], out_count), lanes(m)],
                o_sems.at[i * tiles + m],
            )
            for m in range(tiles)
        ]

    def vector(i, carry):
        wait(vector_copies(i))

        def load_field(q, carry):
            for part in range(2):
                for r in range(rows):
                    u0[part, q, r + 1] = gather(x_in, (2 * i + part, q), r)
                finish(u0, (part, q))
            return carry

        lax.fori_loop(0, reach[0], load_field, 0)

        def order_1(p, carry):
            keep = inside(p, 1)
            for part in range(2):
                for r0, n in pieces(rows):
                    centre, total = neighbour_sum(u0, (part,), p + 1, r0, n)
                    for stack in range(2):
                        u1[2 * stack + part, p, pl.ds(r0 + 1, n)] = keep * (
                            total - w[stack, p, pl.ds(r0, n)] * centre
                        )
            for chain in range(4):
                finish(u1, (chain, p))
            return carry

        lax.fori_loop(0, reach[1], order_1, 0)
        for k, source, target in ((2, u1, u2), (3, u2, u3)):

            def order_k(p, carry, k=k, source=source, target=target):
                keep = inside(p, k)
                for chain in range(4):
                    for r0, n in pieces(rows):
                        centre, total = neighbour_sum(source, (chain,), p + 1, r0, n)
                        target[chain, p, pl.ds(r0 + 1, n)] = keep * (
                            total - w[chain // 2, p + k - 1, pl.ds(r0, n)] * centre
                        )
                    finish(target, (chain, p))
                return carry

            lax.fori_loop(0, reach[k], order_k, 0)

        def last(p, carry):
            for r0, n in pieces(rows):
                at = pl.ds(r0 + 1, n)
                plain = pl.ds(r0, n)
                rho = acc[p, plain]
                for stack in range(2):
                    ev, od = [], []
                    for part in range(2):
                        chain = 2 * stack + part
                        centre, total = neighbour_sum(u3, (chain,), p + 1, r0, n)
                        fourth = total - w[stack, p + 3, plain] * centre
                        ev.append(
                            u0[part, p + 4, at]
                            - (s**2 / 2) * u2[chain, p + 2, at]
                            + (s**4 / 24) * fourth
                        )
                        od.append(s * u1[chain, p + 3, at] - (s**3 / 6) * centre)
                    real, imag = ev[0] - od[1], od[0] + ev[1]
                    size = real * real + imag * imag
                    rho = rho + size if stack else rho - size
                acc[p, plain] = rho
                for j in range(n):
                    scatter(b_out, (2 * i, p), r0 + j, real[j])
                    scatter(b_out, (2 * i + 1, p), r0 + j, imag[j])
            return carry

        lax.fori_loop(0, planes, last, 0)
        for copy in b_copies(i):
            copy.start()
        return carry

    lax.fori_loop(0, n_vectors, vector, 0)

    def spread(p, carry):
        flat = acc[p].reshape(height, tiles * LANES)
        wave = jnp.dot(
            flat, table_ref[...], precision=highest, preferred_element_type=jnp.float32
        ).reshape(acc.shape[1:])
        for r in range(rows):
            scatter(r_out, (p,), r, wave[r])
        return carry

    lax.fori_loop(0, planes, spread, 0)
    out = [
        pltpu.make_async_copy(
            r_out.at[m, :, inner], rho_out.at[:, :, lanes(m)], o_sems.at[n_vectors * tiles + m]
        )
        for m in range(tiles)
    ]
    for copy in out:
        copy.start()
    for i in range(n_vectors):
        out += b_copies(i)
    for copy in out:
        copy.wait()


def taylor(span, flags, mask, own, potential, added, mates, table, sources, b):
    n_fields, planes, _, size_z = own.shape
    out_rows, _, window = span
    height = window[1] - window[0]
    rows = height // SUBS
    tiles = size_z // LANES
    held = lambda *lead: pltpu.VMEM(lead + (rows + 2, SUBS, size_z), jnp.float32)
    plain = lambda *lead: pltpu.VMEM(lead + (rows, SUBS, size_z), jnp.float32)
    natural = lambda *lead: pltpu.VMEM((tiles,) + lead + (height, LANES), jnp.float32)
    hbm = pl.BlockSpec(memory_space=pl.ANY)
    smem = pl.BlockSpec(memory_space=pltpu.SMEM)
    vmem = pl.BlockSpec(memory_space=pltpu.VMEM)
    shape = [(piece, to) for _, piece, to in sources]
    operands = [own, potential, added, *mates, table] + [m for msgs, _, _ in sources for m in msgs]
    aliases = {}
    if b is not None:
        operands.append(b)
        aliases = {2 + len(operands) - 1: 0}
    return pl.pallas_call(
        functools.partial(taylor_kernel, span, shape, planes, b is None),
        out_shape=(
            jax.ShapeDtypeStruct(own.shape, jnp.float32),
            jax.ShapeDtypeStruct((planes, out_rows[1] - out_rows[0], size_z), jnp.float32),
        ),
        in_specs=[smem, smem] + [hbm] * 6 + [vmem] + [hbm] * (len(operands) - 7),
        out_specs=(hbm, hbm),
        input_output_aliases=aliases,
        scratch_shapes=[
            natural(n_fields, planes + 8),
            natural(2, planes + 6),
            natural(n_fields, planes),
            natural(planes),
            held(2, planes + 8),
            held(4, planes + 6),
            held(4, planes + 4),
            held(4, planes + 2),
            plain(2, planes + 6),
            plain(planes),
            pltpu.SemaphoreType.DMA((tiles * (2 + 4 * len(sources)),)),
            pltpu.SemaphoreType.DMA((tiles * n_fields * (1 + 2 * len(sources)),)),
            pltpu.SemaphoreType.DMA((tiles * (n_fields // 2 + 1),)),
        ],
        cost_estimate=pl.CostEstimate(
            flops=rows * SUBS * size_z * planes * 120000, transcendentals=0, bytes_accessed=20 << 20
        ),
        name="taylor",
    )(flags, mask, *operands)


def elements_kernel(n_states, parts, last_step, rec_ref, add_ref, b_ref, q_ref, out_ref, acc, table):
    step = pl.program_id(0) * pl.num_programs(1) + pl.program_id(1)

    @pl.when(step == 0)
    def _():
        acc[...] = jnp.zeros_like(acc)
        table[...] = reorder_table(table.shape[0], back=True)

    field = rec_ref[0] + add_ref[0]
    group = 16
    total = acc[...]
    for g in range(field.shape[0] // group):
        at = slice(g * group, (g + 1) * group)
        weighted = [field[at] * b_ref[j, 0, at] for j in range(parts)]
        weighted = jnp.concatenate(weighted, axis=0).astype(jnp.bfloat16)
        weighted = jnp.dot(weighted, table[...], preferred_element_type=jnp.float32)
        weighted = weighted.astype(jnp.bfloat16)
        states = q_ref[:, 0, at].reshape(n_states * group, field.shape[-1])
        total += lax.dot_general(
            states, weighted, (((1,), (1,)), ((), ())), preferred_element_type=jnp.float32
        )
    acc[...] = total

    @pl.when(step == last_step)
    def _():
        found = acc[...].reshape(n_states, group, parts * group)
        row = lax.broadcasted_iota(jnp.int32, found.shape, 1)
        col = lax.broadcasted_iota(jnp.int32, found.shape, 2)
        own = jnp.sum(jnp.where(row == col % group, found, 0.0), axis=1)
        fold_r = lax.broadcasted_iota(jnp.int32, (parts * group, parts), 0)
        fold_c = lax.broadcasted_iota(jnp.int32, (parts * group, parts), 1)
        fold = jnp.where(fold_r // group == fold_c, 1.0, 0.0)
        out_ref[...] = jnp.dot(own, fold, precision=highest, preferred_element_type=jnp.float32)


def elements(received, added, b, states):
    n_states, planes, size_y, size_z = states.shape
    block = 64
    parts = b.shape[0]
    grid = (planes, size_y // block)
    field = pl.BlockSpec((1, block, size_z), lambda p, y: (p, y, 0))
    vec = pl.BlockSpec((parts, 1, block, size_z), lambda p, y: (0, p, y, 0))
    return pl.pallas_call(
        functools.partial(elements_kernel, n_states, parts, planes * (size_y // block) - 1),
        grid=grid,
        out_shape=jax.ShapeDtypeStruct((n_states, parts), jnp.float32),
        in_specs=[field, field]
        + [vec]
        + [pl.BlockSpec((n_states, 1, block, size_z), lambda p, y: (0, p, y, 0))],
        out_specs=pl.BlockSpec((n_states, parts), lambda p, y: (0, 0)),
        scratch_shapes=[
            pltpu.VMEM((n_states * 16, parts * 16), jnp.float32),
            pltpu.VMEM((size_z, size_z), jnp.bfloat16),
        ],
        name="elements",
    )(received, added, b, states)


def moments_kernel(f_ref, low_ref, high_ref, r_ref, to_right, to_left):
    planes = f_ref.shape[0]

    def step(q, carry):
        at = pl.ds(pl.multiple_of(q * SUBS, SUBS), SUBS)
        r = r_ref[at, :]
        up = low_ref[0, at, :] * f_ref[0, at, :]
        for j in range(1, planes):
            up = r * up + low_ref[j, at, :] * f_ref[j, at, :]
        down = high_ref[planes - 1, at, :] * f_ref[planes - 1, at, :]
        for j in range(planes - 2, -1, -1):
            down = r * down + high_ref[j, at, :] * f_ref[j, at, :]
        to_right[at, :] = up
        to_left[at, :] = down
        return carry

    lax.fori_loop(0, f_ref.shape[1] // SUBS, step, 0, unroll=4)


def solve_kernel(n_far, side_ref, f_ref, low_ref, high_ref, r_ref, scale_ref, *refs):
    far, decay, out = refs[:n_far], refs[n_far : 2 * n_far], refs[2 * n_far]
    planes = f_ref.shape[0]

    def step(q, carry):
        at = pl.ds(pl.multiple_of(q * SUBS, SUBS), SUBS)
        r = r_ref[at, :]
        up, down = jnp.zeros_like(r), jnp.zeros_like(r)
        for k in range(n_far):
            value = decay[k][at, :] * far[k][at, :]
            up = up + side_ref[k] * value
            down = down + (1.0 - side_ref[k]) * value
        below = []
        for j in range(planes):
            up = r * up + low_ref[j, at, :] * f_ref[j, at, :]
            below.append(up)
        for j in range(planes - 1, -1, -1):
            down = r * down
            out[j, at, :] = scale_ref[at, :] * (
                high_ref[j, at, :] * below[j] + low_ref[j, at, :] * down
            )
            down = down + high_ref[j, at, :] * f_ref[j, at, :]
        return carry

    lax.fori_loop(0, f_ref.shape[1] // SUBS, step, 0, unroll=2)


class Poisson:
    def __init__(self, planes, size_y, size_z):
        self.count = lax.axis_size("grid")
        self.place = lax.axis_index("grid")
        self.chip, self.core = self.place // 2, self.place % 2
        self.first = self.core == 0
        self.planes, self.half = planes, size_z // 2
        self.table_y = sine_table(size_y)
        at = jnp.arange(size_z, dtype=jnp.int32)
        self.table_z = sine_table(size_z, z_of(at, size_z // LANES))
        full_x = planes * self.count
        sine_half = lambda n: jnp.sin(
            (0.5 * jnp.pi / (n + 1)) * (jnp.arange(n, dtype=jnp.int32) + 1).astype(jnp.float32)
        )
        of_y = 4.0 * sine_half(size_y) ** 2
        of_z = self.pick(4.0 * sine_half(size_z) ** 2, True)
        mu = of_y[:, None] + of_z[None, :]
        root = jnp.sqrt(mu + 0.25 * mu * mu)
        theta = jnp.log1p(0.5 * mu + root)
        self.r = jnp.exp(-theta)
        x = (2 * planes * self.chip + jnp.arange(2 * planes)).astype(jnp.float32)[:, None, None]
        self.low = -jnp.expm1(-2.0 * theta * (x + 1.0))
        self.high = -jnp.expm1(-2.0 * theta * (full_x - x))
        self.scale = four_pi / (-2.0 * root * jnp.expm1(-2.0 * (full_x + 1) * theta))
        self.hops = list(range(1, self.count // 2))
        other = [self.chip ^ k for k in self.hops]
        self.side = jnp.stack([o < self.chip for o in other]).astype(jnp.float32)
        self.decay = [
            jnp.exp(-(2.0 * planes) * theta * (jnp.abs(o - self.chip) - 1).astype(jnp.float32))
            for o in other
        ]
        self.total = 0.0

    def pick(self, array, mine):
        take = self.first if mine else jnp.logical_not(self.first)
        return jnp.where(take, array[..., : self.half], array[..., self.half :])

    def swap(self, array):
        return lax.ppermute(array, "grid", [(i, i ^ 1) for i in range(self.count)])

    def add(self, piece, at):
        mine, got = self.pick(piece, True), self.swap(self.pick(piece, False))
        both = jnp.where(
            self.first, jnp.concatenate([mine, got]), jnp.concatenate([got, mine])
        )
        rows = self.table_y[at : at + piece.shape[1]]
        self.total += jnp.einsum("xyl,yk->xkl", both, rows, precision=highest)

    def solve(self):
        shape = jax.ShapeDtypeStruct(self.r.shape, jnp.float32)
        vmem = pl.BlockSpec(memory_space=pltpu.VMEM)
        to_right, to_left = pl.pallas_call(
            moments_kernel,
            out_shape=(shape, shape),
            in_specs=[vmem] * 4,
            out_specs=(vmem, vmem),
            name="moments",
        )(self.total, self.low, self.high, self.r)
        far = []
        for k in self.hops:
            sent = jnp.where((self.chip ^ k) > self.chip, to_right, to_left)
            far.append(
                lax.ppermute(sent, "grid", [(i, i ^ (2 * k)) for i in range(self.count)])
            )
        field = pl.pallas_call(
            functools.partial(solve_kernel, len(far)),
            out_shape=jax.ShapeDtypeStruct(self.total.shape, jnp.float32),
            in_specs=[pl.BlockSpec(memory_space=pltpu.SMEM)] + [vmem] * (5 + 2 * len(far)),
            out_specs=vmem,
            name="solve",
        )(self.side, self.total, self.low, self.high, self.r, self.scale, *far, *self.decay)
        field = jnp.einsum("xkl,ky->xyl", field, self.table_y, precision=highest)
        lower, upper = field[: self.planes], field[self.planes :]
        mine = jnp.where(self.first, lower, upper)
        got = self.swap(jnp.where(self.first, upper, lower))
        flip = lambda mine: self.pick(self.table_z, mine).T
        back = lambda part, table: jnp.einsum("xyl,lz->xyz", part, table, precision=highest)
        return back(mine, flip(True)) + back(got, flip(False))


def scatter_sum(value, axis):
    count = lax.axis_size(axis)
    place = lax.axis_index(axis)
    step = count // 2
    while step:
        half = value.shape[0] // 2
        upper = (place // step) % 2 == 1
        low, high = value[:half], value[half:]
        pairs = [(i, i ^ step) for i in range(count)]
        sent = lax.ppermute(jnp.where(upper, low, high), axis, pairs)
        value = jnp.where(upper, high, low) + sent
        step //= 2
    return value


def on_device(vectors, potential, added_field, qp_states):
    own = vectors.reshape((-1,) + vectors.shape[3:])
    count = lax.axis_size("grid")
    groups = lax.axis_size("grp")
    place = lax.axis_index("grid")
    n_fields, planes, size_y, size_z = own.shape
    assert planes == ORDER and n_fields == 6
    assert count % 2 == 0
    mask = jnp.stack([place > 0, place < count - 1]).astype(jnp.float32)
    even = place % 2 == 0
    flags = jnp.stack([even, jnp.logical_not(even)]).astype(jnp.int32)
    mate_pairs = [(i, i ^ 1) for i in range(count)]
    chip_pairs = []
    for i in range(1, count - 1, 2):
        chip_pairs += [(i, i + 1), (i + 1, i)]
    relayed = count == 8
    left, right = count // 2 - 1, count // 2
    first_leg = [(left, count - 1), (right, 0)]
    second_leg = [(count - 1, right), (0, left)]
    layout = spans(size_y, SHARES)
    split = 4

    def source(lo, hi):
        return start if (lo, hi) == first_rows else (own, potential, added)

    def message(lo, hi):
        vec, *parts = source(lo, hi)
        edge = lambda f: jnp.where(even, f[:-1, lo:hi], f[1:, lo:hi])
        block = vec[split:, :, lo:hi].reshape(-1, hi - lo, size_z)
        return jnp.concatenate([block] + [edge(f) for f in parts])

    start = reorder(own, potential, added_field[0], layout[0][1][1])
    own, potential, added = reorder(own, potential, added_field[0], size_y)
    first_rows = layout[0][1]
    hops = [None] * len(layout)
    if relayed:
        hops[0] = lax.ppermute(message(*first_rows), "grid", first_leg)
    messages = []
    mates = None
    for c, (_, (lo, hi), _) in enumerate(layout):
        block = source(lo, hi)[0][:split, :, lo:hi].reshape(-1, hi - lo, size_z)
        direct = lax.ppermute(block, "grid", chip_pairs)
        rest, pairs = message(lo, hi), chip_pairs
        if mates is None:
            mates = [lax.ppermute(f, "grid", mate_pairs) for f in (own, potential, added)]
        if relayed:
            if c == 1:
                hops[1] = lax.ppermute(message(lo, hi), "grid", first_leg)
            if c == 2:
                late = lax.ppermute(message(lo, size_y), "grid", first_leg)
                hops[2:] = [late[:, l - lo : h - lo] for _, (l, h), _ in layout[2:]]
            ends = jnp.logical_or(place == 0, place == count - 1)
            rest = jnp.where(ends, hops[c], rest)
            pairs = [p for p in chip_pairs if set(p) != {left, right}] + second_leg
        messages.append((direct, lax.ppermute(rest, "grid", pairs)))

    poisson = Poisson(planes, size_y, size_z)
    group_pairs = [(g, g + groups // 2) for g in range(groups // 2)]
    b, arrived = None, []
    for c, span in enumerate(layout):
        _, (lo, hi), window = span
        sources = []
        if c:
            before = layout[c - 1][1]
            sources.append((messages[c - 1], (window[0] - before[0], lo - window[0]), 0))
        sources.append((messages[c], (0, hi - lo), lo - window[0]))
        if c >= 2:
            b, arrived[c - 2] = lax.optimization_barrier((b, arrived[c - 2]))
        if c == len(layout) - 1:
            b, arrived[c - 1] = lax.optimization_barrier((b, arrived[c - 1]))
        b, rho = taylor(span, flags, mask, own, potential, added, mates, poisson.table_z, sources, b)
        arrived.append(lax.ppermute(rho, "grp", group_pairs))
    for c, ((o0, _), _, _) in enumerate(layout):
        poisson.add(arrived[c], o0)
    received = poisson.solve()
    partial = elements(received, added, b, qp_states)
    return scatter_sum(partial, "grid")[None]


def solution(mesh):
    in_specs = (
        P("grp", None, None, "grid", None, None),
        P("grid", None, None),
        P("grp", "grid", None, None),
        P(None, "grid", None, None),
    )
    out_specs = P("grp", "grid", None)
    return jax.shard_map(
        on_device, mesh=mesh, in_specs=in_specs, out_specs=out_specs, check_vma=False
    )
```

```python
import functools

import jax
import jax.numpy as jnp
from jax import lax
from jax.experimental import pallas as pl
from jax.experimental.pallas import tpu as pltpu
from jax.sharding import PartitionSpec as P


ORDER = 4
LANES = 128
SUBS = 8
SHARES = (6, 11, 11, 4)
AHEAD = 2

time_step = 0.2
four_pi = 12.566370614359172
highest = lax.Precision.HIGHEST


def sine_table(length):
    indices = jnp.arange(length, dtype=jnp.int32) + 1
    products = indices[:, None] * indices[None, :] % (2 * (length + 1))
    return jnp.sqrt(2.0 / (length + 1)) * jnp.sin(
        jnp.pi * products.astype(jnp.float32) / (length + 1)
    )


def edge_rows(first, last):
    sub = lax.broadcasted_iota(jnp.int32, first.shape, 0)
    before = jnp.where(sub == 0, 0.0, pltpu.roll(last, 1, 0))
    after = jnp.where(sub == SUBS - 1, 0.0, pltpu.roll(first, SUBS - 1, 0))
    return before, after


def across_lanes(tiles):
    shape = tiles[0].shape
    lane = lax.broadcasted_iota(jnp.int32, shape, len(shape) - 1)
    up = [pltpu.roll(t, 1, len(shape) - 1) for t in tiles]
    down = [pltpu.roll(t, LANES - 1, len(shape) - 1) for t in tiles]
    sums = []
    for m in range(len(tiles)):
        low = up[m - 1] if m > 0 else 0.0
        high = down[m + 1] if m < len(tiles) - 1 else 0.0
        sums.append(
            jnp.where(lane == 0, low, up[m]) + jnp.where(lane == LANES - 1, high, down[m])
        )
    return sums


def neighbour_sum(ref, lead, p, r0, n):
    block = ref[lead + (p, pl.ds(r0, n + 2))]
    x_low = ref[lead + (p - 1, pl.ds(r0 + 1, n))]
    x_high = ref[lead + (p + 1, pl.ds(r0 + 1, n))]
    centre = block[1:-1]
    plain = (block[2:] + block[:-2]) + (x_low + x_high)
    tiles = block.shape[-1] // LANES
    cut = lambda a, m: a[..., m * LANES : (m + 1) * LANES]
    z_sums = across_lanes([cut(centre, m) for m in range(tiles)])
    total = jnp.concatenate([cut(plain, m) + z_sums[m] for m in range(tiles)], axis=-1)
    return centre, total


def spans(size_y, shares):
    edges = [0]
    for share in shares:
        edges.append(edges[-1] + share * size_y // sum(shares))
    found, low = [], 0
    for o0, o1 in zip(edges[:-1], edges[1:]):
        high = min(o1 + SUBS, size_y)
        found.append(((o0, o1), (low, high), (max(o0 - SUBS, 0), high)))
        low = high
    return found


def pieces(rows):
    count = -(-rows // 5)
    sizes = [rows // count + (1 if j < rows % count else 0) for j in range(count)]
    starts = [sum(sizes[:j]) for j in range(count)]
    return list(zip(starts, sizes))


def taylor_kernel(
    span, sources, planes, first_call, flag_ref, mask_ref, own_ref, pot_ref, add_ref, mate_ref,
    mate_pot, mate_add, table_ref, *refs
):
    out_rows, _, window = span
    msgs, refs = refs[: 2 * len(sources)], refs[2 * len(sources) :]
    if not first_call:
        refs = refs[1:]
    b_ref, rho_out, x_in, f_in, b_out, r_out, u0, u1, u2, u3, w, acc, f_sems, x_sems, o_sems = refs
    s = 0.5 * time_step
    halo = ORDER
    tiles, n_fields = x_in.shape[:2]
    n_vectors = n_fields // 2
    height = window[1] - window[0]
    rows = height // SUBS
    reach = [planes + 2 * (halo - k) for k in range(ORDER + 1)]
    lanes = lambda m: pl.ds(m * LANES, LANES)

    def own_copies(source, target, sem):
        at = pl.ds(window[0], height)
        return [
            (pltpu.make_async_copy(source.at[:, at, lanes(m)], target(m, pl.ds(0, height)), sem()), None, None)
            for m in range(tiles)
        ]

    def halo_copies(side, p0, n, mate, target, sem):
        found = []
        for j, ((start, size), to) in enumerate(sources):
            ref, p = msgs[2 * j], p0
            if not isinstance(p0, int):
                ref, p = msgs[2 * j + 1], 0
            elif p0 >= ref.shape[0]:
                ref, p = msgs[2 * j + 1], p0 - ref.shape[0]
            first = mate.shape[0] - n if side == "low" else 0
            for m in range(tiles):
                goal, done = target(m, pl.ds(to, size)), sem()
                near = pltpu.make_async_copy(
                    mate.at[pl.ds(first, n), pl.ds(window[0] + to, size), lanes(m)], goal, done
                )
                far = pltpu.make_async_copy(
                    ref.at[pl.ds(p, n), pl.ds(start, size), lanes(m)], goal, done
                )
                found.append((near, far, flag_ref[0 if side == "low" else 1]))
        return found

    def counter(sems, first=0):
        used = [0]

        def sem():
            used[0] += 1
            return sems.at[first + used[0] - 1]

        return sem

    def field_copies():
        sem, found = counter(f_sems), []
        for which, (ref, mate) in enumerate(((pot_ref, mate_pot), (add_ref, mate_add))):
            p0 = n_fields * planes + which * (halo - 1)
            for side, to in (("low", 0), ("high", halo - 1 + planes)):
                goal = lambda m, at, to=to: f_in.at[m, which, pl.ds(to, halo - 1), at]
                found += halo_copies(side, p0, halo - 1, mate, goal, sem)
            goal = lambda m, at: f_in.at[m, which, pl.ds(halo - 1, planes), at]
            found += own_copies(ref, goal, sem)
        return found

    per_vector = x_sems.shape[0] // n_vectors

    def vector_copies(i):
        sem, found = counter(x_sems, i * per_vector), []
        for part in range(2):
            j = 2 * i + part
            for side, to in (("low", 0), ("high", halo + planes)):
                goal = lambda m, at, to=to: x_in.at[m, j, pl.ds(to, halo), at]
                found += halo_copies(side, j * planes, halo, mate_ref.at[j], goal, sem)
            goal = lambda m, at: x_in.at[m, j, pl.ds(halo, planes), at]
            found += own_copies(own_ref.at[j], goal, sem)
        return found

    def start(copies):
        for near, far, flag in copies:
            if far is None:
                near.start()
            else:
                pl.when(flag == 0)(near.start)
                pl.when(flag == 1)(far.start)

    def wait(copies):
        for near, _, _ in copies:
            near.wait()

    start(field_copies())
    for i in range(n_vectors):
        start(vector_copies(i))

    def gather(ref, lead, r):
        at = pl.ds(r, SUBS, stride=rows)
        return jnp.concatenate([ref[(m,) + lead + (at, slice(None))] for m in range(tiles)], axis=1)

    def scatter(ref, lead, r, value):
        at = pl.ds(r, SUBS, stride=rows)
        for m in range(tiles):
            ref[(m,) + lead + (at, slice(None))] = value[:, m * LANES : (m + 1) * LANES]

    wait(field_copies())

    def load_w(q, carry):
        for r in range(rows):
            pot = 2.0 * gather(f_in, (0, q), r) + 6.0
            w[0, q, r] = pot
            w[1, q, r] = pot + 2.0 * gather(f_in, (1, q), r)
        return carry

    lax.fori_loop(0, reach[1], load_w, 0)
    acc[...] = jnp.zeros_like(acc)

    def finish(ref, lead):
        before, after = edge_rows(ref[lead + (1,)], ref[lead + (rows,)])
        ref[lead + (0,)] = before
        ref[lead + (rows + 1,)] = after

    def inside(p, k):
        side = halo - k
        low = jnp.where(p < side, mask_ref[0], 1.0)
        return jnp.where(p >= side + planes, mask_ref[1], low)

    out_count = out_rows[1] - out_rows[0]
    inner = pl.ds(out_rows[0] - window[0], out_count)

    def b_copies(i):
        return [
            pltpu.make_async_copy(
                b_out.at[m, pl.ds(2 * i, 2), :, inner],
                b_ref.at[pl.ds(2 * i, 2), :, pl.ds(out_rows[0], out_count), lanes(m)],
                o_sems.at[i * tiles + m],
            )
            for m in range(tiles)
        ]

    def vector(i, carry):
        wait(vector_copies(i))

        def load_field(q, carry):
            for part in range(2):
                for r in range(rows):
                    u0[part, q, r + 1] = gather(x_in, (2 * i + part, q), r)
                finish(u0, (part, q))
            return carry

        lax.fori_loop(0, reach[0], load_field, 0)

        def order_1(p, carry):
            keep = inside(p, 1)
            for part in range(2):
                for r0, n in pieces(rows):
                    centre, total = neighbour_sum(u0, (part,), p + 1, r0, n)
                    for stack in range(2):
                        u1[2 * stack + part, p, pl.ds(r0 + 1, n)] = keep * (
                            total - w[stack, p, pl.ds(r0, n)] * centre
                        )
            for chain in range(4):
                finish(u1, (chain, p))
            return carry

        lax.fori_loop(0, reach[1], order_1, 0)
        for k, source, target in ((2, u1, u2), (3, u2, u3)):

            def order_k(p, carry, k=k, source=source, target=target):
                keep = inside(p, k)
                for chain in range(4):
                    for r0, n in pieces(rows):
                        centre, total = neighbour_sum(source, (chain,), p + 1, r0, n)
                        target[chain, p, pl.ds(r0 + 1, n)] = keep * (
                            total - w[chain // 2, p + k - 1, pl.ds(r0, n)] * centre
                        )
                    finish(target, (chain, p))
                return carry

            lax.fori_loop(0, reach[k], order_k, 0)

        def last(p, carry):
            for r0, n in pieces(rows):
                at = pl.ds(r0 + 1, n)
                plain = pl.ds(r0, n)
                rho = acc[p, plain]
                for stack in range(2):
                    ev, od = [], []
                    for part in range(2):
                        chain = 2 * stack + part
                        centre, total = neighbour_sum(u3, (chain,), p + 1, r0, n)
                        fourth = total - w[stack, p + 3, plain] * centre
                        ev.append(
                            u0[part, p + 4, at]
                            - (s**2 / 2) * u2[chain, p + 2, at]
                            + (s**4 / 24) * fourth
                        )
                        od.append(s * u1[chain, p + 3, at] - (s**3 / 6) * centre)
                    real, imag = ev[0] - od[1], od[0] + ev[1]
                    size = real * real + imag * imag
                    rho = rho + size if stack else rho - size
                acc[p, plain] = rho
                for j in range(n):
                    scatter(b_out, (2 * i, p), r0 + j, real[j])
                    scatter(b_out, (2 * i + 1, p), r0 + j, imag[j])
            return carry

        lax.fori_loop(0, planes, last, 0)
        for copy in b_copies(i):
            copy.start()
        return carry

    lax.fori_loop(0, n_vectors, vector, 0)

    def spread(p, carry):
        flat = acc[p].reshape(height, tiles * LANES)
        wave = jnp.dot(
            flat, table_ref[...], precision=highest, preferred_element_type=jnp.float32
        ).reshape(acc.shape[1:])
        for r in range(rows):
            scatter(r_out, (p,), r, wave[r])
        return carry

    lax.fori_loop(0, planes, spread, 0)
    out = [
        pltpu.make_async_copy(
            r_out.at[m, :, inner], rho_out.at[:, :, lanes(m)], o_sems.at[n_vectors * tiles + m]
        )
        for m in range(tiles)
    ]
    for copy in out:
        copy.start()
    for i in range(n_vectors):
        out += b_copies(i)
    for copy in out:
        copy.wait()


def taylor(span, flags, mask, own, potential, added, mates, table, sources, b):
    n_fields, planes, _, size_z = own.shape
    out_rows, _, window = span
    height = window[1] - window[0]
    rows = height // SUBS
    tiles = size_z // LANES
    held = lambda *lead: pltpu.VMEM(lead + (rows + 2, SUBS, size_z), jnp.float32)
    plain = lambda *lead: pltpu.VMEM(lead + (rows, SUBS, size_z), jnp.float32)
    natural = lambda *lead: pltpu.VMEM((tiles,) + lead + (height, LANES), jnp.float32)
    hbm = pl.BlockSpec(memory_space=pl.ANY)
    smem = pl.BlockSpec(memory_space=pltpu.SMEM)
    vmem = pl.BlockSpec(memory_space=pltpu.VMEM)
    shape = [(piece, to) for _, piece, to in sources]
    operands = [own, potential, added, *mates, table] + [m for msgs, _, _ in sources for m in msgs]
    aliases = {}
    if b is not None:
        operands.append(b)
        aliases = {2 + len(operands) - 1: 0}
    return pl.pallas_call(
        functools.partial(taylor_kernel, span, shape, planes, b is None),
        out_shape=(
            jax.ShapeDtypeStruct(own.shape, jnp.float32),
            jax.ShapeDtypeStruct((planes, out_rows[1] - out_rows[0], size_z), jnp.float32),
        ),
        in_specs=[smem, smem] + [hbm] * 6 + [vmem] + [hbm] * (len(operands) - 7),
        out_specs=(hbm, hbm),
        input_output_aliases=aliases,
        scratch_shapes=[
            natural(n_fields, planes + 8),
            natural(2, planes + 6),
            natural(n_fields, planes),
            natural(planes),
            held(2, planes + 8),
            held(4, planes + 6),
            held(4, planes + 4),
            held(4, planes + 2),
            plain(2, planes + 6),
            plain(planes),
            pltpu.SemaphoreType.DMA((tiles * (2 + 4 * len(sources)),)),
            pltpu.SemaphoreType.DMA((tiles * n_fields * (1 + 2 * len(sources)),)),
            pltpu.SemaphoreType.DMA((tiles * (n_fields // 2 + 1),)),
        ],
        cost_estimate=pl.CostEstimate(
            flops=rows * SUBS * size_z * planes * 120000, transcendentals=0, bytes_accessed=20 << 20
        ),
        name="taylor",
    )(flags, mask, *operands)


def elements_kernel(n_states, parts, last_step, rec_ref, add_ref, b_ref, q_ref, out_ref, acc):
    step = pl.program_id(0) * pl.num_programs(1) + pl.program_id(1)

    @pl.when(step == 0)
    def _():
        acc[...] = jnp.zeros_like(acc)

    field = rec_ref[0] + add_ref[0]
    group = 16
    total = acc[...]
    for g in range(field.shape[0] // group):
        at = slice(g * group, (g + 1) * group)
        weighted = [field[at] * b_ref[j, 0, at] for j in range(parts)]
        weighted = jnp.concatenate(weighted, axis=0).astype(jnp.bfloat16)
        states = q_ref[:, 0, at].reshape(n_states * group, field.shape[-1])
        total += lax.dot_general(
            states, weighted, (((1,), (1,)), ((), ())), preferred_element_type=jnp.float32
        )
    acc[...] = total

    @pl.when(step == last_step)
    def _():
        found = acc[...].reshape(n_states, group, parts * group)
        row = lax.broadcasted_iota(jnp.int32, found.shape, 1)
        col = lax.broadcasted_iota(jnp.int32, found.shape, 2)
        own = jnp.sum(jnp.where(row == col % group, found, 0.0), axis=1)
        fold_r = lax.broadcasted_iota(jnp.int32, (parts * group, parts), 0)
        fold_c = lax.broadcasted_iota(jnp.int32, (parts * group, parts), 1)
        fold = jnp.where(fold_r // group == fold_c, 1.0, 0.0)
        out_ref[...] = jnp.dot(own, fold, precision=highest, preferred_element_type=jnp.float32)


def elements(received, added, b, states):
    n_states, planes, size_y, size_z = states.shape
    block = 64
    parts = b.shape[0]
    grid = (planes, size_y // block)
    field = pl.BlockSpec((1, block, size_z), lambda p, y: (p, y, 0))
    vec = pl.BlockSpec((parts, 1, block, size_z), lambda p, y: (0, p, y, 0))
    return pl.pallas_call(
        functools.partial(elements_kernel, n_states, parts, planes * (size_y // block) - 1),
        grid=grid,
        out_shape=jax.ShapeDtypeStruct((n_states, parts), jnp.float32),
        in_specs=[field, field]
        + [vec]
        + [pl.BlockSpec((n_states, 1, block, size_z), lambda p, y: (0, p, y, 0))],
        out_specs=pl.BlockSpec((n_states, parts), lambda p, y: (0, 0)),
        scratch_shapes=[pltpu.VMEM((n_states * 16, parts * 16), jnp.float32)],
        name="elements",
    )(received, added, b, states)


def moments_kernel(side_ref, f_ref, low_ref, high_ref, r_ref, *outs):
    planes = f_ref.shape[0]

    def step(q, carry):
        at = pl.ds(pl.multiple_of(q * SUBS, SUBS), SUBS)
        r = r_ref[at, :]
        up = low_ref[0, at, :] * f_ref[0, at, :]
        for j in range(1, planes):
            up = r * up + low_ref[j, at, :] * f_ref[j, at, :]
        down = high_ref[planes - 1, at, :] * f_ref[planes - 1, at, :]
        for j in range(planes - 2, -1, -1):
            down = r * down + high_ref[j, at, :] * f_ref[j, at, :]
        for k, out in enumerate(outs):
            out[at, :] = jnp.where(side_ref[k] > 0.5, down, up)
        return carry

    lax.fori_loop(0, f_ref.shape[1] // SUBS, step, 0, unroll=4)


def solve_kernel(n_far, side_ref, f_ref, low_ref, high_ref, r_ref, scale_ref, *refs):
    far, decay, out = refs[:n_far], refs[n_far : 2 * n_far], refs[2 * n_far]
    planes = f_ref.shape[0]

    def step(q, carry):
        at = pl.ds(pl.multiple_of(q * SUBS, SUBS), SUBS)
        r = r_ref[at, :]
        up, down = jnp.zeros_like(r), jnp.zeros_like(r)
        for k in range(n_far):
            value = decay[k][at, :] * far[k][at, :]
            up = up + side_ref[k] * value
            down = down + (1.0 - side_ref[k]) * value
        below = []
        for j in range(planes):
            up = r * up + low_ref[j, at, :] * f_ref[j, at, :]
            below.append(up)
        for j in range(planes - 1, -1, -1):
            down = r * down
            out[j, at, :] = scale_ref[at, :] * (
                high_ref[j, at, :] * below[j] + low_ref[j, at, :] * down
            )
            down = down + high_ref[j, at, :] * f_ref[j, at, :]
        return carry

    lax.fori_loop(0, f_ref.shape[1] // SUBS, step, 0, unroll=2)


class Poisson:
    def __init__(self, planes, size_y, size_z):
        self.count = lax.axis_size("grid")
        self.place = lax.axis_index("grid")
        self.chip, self.core = self.place // 2, self.place % 2
        self.first = self.core == 0
        self.planes, self.half = planes, size_z // 2
        self.table_y, self.table_z = sine_table(size_y), sine_table(size_z)
        full_x = planes * self.count
        sine_half = lambda n: jnp.sin(
            (0.5 * jnp.pi / (n + 1)) * (jnp.arange(n, dtype=jnp.int32) + 1).astype(jnp.float32)
        )
        of_y = 4.0 * sine_half(size_y) ** 2
        of_z = self.pick(4.0 * sine_half(size_z) ** 2, True)
        mu = of_y[:, None] + of_z[None, :]
        root = jnp.sqrt(mu + 0.25 * mu * mu)
        theta = jnp.log1p(0.5 * mu + root)
        self.r = jnp.exp(-theta)
        x = (2 * planes * self.chip + jnp.arange(2 * planes)).astype(jnp.float32)[:, None, None]
        self.low = -jnp.expm1(-2.0 * theta * (x + 1.0))
        self.high = -jnp.expm1(-2.0 * theta * (full_x - x))
        self.scale = four_pi / (-2.0 * root * jnp.expm1(-2.0 * (full_x + 1) * theta))
        self.hops = list(range(1, self.count // 2))
        other = [self.chip ^ k for k in self.hops]
        self.side = jnp.stack([o < self.chip for o in other]).astype(jnp.float32)
        self.decay = [
            jnp.exp(-(2.0 * planes) * theta * (jnp.abs(o - self.chip) - 1).astype(jnp.float32))
            for o in other
        ]
        self.total = 0.0

    def pick(self, array, mine):
        take = self.first if mine else jnp.logical_not(self.first)
        return jnp.where(take, array[..., : self.half], array[..., self.half :])

    def swap(self, array):
        return lax.ppermute(array, "grid", [(i, i ^ 1) for i in range(self.count)])

    def add(self, piece, at):
        mine, got = self.pick(piece, True), self.swap(self.pick(piece, False))
        both = jnp.where(
            self.first, jnp.concatenate([mine, got]), jnp.concatenate([got, mine])
        )
        rows = self.table_y[at : at + piece.shape[1]]
        self.total += jnp.einsum("xyl,yk->xkl", both, rows, precision=highest)

    def solve(self):
        shape = jax.ShapeDtypeStruct(self.r.shape, jnp.float32)
        vmem = pl.BlockSpec(memory_space=pltpu.VMEM)
        smem = pl.BlockSpec(memory_space=pltpu.SMEM)
        sums = pl.pallas_call(
            moments_kernel,
            out_shape=[shape] * len(self.hops),
            in_specs=[smem] + [vmem] * 4,
            out_specs=[vmem] * len(self.hops),
            name="moments",
        )(self.side, self.total, self.low, self.high, self.r)
        far = [
            lax.ppermute(sent, "grid", [(i, i ^ (2 * k)) for i in range(self.count)])
            for k, sent in zip(self.hops, sums)
        ]
        field = pl.pallas_call(
            functools.partial(solve_kernel, len(far)),
            out_shape=jax.ShapeDtypeStruct(self.total.shape, jnp.float32),
            in_specs=[pl.BlockSpec(memory_space=pltpu.SMEM)] + [vmem] * (5 + 2 * len(far)),
            out_specs=vmem,
            name="solve",
        )(self.side, self.total, self.low, self.high, self.r, self.scale, *far, *self.decay)
        field = jnp.einsum("xkl,ky->xyl", field, self.table_y, precision=highest)
        lower, upper = field[: self.planes], field[self.planes :]
        mine = jnp.where(self.first, lower, upper)
        got = self.swap(jnp.where(self.first, upper, lower))
        flip = lambda mine: self.pick(self.table_z.T, mine).T
        back = lambda part, table: jnp.einsum("xyl,lz->xyz", part, table, precision=highest)
        return back(mine, flip(True)) + back(got, flip(False))


def scatter_sum(value, axis):
    count = lax.axis_size(axis)
    place = lax.axis_index(axis)
    step = count // 2
    while step:
        half = value.shape[0] // 2
        upper = (place // step) % 2 == 1
        low, high = value[:half], value[half:]
        pairs = [(i, i ^ step) for i in range(count)]
        sent = lax.ppermute(jnp.where(upper, low, high), axis, pairs)
        value = jnp.where(upper, high, low) + sent
        step //= 2
    return value


def on_device(vectors, potential, added_field, qp_states):
    own = vectors.reshape((-1,) + vectors.shape[3:])
    added = added_field[0]
    count = lax.axis_size("grid")
    groups = lax.axis_size("grp")
    place = lax.axis_index("grid")
    n_fields, planes, size_y, size_z = own.shape
    assert planes == ORDER and n_fields == 6
    assert count % 2 == 0
    mask = jnp.stack([place > 0, place < count - 1]).astype(jnp.float32)
    even = place % 2 == 0
    flags = jnp.stack([even, jnp.logical_not(even)]).astype(jnp.int32)
    mate_pairs = [(i, i ^ 1) for i in range(count)]
    chip_pairs = []
    for i in range(1, count - 1, 2):
        chip_pairs += [(i, i + 1), (i + 1, i)]
    relayed = count == 8
    left, right = count // 2 - 1, count // 2
    first_leg = [(left, count - 1), (right, 0)]
    second_leg = [(count - 1, right), (0, left)]
    layout = spans(size_y, SHARES)
    split = 4

    def message(lo, hi):
        edge = lambda f: jnp.where(even, f[:-1, lo:hi], f[1:, lo:hi])
        parts = [own[split:, :, lo:hi].reshape(-1, hi - lo, size_z), edge(potential), edge(added)]
        return jnp.concatenate(parts)

    ends = jnp.logical_or(place == 0, place == count - 1)

    def exchange(c, after):
        lo, hi = layout[c][1]
        block = own
        if after is not None:
            block, _ = lax.optimization_barrier((own, after))
        block = block[:split, :, lo:hi].reshape(-1, hi - lo, size_z)
        direct = lax.ppermute(block, "grid", chip_pairs)
        rest, pairs = message(lo, hi), chip_pairs
        if relayed:
            hop = lax.ppermute(rest, "grid", first_leg)
            if after is not None:
                hop, _ = lax.optimization_barrier((hop, after))
            rest = jnp.where(ends, hop, rest)
            pairs = [p for p in chip_pairs if set(p) != {left, right}] + second_leg
        elif after is not None:
            rest, _ = lax.optimization_barrier((rest, after))
        return direct, lax.ppermute(rest, "grid", pairs)

    messages = [exchange(c, None) for c in range(AHEAD)]
    mates = [lax.ppermute(f, "grid", mate_pairs) for f in (own, potential, added)]
    poisson = Poisson(planes, size_y, size_z)
    group_pairs = [(g, g + groups // 2) for g in range(groups // 2)]
    b, arrived = None, []
    for c, span in enumerate(layout):
        _, (lo, hi), window = span
        sources = []
        if c:
            before = layout[c - 1][1]
            sources.append((messages[c - 1], (window[0] - before[0], lo - window[0]), 0))
        sources.append((messages[c], (0, hi - lo), lo - window[0]))
        if c >= 2:
            b, arrived[c - 2] = lax.optimization_barrier((b, arrived[c - 2]))
        if c == len(layout) - 1:
            b, arrived[c - 1] = lax.optimization_barrier((b, arrived[c - 1]))
        b, rho = taylor(span, flags, mask, own, potential, added, mates, poisson.table_z, sources, b)
        if c + AHEAD < len(layout):
            messages.append(exchange(c + AHEAD, rho))
        arrived.append(lax.ppermute(rho, "grp", group_pairs))
    for c, ((o0, _), _, _) in enumerate(layout):
        poisson.add(arrived[c], o0)
    received = poisson.solve()
    partial = elements(received, added, b, qp_states)
    return scatter_sum(partial, "grid")[None]


def solution(mesh):
    in_specs = (
        P("grp", None, None, "grid", None, None),
        P("grid", None, None),
        P("grp", "grid", None, None),
        P(None, "grid", None, None),
    )
    out_specs = P("grp", "grid", None)
    return jax.shard_map(
        on_device, mesh=mesh, in_specs=in_specs, out_specs=out_specs, check_vma=False
    )
```

```python
import functools

import jax
import jax.numpy as jnp
from jax import lax
from jax.experimental import pallas as pl
from jax.experimental.pallas import tpu as pltpu
from jax.sharding import PartitionSpec as P


ORDER = 4
LANES = 128
SUBS = 8
SHARES = (6, 10, 10, 6)
AHEAD = 2

time_step = 0.2
four_pi = 12.566370614359172
highest = lax.Precision.HIGHEST


def sine_table(length):
    indices = jnp.arange(length, dtype=jnp.int32) + 1
    products = indices[:, None] * indices[None, :] % (2 * (length + 1))
    return jnp.sqrt(2.0 / (length + 1)) * jnp.sin(
        jnp.pi * products.astype(jnp.float32) / (length + 1)
    )


def edge_rows(first, last):
    sub = lax.broadcasted_iota(jnp.int32, first.shape, 0)
    before = jnp.where(sub == 0, 0.0, pltpu.roll(last, 1, 0))
    after = jnp.where(sub == SUBS - 1, 0.0, pltpu.roll(first, SUBS - 1, 0))
    return before, after


def across_lanes(tiles):
    shape = tiles[0].shape
    lane = lax.broadcasted_iota(jnp.int32, shape, len(shape) - 1)
    up = [pltpu.roll(t, 1, len(shape) - 1) for t in tiles]
    down = [pltpu.roll(t, LANES - 1, len(shape) - 1) for t in tiles]
    sums = []
    for m in range(len(tiles)):
        low = up[m - 1] if m > 0 else 0.0
        high = down[m + 1] if m < len(tiles) - 1 else 0.0
        sums.append(
            jnp.where(lane == 0, low, up[m]) + jnp.where(lane == LANES - 1, high, down[m])
        )
    return sums


def neighbour_sum(ref, lead, p, r0, n):
    block = ref[lead + (p, pl.ds(r0, n + 2))]
    x_low = ref[lead + (p - 1, pl.ds(r0 + 1, n))]
    x_high = ref[lead + (p + 1, pl.ds(r0 + 1, n))]
    centre = block[1:-1]
    plain = (block[2:] + block[:-2]) + (x_low + x_high)
    tiles = block.shape[-1] // LANES
    cut = lambda a, m: a[..., m * LANES : (m + 1) * LANES]
    z_sums = across_lanes([cut(centre, m) for m in range(tiles)])
    total = jnp.concatenate([cut(plain, m) + z_sums[m] for m in range(tiles)], axis=-1)
    return centre, total


def spans(size_y, shares):
    edges = [0]
    for share in shares:
        edges.append(edges[-1] + share * size_y // sum(shares))
    found, low = [], 0
    for o0, o1 in zip(edges[:-1], edges[1:]):
        high = min(o1 + SUBS, size_y)
        found.append(((o0, o1), (low, high), (max(o0 - SUBS, 0), high)))
        low = high
    return found


def pieces(rows):
    count = -(-rows // 5)
    sizes = [rows // count + (1 if j < rows % count else 0) for j in range(count)]
    starts = [sum(sizes[:j]) for j in range(count)]
    return list(zip(starts, sizes))


def taylor_kernel(
    span, sources, planes, first_call, flag_ref, mask_ref, own_ref, pot_ref, add_ref, mate_ref,
    mate_pot, mate_add, table_ref, *refs
):
    out_rows, _, window = span
    msgs, refs = refs[: 2 * len(sources)], refs[2 * len(sources) :]
    if not first_call:
        refs = refs[1:]
    b_ref, rho_out, x_in, f_in, b_out, r_out, u0, u1, u2, u3, w, acc, f_sems, x_sems, o_sems = refs
    s = 0.5 * time_step
    halo = ORDER
    tiles, n_fields = x_in.shape[:2]
    n_vectors = n_fields // 2
    height = window[1] - window[0]
    rows = height // SUBS
    reach = [planes + 2 * (halo - k) for k in range(ORDER + 1)]
    lanes = lambda m: pl.ds(m * LANES, LANES)

    def own_copies(source, target, sem):
        at = pl.ds(window[0], height)
        return [
            (pltpu.make_async_copy(source.at[:, at, lanes(m)], target(m, pl.ds(0, height)), sem()), None, None)
            for m in range(tiles)
        ]

    def halo_copies(side, p0, n, mate, target, sem):
        found = []
        for j, ((start, size), to) in enumerate(sources):
            ref, p = msgs[2 * j], p0
            if not isinstance(p0, int):
                ref, p = msgs[2 * j + 1], 0
            elif p0 >= ref.shape[0]:
                ref, p = msgs[2 * j + 1], p0 - ref.shape[0]
            first = mate.shape[0] - n if side == "low" else 0
            for m in range(tiles):
                goal, done = target(m, pl.ds(to, size)), sem()
                near = pltpu.make_async_copy(
                    mate.at[pl.ds(first, n), pl.ds(window[0] + to, size), lanes(m)], goal, done
                )
                far = pltpu.make_async_copy(
                    ref.at[pl.ds(p, n), pl.ds(start, size), lanes(m)], goal, done
                )
                found.append((near, far, flag_ref[0 if side == "low" else 1]))
        return found

    def counter(sems, first=0):
        used = [0]

        def sem():
            used[0] += 1
            return sems.at[first + used[0] - 1]

        return sem

    def field_copies():
        sem, found = counter(f_sems), []
        for which, (ref, mate) in enumerate(((pot_ref, mate_pot), (add_ref, mate_add))):
            p0 = n_fields * planes + which * (halo - 1)
            for side, to in (("low", 0), ("high", halo - 1 + planes)):
                goal = lambda m, at, to=to: f_in.at[m, which, pl.ds(to, halo - 1), at]
                found += halo_copies(side, p0, halo - 1, mate, goal, sem)
            goal = lambda m, at: f_in.at[m, which, pl.ds(halo - 1, planes), at]
            found += own_copies(ref, goal, sem)
        return found

    per_vector = x_sems.shape[0] // n_vectors

    def vector_copies(i):
        sem, found = counter(x_sems, i * per_vector), []
        for part in range(2):
            j = 2 * i + part
            for side, to in (("low", 0), ("high", halo + planes)):
                goal = lambda m, at, to=to: x_in.at[m, j, pl.ds(to, halo), at]
                found += halo_copies(side, j * planes, halo, mate_ref.at[j], goal, sem)
            goal = lambda m, at: x_in.at[m, j, pl.ds(halo, planes), at]
            found += own_copies(own_ref.at[j], goal, sem)
        return found

    def start(copies):
        for near, far, flag in copies:
            if far is None:
                near.start()
            else:
                pl.when(flag == 0)(near.start)
                pl.when(flag == 1)(far.start)

    def wait(copies):
        for near, _, _ in copies:
            near.wait()

    start(field_copies())
    for i in range(n_vectors):
        start(vector_copies(i))

    def gather(ref, lead, r):
        at = pl.ds(r, SUBS, stride=rows)
        return jnp.concatenate([ref[(m,) + lead + (at, slice(None))] for m in range(tiles)], axis=1)

    def scatter(ref, lead, r, value):
        at = pl.ds(r, SUBS, stride=rows)
        for m in range(tiles):
            ref[(m,) + lead + (at, slice(None))] = value[:, m * LANES : (m + 1) * LANES]

    wait(field_copies())

    def load_w(q, carry):
        for r in range(rows):
            pot = 2.0 * gather(f_in, (0, q), r) + 6.0
            w[0, q, r] = pot
            w[1, q, r] = pot + 2.0 * gather(f_in, (1, q), r)
        return carry

    lax.fori_loop(0, reach[1], load_w, 0)
    acc[...] = jnp.zeros_like(acc)

    def finish(ref, lead):
        before, after = edge_rows(ref[lead + (1,)], ref[lead + (rows,)])
        ref[lead + (0,)] = before
        ref[lead + (rows + 1,)] = after

    def inside(p, k):
        side = halo - k
        low = jnp.where(p < side, mask_ref[0], 1.0)
        return jnp.where(p >= side + planes, mask_ref[1], low)

    out_count = out_rows[1] - out_rows[0]
    inner = pl.ds(out_rows[0] - window[0], out_count)

    def b_copies(i):
        return [
            pltpu.make_async_copy(
                b_out.at[m, pl.ds(2 * i, 2), :, inner],
                b_ref.at[pl.ds(2 * i, 2), :, pl.ds(out_rows[0], out_count), lanes(m)],
                o_sems.at[i * tiles + m],
            )
            for m in range(tiles)
        ]

    def vector(i, carry):
        wait(vector_copies(i))

        def load_field(q, carry):
            for part in range(2):
                for r in range(rows):
                    u0[part, q, r + 1] = gather(x_in, (2 * i + part, q), r)
                finish(u0, (part, q))
            return carry

        lax.fori_loop(0, reach[0], load_field, 0)

        def order_1(p, carry):
            keep = inside(p, 1)
            for part in range(2):
                for r0, n in pieces(rows):
                    centre, total = neighbour_sum(u0, (part,), p + 1, r0, n)
                    for stack in range(2):
                        u1[2 * stack + part, p, pl.ds(r0 + 1, n)] = keep * (
                            total - w[stack, p, pl.ds(r0, n)] * centre
                        )
            for chain in range(4):
                finish(u1, (chain, p))
            return carry

        lax.fori_loop(0, reach[1], order_1, 0, unroll=2)
        for k, source, target in ((2, u1, u2), (3, u2, u3)):

            def order_k(p, carry, k=k, source=source, target=target):
                keep = inside(p, k)
                for chain in range(4):
                    for r0, n in pieces(rows):
                        centre, total = neighbour_sum(source, (chain,), p + 1, r0, n)
                        target[chain, p, pl.ds(r0 + 1, n)] = keep * (
                            total - w[chain // 2, p + k - 1, pl.ds(r0, n)] * centre
                        )
                    finish(target, (chain, p))
                return carry

            lax.fori_loop(0, reach[k], order_k, 0, unroll=2)

        def last(p, carry):
            for r0, n in pieces(rows):
                at = pl.ds(r0 + 1, n)
                plain = pl.ds(r0, n)
                rho = acc[p, plain]
                for stack in range(2):
                    ev, od = [], []
                    for part in range(2):
                        chain = 2 * stack + part
                        centre, total = neighbour_sum(u3, (chain,), p + 1, r0, n)
                        fourth = total - w[stack, p + 3, plain] * centre
                        ev.append(
                            u0[part, p + 4, at]
                            - (s**2 / 2) * u2[chain, p + 2, at]
                            + (s**4 / 24) * fourth
                        )
                        od.append(s * u1[chain, p + 3, at] - (s**3 / 6) * centre)
                    real, imag = ev[0] - od[1], od[0] + ev[1]
                    size = real * real + imag * imag
                    rho = rho + size if stack else rho - size
                acc[p, plain] = rho
                for j in range(n):
                    scatter(b_out, (2 * i, p), r0 + j, real[j])
                    scatter(b_out, (2 * i + 1, p), r0 + j, imag[j])
            return carry

        lax.fori_loop(0, planes, last, 0, unroll=2)
        for copy in b_copies(i):
            copy.start()
        return carry

    lax.fori_loop(0, n_vectors, vector, 0)

    def spread(p, carry):
        flat = acc[p].reshape(height, tiles * LANES)
        wave = jnp.dot(
            flat, table_ref[...], precision=highest, preferred_element_type=jnp.float32
        ).reshape(acc.shape[1:])
        for r in range(rows):
            scatter(r_out, (p,), r, wave[r])
        return carry

    lax.fori_loop(0, planes, spread, 0, unroll=2)
    out = [
        pltpu.make_async_copy(
            r_out.at[m, :, inner], rho_out.at[:, :, lanes(m)], o_sems.at[n_vectors * tiles + m]
        )
        for m in range(tiles)
    ]
    for copy in out:
        copy.start()
    for i in range(n_vectors):
        out += b_copies(i)
    for copy in out:
        copy.wait()


def taylor(span, flags, mask, own, potential, added, mates, table, sources, b):
    n_fields, planes, _, size_z = own.shape
    out_rows, _, window = span
    height = window[1] - window[0]
    rows = height // SUBS
    tiles = size_z // LANES
    held = lambda *lead: pltpu.VMEM(lead + (rows + 2, SUBS, size_z), jnp.float32)
    plain = lambda *lead: pltpu.VMEM(lead + (rows, SUBS, size_z), jnp.float32)
    natural = lambda *lead: pltpu.VMEM((tiles,) + lead + (height, LANES), jnp.float32)
    hbm = pl.BlockSpec(memory_space=pl.ANY)
    smem = pl.BlockSpec(memory_space=pltpu.SMEM)
    vmem = pl.BlockSpec(memory_space=pltpu.VMEM)
    shape = [(piece, to) for _, piece, to in sources]
    operands = [own, potential, added, *mates, table] + [m for msgs, _, _ in sources for m in msgs]
    aliases = {}
    if b is not None:
        operands.append(b)
        aliases = {2 + len(operands) - 1: 0}
    return pl.pallas_call(
        functools.partial(taylor_kernel, span, shape, planes, b is None),
        out_shape=(
            jax.ShapeDtypeStruct(own.shape, jnp.float32),
            jax.ShapeDtypeStruct((planes, out_rows[1] - out_rows[0], size_z), jnp.float32),
        ),
        in_specs=[smem, smem] + [hbm] * 6 + [vmem] + [hbm] * (len(operands) - 7),
        out_specs=(hbm, hbm),
        input_output_aliases=aliases,
        scratch_shapes=[
            natural(n_fields, planes + 8),
            natural(2, planes + 6),
            natural(n_fields, planes),
            natural(planes),
            held(2, planes + 8),
            held(4, planes + 6),
            held(4, planes + 4),
            held(4, planes + 2),
            plain(2, planes + 6),
            plain(planes),
            pltpu.SemaphoreType.DMA((tiles * (2 + 4 * len(sources)),)),
            pltpu.SemaphoreType.DMA((tiles * n_fields * (1 + 2 * len(sources)),)),
            pltpu.SemaphoreType.DMA((tiles * (n_fields // 2 + 1),)),
        ],
        cost_estimate=pl.CostEstimate(
            flops=rows * SUBS * size_z * planes * 120000, transcendentals=0, bytes_accessed=20 << 20
        ),
        name="taylor",
    )(flags, mask, *operands)


def elements_kernel(n_states, parts, last_step, rec_ref, add_ref, b_ref, q_ref, out_ref, acc):
    step = pl.program_id(0) * pl.num_programs(1) + pl.program_id(1)

    @pl.when(step == 0)
    def _():
        acc[...] = jnp.zeros_like(acc)

    field = rec_ref[0] + add_ref[0]
    group = 16
    total = acc[...]
    for g in range(field.shape[0] // group):
        at = slice(g * group, (g + 1) * group)
        weighted = [field[at] * b_ref[j, 0, at] for j in range(parts)]
        weighted = jnp.concatenate(weighted, axis=0).astype(jnp.bfloat16)
        states = q_ref[:, 0, at].reshape(n_states * group, field.shape[-1])
        total += lax.dot_general(
            states, weighted, (((1,), (1,)), ((), ())), preferred_element_type=jnp.float32
        )
    acc[...] = total

    @pl.when(step == last_step)
    def _():
        found = acc[...].reshape(n_states, group, parts * group)
        row = lax.broadcasted_iota(jnp.int32, found.shape, 1)
        col = lax.broadcasted_iota(jnp.int32, found.shape, 2)
        own = jnp.sum(jnp.where(row == col % group, found, 0.0), axis=1)
        fold_r = lax.broadcasted_iota(jnp.int32, (parts * group, parts), 0)
        fold_c = lax.broadcasted_iota(jnp.int32, (parts * group, parts), 1)
        fold = jnp.where(fold_r // group == fold_c, 1.0, 0.0)
        out_ref[...] = jnp.dot(own, fold, precision=highest, preferred_element_type=jnp.float32)


def elements(received, added, b, states):
    n_states, planes, size_y, size_z = states.shape
    block = 64
    parts = b.shape[0]
    grid = (planes, size_y // block)
    field = pl.BlockSpec((1, block, size_z), lambda p, y: (p, y, 0))
    vec = pl.BlockSpec((parts, 1, block, size_z), lambda p, y: (0, p, y, 0))
    return pl.pallas_call(
        functools.partial(elements_kernel, n_states, parts, planes * (size_y // block) - 1),
        grid=grid,
        out_shape=jax.ShapeDtypeStruct((n_states, parts), jnp.float32),
        in_specs=[field, field]
        + [vec]
        + [pl.BlockSpec((n_states, 1, block, size_z), lambda p, y: (0, p, y, 0))],
        out_specs=pl.BlockSpec((n_states, parts), lambda p, y: (0, 0)),
        scratch_shapes=[pltpu.VMEM((n_states * 16, parts * 16), jnp.float32)],
        name="elements",
    )(received, added, b, states)


def moments_kernel(side_ref, f_ref, low_ref, high_ref, r_ref, *outs):
    planes = f_ref.shape[0]

    def step(q, carry):
        at = pl.ds(pl.multiple_of(q * SUBS, SUBS), SUBS)
        r = r_ref[at, :]
        up = low_ref[0, at, :] * f_ref[0, at, :]
        for j in range(1, planes):
            up = r * up + low_ref[j, at, :] * f_ref[j, at, :]
        down = high_ref[planes - 1, at, :] * f_ref[planes - 1, at, :]
        for j in range(planes - 2, -1, -1):
            down = r * down + high_ref[j, at, :] * f_ref[j, at, :]
        for k, out in enumerate(outs):
            out[at, :] = jnp.where(side_ref[k] > 0.5, down, up)
        return carry

    lax.fori_loop(0, f_ref.shape[1] // SUBS, step, 0, unroll=4)


def solve_kernel(n_far, side_ref, f_ref, low_ref, high_ref, r_ref, scale_ref, *refs):
    far, decay, out = refs[:n_far], refs[n_far : 2 * n_far], refs[2 * n_far]
    planes = f_ref.shape[0]

    def step(q, carry):
        at = pl.ds(pl.multiple_of(q * SUBS, SUBS), SUBS)
        r = r_ref[at, :]
        up, down = jnp.zeros_like(r), jnp.zeros_like(r)
        for k in range(n_far):
            value = decay[k][at, :] * far[k][at, :]
            up = up + side_ref[k] * value
            down = down + (1.0 - side_ref[k]) * value
        below = []
        for j in range(planes):
            up = r * up + low_ref[j, at, :] * f_ref[j, at, :]
            below.append(up)
        for j in range(planes - 1, -1, -1):
            down = r * down
            out[j, at, :] = scale_ref[at, :] * (
                high_ref[j, at, :] * below[j] + low_ref[j, at, :] * down
            )
            down = down + high_ref[j, at, :] * f_ref[j, at, :]
        return carry

    lax.fori_loop(0, f_ref.shape[1] // SUBS, step, 0, unroll=2)


class Poisson:
    def __init__(self, planes, size_y, size_z):
        self.count = lax.axis_size("grid")
        self.place = lax.axis_index("grid")
        self.chip, self.core = self.place // 2, self.place % 2
        self.first = self.core == 0
        self.planes, self.half = planes, size_z // 2
        self.table_y, self.table_z = sine_table(size_y), sine_table(size_z)
        full_x = planes * self.count
        sine_half = lambda n: jnp.sin(
            (0.5 * jnp.pi / (n + 1)) * (jnp.arange(n, dtype=jnp.int32) + 1).astype(jnp.float32)
        )
        of_y = 4.0 * sine_half(size_y) ** 2
        of_z = self.pick(4.0 * sine_half(size_z) ** 2, True)
        mu = of_y[:, None] + of_z[None, :]
        root = jnp.sqrt(mu + 0.25 * mu * mu)
        theta = jnp.log1p(0.5 * mu + root)
        self.r = jnp.exp(-theta)
        x = (2 * planes * self.chip + jnp.arange(2 * planes)).astype(jnp.float32)[:, None, None]
        self.low = -jnp.expm1(-2.0 * theta * (x + 1.0))
        self.high = -jnp.expm1(-2.0 * theta * (full_x - x))
        self.scale = four_pi / (-2.0 * root * jnp.expm1(-2.0 * (full_x + 1) * theta))
        self.hops = list(range(1, self.count // 2))
        other = [self.chip ^ k for k in self.hops]
        self.side = jnp.stack([o < self.chip for o in other]).astype(jnp.float32)
        self.decay = [
            jnp.exp(-(2.0 * planes) * theta * (jnp.abs(o - self.chip) - 1).astype(jnp.float32))
            for o in other
        ]
        self.total = 0.0

    def pick(self, array, mine):
        take = self.first if mine else jnp.logical_not(self.first)
        return jnp.where(take, array[..., : self.half], array[..., self.half :])

    def swap(self, array):
        return lax.ppermute(array, "grid", [(i, i ^ 1) for i in range(self.count)])

    def add(self, piece, at):
        mine, got = self.pick(piece, True), self.swap(self.pick(piece, False))
        both = jnp.where(
            self.first, jnp.concatenate([mine, got]), jnp.concatenate([got, mine])
        )
        rows = self.table_y[at : at + piece.shape[1]]
        self.total += jnp.einsum("xyl,yk->xkl", both, rows, precision=highest)

    def solve(self):
        shape = jax.ShapeDtypeStruct(self.r.shape, jnp.float32)
        vmem = pl.BlockSpec(memory_space=pltpu.VMEM)
        smem = pl.BlockSpec(memory_space=pltpu.SMEM)
        sums = pl.pallas_call(
            moments_kernel,
            out_shape=[shape] * len(self.hops),
            in_specs=[smem] + [vmem] * 4,
            out_specs=[vmem] * len(self.hops),
            name="moments",
        )(self.side, self.total, self.low, self.high, self.r)
        far = [
            lax.ppermute(sent, "grid", [(i, i ^ (2 * k)) for i in range(self.count)])
            for k, sent in zip(self.hops, sums)
        ]
        field = pl.pallas_call(
            functools.partial(solve_kernel, len(far)),
            out_shape=jax.ShapeDtypeStruct(self.total.shape, jnp.float32),
            in_specs=[pl.BlockSpec(memory_space=pltpu.SMEM)] + [vmem] * (5 + 2 * len(far)),
            out_specs=vmem,
            name="solve",
        )(self.side, self.total, self.low, self.high, self.r, self.scale, *far, *self.decay)
        field = jnp.einsum("xkl,ky->xyl", field, self.table_y, precision=highest)
        lower, upper = field[: self.planes], field[self.planes :]
        mine = jnp.where(self.first, lower, upper)
        got = self.swap(jnp.where(self.first, upper, lower))
        flip = lambda mine: self.pick(self.table_z.T, mine).T
        back = lambda part, table: jnp.einsum("xyl,lz->xyz", part, table, precision=highest)
        return back(mine, flip(True)) + back(got, flip(False))


def scatter_sum(value, axis):
    count = lax.axis_size(axis)
    place = lax.axis_index(axis)
    step = count // 2
    while step:
        half = value.shape[0] // 2
        upper = (place // step) % 2 == 1
        low, high = value[:half], value[half:]
        pairs = [(i, i ^ step) for i in range(count)]
        sent = lax.ppermute(jnp.where(upper, low, high), axis, pairs)
        value = jnp.where(upper, high, low) + sent
        step //= 2
    return value


def on_device(vectors, potential, added_field, qp_states):
    own = vectors.reshape((-1,) + vectors.shape[3:])
    added = added_field[0]
    count = lax.axis_size("grid")
    groups = lax.axis_size("grp")
    place = lax.axis_index("grid")
    n_fields, planes, size_y, size_z = own.shape
    assert planes == ORDER and n_fields == 6
    assert count % 2 == 0
    mask = jnp.stack([place > 0, place < count - 1]).astype(jnp.float32)
    even = place % 2 == 0
    flags = jnp.stack([even, jnp.logical_not(even)]).astype(jnp.int32)
    mate_pairs = [(i, i ^ 1) for i in range(count)]
    chip_pairs = []
    for i in range(1, count - 1, 2):
        chip_pairs += [(i, i + 1), (i + 1, i)]
    relayed = count == 8
    left, right = count // 2 - 1, count // 2
    first_leg = [(left, count - 1), (right, 0)]
    second_leg = [(count - 1, right), (0, left)]
    layout = spans(size_y, SHARES)
    split = 4

    def message(lo, hi):
        edge = lambda f: jnp.where(even, f[:-1, lo:hi], f[1:, lo:hi])
        parts = [own[split:, :, lo:hi].reshape(-1, hi - lo, size_z), edge(potential), edge(added)]
        return jnp.concatenate(parts)

    ends = jnp.logical_or(place == 0, place == count - 1)

    def exchange(c, after):
        lo, hi = layout[c][1]
        held = lambda a: a if after is None else lax.optimization_barrier((a, after))[0]
        block = own[:split, :, lo:hi].reshape(-1, hi - lo, size_z)
        rest, pairs = message(lo, hi), chip_pairs
        if relayed:
            hop = lax.ppermute(rest, "grid", first_leg)
            rest = jnp.where(ends, hop, rest)
            pairs = [p for p in chip_pairs if set(p) != {left, right}] + second_leg
        direct = lax.ppermute(held(block), "grid", chip_pairs)
        return direct, lax.ppermute(held(rest), "grid", pairs)

    messages = [exchange(c, None) for c in range(AHEAD)]
    mates = [lax.ppermute(f, "grid", mate_pairs) for f in (own, potential, added)]
    poisson = Poisson(planes, size_y, size_z)
    group_pairs = [(g, g + groups // 2) for g in range(groups // 2)]
    b, arrived = None, []
    for c, span in enumerate(layout):
        _, (lo, hi), window = span
        sources = []
        if c:
            before = layout[c - 1][1]
            sources.append((messages[c - 1], (window[0] - before[0], lo - window[0]), 0))
        sources.append((messages[c], (0, hi - lo), lo - window[0]))
        if c >= 2:
            b, arrived[c - 2] = lax.optimization_barrier((b, arrived[c - 2]))
        if c == len(layout) - 1:
            b, arrived[c - 1] = lax.optimization_barrier((b, arrived[c - 1]))
        b, rho = taylor(span, flags, mask, own, potential, added, mates, poisson.table_z, sources, b)
        if c + AHEAD < len(layout):
            messages.append(exchange(c + AHEAD, (messages[c + AHEAD - 1], rho)))
        arrived.append(lax.ppermute(rho, "grp", group_pairs))
    for c, ((o0, _), _, _) in enumerate(layout):
        poisson.add(arrived[c], o0)
    received = poisson.solve()
    partial = elements(received, added, b, qp_states)
    return scatter_sum(partial, "grid")[None]


def solution(mesh):
    in_specs = (
        P("grp", None, None, "grid", None, None),
        P("grid", None, None),
        P("grp", "grid", None, None),
        P(None, "grid", None, None),
    )
    out_specs = P("grp", "grid", None)
    return jax.shard_map(
        on_device, mesh=mesh, in_specs=in_specs, out_specs=out_specs, check_vma=False
    )
```

```python
import functools

import jax
import jax.numpy as jnp
from jax import lax
from jax.experimental import pallas as pl
from jax.experimental.pallas import tpu as pltpu
from jax.sharding import PartitionSpec as P


ORDER = 4
LANES = 128
SUBS = 8
SHARES = (6, 10, 10, 6)
AHEAD = 2

time_step = 0.2
four_pi = 12.566370614359172
highest = lax.Precision.HIGHEST


def sine_table(length):
    indices = jnp.arange(length, dtype=jnp.int32) + 1
    products = indices[:, None] * indices[None, :] % (2 * (length + 1))
    return jnp.sqrt(2.0 / (length + 1)) * jnp.sin(
        jnp.pi * products.astype(jnp.float32) / (length + 1)
    )


def edge_rows(first, last):
    sub = lax.broadcasted_iota(jnp.int32, first.shape, 0)
    before = jnp.where(sub == 0, 0.0, pltpu.roll(last, 1, 0))
    after = jnp.where(sub == SUBS - 1, 0.0, pltpu.roll(first, SUBS - 1, 0))
    return before, after


def across_lanes(tiles):
    shape = tiles[0].shape
    lane = lax.broadcasted_iota(jnp.int32, shape, len(shape) - 1)
    up = [pltpu.roll(t, 1, len(shape) - 1) for t in tiles]
    down = [pltpu.roll(t, LANES - 1, len(shape) - 1) for t in tiles]
    sums = []
    for m in range(len(tiles)):
        low = up[m - 1] if m > 0 else 0.0
        high = down[m + 1] if m < len(tiles) - 1 else 0.0
        sums.append(
            jnp.where(lane == 0, low, up[m]) + jnp.where(lane == LANES - 1, high, down[m])
        )
    return sums


def neighbour_sum(ref, lead, p, r0, n):
    block = ref[lead + (p, pl.ds(r0, n + 2))]
    x_low = ref[lead + (p - 1, pl.ds(r0 + 1, n))]
    x_high = ref[lead + (p + 1, pl.ds(r0 + 1, n))]
    centre = block[1:-1]
    plain = (block[2:] + block[:-2]) + (x_low + x_high)
    tiles = block.shape[-1] // LANES
    cut = lambda a, m: a[..., m * LANES : (m + 1) * LANES]
    z_sums = across_lanes([cut(centre, m) for m in range(tiles)])
    total = jnp.concatenate([cut(plain, m) + z_sums[m] for m in range(tiles)], axis=-1)
    return centre, total


def spans(size_y, shares):
    edges = [0]
    for share in shares:
        edges.append(edges[-1] + share * size_y // sum(shares))
    found, low = [], 0
    for o0, o1 in zip(edges[:-1], edges[1:]):
        high = min(o1 + SUBS, size_y)
        found.append(((o0, o1), (low, high), (max(o0 - SUBS, 0), high)))
        low = high
    return found


def pieces(rows):
    count = -(-rows // 5)
    sizes = [rows // count + (1 if j < rows % count else 0) for j in range(count)]
    starts = [sum(sizes[:j]) for j in range(count)]
    return list(zip(starts, sizes))


def taylor_kernel(
    span, sources, planes, first_call, flag_ref, mask_ref, own_ref, pot_ref, add_ref, mate_ref,
    mate_pot, mate_add, table_ref, *refs
):
    out_rows, _, window = span
    msgs, refs = refs[: 2 * len(sources)], refs[2 * len(sources) :]
    if not first_call:
        refs = refs[1:]
    b_ref, rho_out, x_in, f_in, b_out, r_out, u0, u1, u2, u3, w, acc, f_sems, x_sems, o_sems = refs
    s = 0.5 * time_step
    halo = ORDER
    tiles, n_fields = x_in.shape[:2]
    n_vectors = n_fields // 2
    height = window[1] - window[0]
    rows = height // SUBS
    reach = [planes + 2 * (halo - k) for k in range(ORDER + 1)]
    lanes = lambda m: pl.ds(m * LANES, LANES)

    def own_copies(source, target, sem):
        at = pl.ds(window[0], height)
        return [
            (pltpu.make_async_copy(source.at[:, at, lanes(m)], target(m, pl.ds(0, height)), sem()), None, None)
            for m in range(tiles)
        ]

    def halo_copies(side, p0, n, mate, target, sem):
        found = []
        for j, ((start, size), to) in enumerate(sources):
            ref, p = msgs[2 * j], p0
            if not isinstance(p0, int):
                ref, p = msgs[2 * j + 1], 0
            elif p0 >= ref.shape[0]:
                ref, p = msgs[2 * j + 1], p0 - ref.shape[0]
            first = mate.shape[0] - n if side == "low" else 0
            for m in range(tiles):
                goal, done = target(m, pl.ds(to, size)), sem()
                near = pltpu.make_async_copy(
                    mate.at[pl.ds(first, n), pl.ds(window[0] + to, size), lanes(m)], goal, done
                )
                far = pltpu.make_async_copy(
                    ref.at[pl.ds(p, n), pl.ds(start, size), lanes(m)], goal, done
                )
                found.append((near, far, flag_ref[0 if side == "low" else 1]))
        return found

    def counter(sems, first=0):
        used = [0]

        def sem():
            used[0] += 1
            return sems.at[first + used[0] - 1]

        return sem

    def field_copies():
        sem, found = counter(f_sems), []
        for which, (ref, mate) in enumerate(((pot_ref, mate_pot), (add_ref, mate_add))):
            p0 = n_fields * planes + which * (halo - 1)
            for side, to in (("low", 0), ("high", halo - 1 + planes)):
                goal = lambda m, at, to=to: f_in.at[m, which, pl.ds(to, halo - 1), at]
                found += halo_copies(side, p0, halo - 1, mate, goal, sem)
            goal = lambda m, at: f_in.at[m, which, pl.ds(halo - 1, planes), at]
            found += own_copies(ref, goal, sem)
        return found

    per_vector = x_sems.shape[0] // n_vectors

    def vector_copies(i):
        sem, found = counter(x_sems, i * per_vector), []
        for part in range(2):
            j = 2 * i + part
            for side, to in (("low", 0), ("high", halo + planes)):
                goal = lambda m, at, to=to: x_in.at[m, j, pl.ds(to, halo), at]
                found += halo_copies(side, j * planes, halo, mate_ref.at[j], goal, sem)
            goal = lambda m, at: x_in.at[m, j, pl.ds(halo, planes), at]
            found += own_copies(own_ref.at[j], goal, sem)
        return found

    def start(copies):
        for near, far, flag in copies:
            if far is None:
                near.start()
            else:
                pl.when(flag == 0)(near.start)
                pl.when(flag == 1)(far.start)

    def wait(copies):
        for near, _, _ in copies:
            near.wait()

    start(field_copies())
    for i in range(n_vectors):
        start(vector_copies(i))

    def gather(ref, lead, r):
        at = pl.ds(r, SUBS, stride=rows)
        return jnp.concatenate([ref[(m,) + lead + (at, slice(None))] for m in range(tiles)], axis=1)

    def scatter(ref, lead, r, value):
        at = pl.ds(r, SUBS, stride=rows)
        for m in range(tiles):
            ref[(m,) + lead + (at, slice(None))] = value[:, m * LANES : (m + 1) * LANES]

    wait(field_copies())

    def load_w(q, carry):
        for r in range(rows):
            pot = 2.0 * gather(f_in, (0, q), r) + 6.0
            w[0, q, r] = pot
            w[1, q, r] = pot + 2.0 * gather(f_in, (1, q), r)
        return carry

    lax.fori_loop(0, reach[1], load_w, 0)
    acc[...] = jnp.zeros_like(acc)

    def finish(ref, lead):
        before, after = edge_rows(ref[lead + (1,)], ref[lead + (rows,)])
        ref[lead + (0,)] = before
        ref[lead + (rows + 1,)] = after

    def inside(p, k):
        side = halo - k
        low = jnp.where(p < side, mask_ref[0], 1.0)
        return jnp.where(p >= side + planes, mask_ref[1], low)

    out_count = out_rows[1] - out_rows[0]
    inner = pl.ds(out_rows[0] - window[0], out_count)

    def b_copies(i):
        return [
            pltpu.make_async_copy(
                b_out.at[m, pl.ds(2 * i, 2), :, inner],
                b_ref.at[pl.ds(2 * i, 2), :, pl.ds(out_rows[0], out_count), lanes(m)],
                o_sems.at[i * tiles + m],
            )
            for m in range(tiles)
        ]

    def vector(i, carry):
        wait(vector_copies(i))

        def load_field(q, carry):
            for part in range(2):
                for r in range(rows):
                    u0[part, q, r + 1] = gather(x_in, (2 * i + part, q), r)
                finish(u0, (part, q))
            return carry

        lax.fori_loop(0, reach[0], load_field, 0)

        def order_1(p, carry):
            keep = inside(p, 1)
            for part in range(2):
                for r0, n in pieces(rows):
                    centre, total = neighbour_sum(u0, (part,), p + 1, r0, n)
                    for stack in range(2):
                        u1[2 * stack + part, p, pl.ds(r0 + 1, n)] = keep * (
                            total - w[stack, p, pl.ds(r0, n)] * centre
                        )
            for chain in range(4):
                finish(u1, (chain, p))
            return carry

        lax.fori_loop(0, reach[1], order_1, 0, unroll=2)
        for k, source, target in ((2, u1, u2), (3, u2, u3)):

            def order_k(p, carry, k=k, source=source, target=target):
                keep = inside(p, k)
                for chain in range(4):
                    for r0, n in pieces(rows):
                        centre, total = neighbour_sum(source, (chain,), p + 1, r0, n)
                        target[chain, p, pl.ds(r0 + 1, n)] = keep * (
                            total - w[chain // 2, p + k - 1, pl.ds(r0, n)] * centre
                        )
                    finish(target, (chain, p))
                return carry

            lax.fori_loop(0, reach[k], order_k, 0, unroll=2)

        def last(p, carry):
            for r0, n in pieces(rows):
                at = pl.ds(r0 + 1, n)
                plain = pl.ds(r0, n)
                rho = acc[p, plain]
                for stack in range(2):
                    ev, od = [], []
                    for part in range(2):
                        chain = 2 * stack + part
                        centre, total = neighbour_sum(u3, (chain,), p + 1, r0, n)
                        fourth = total - w[stack, p + 3, plain] * centre
                        ev.append(
                            u0[part, p + 4, at]
                            - (s**2 / 2) * u2[chain, p + 2, at]
                            + (s**4 / 24) * fourth
                        )
                        od.append(s * u1[chain, p + 3, at] - (s**3 / 6) * centre)
                    real, imag = ev[0] - od[1], od[0] + ev[1]
                    size = real * real + imag * imag
                    rho = rho + size if stack else rho - size
                acc[p, plain] = rho
                for j in range(n):
                    scatter(b_out, (2 * i, p), r0 + j, real[j])
                    scatter(b_out, (2 * i + 1, p), r0 + j, imag[j])
            return carry

        lax.fori_loop(0, planes, last, 0, unroll=2)
        for copy in b_copies(i):
            copy.start()
        return carry

    lax.fori_loop(0, n_vectors, vector, 0)

    def spread(p, carry):
        flat = acc[p].reshape(height, tiles * LANES)
        wave = jnp.dot(
            flat, table_ref[...], precision=highest, preferred_element_type=jnp.float32
        ).reshape(acc.shape[1:])
        for r in range(rows):
            scatter(r_out, (p,), r, wave[r])
        return carry

    lax.fori_loop(0, planes, spread, 0, unroll=2)
    out = [
        pltpu.make_async_copy(
            r_out.at[m, :, inner], rho_out.at[:, :, lanes(m)], o_sems.at[n_vectors * tiles + m]
        )
        for m in range(tiles)
    ]
    for copy in out:
        copy.start()
    for i in range(n_vectors):
        out += b_copies(i)
    for copy in out:
        copy.wait()


def taylor(span, flags, mask, own, potential, added, mates, table, sources, b):
    n_fields, planes, _, size_z = own.shape
    out_rows, _, window = span
    height = window[1] - window[0]
    rows = height // SUBS
    tiles = size_z // LANES
    held = lambda *lead: pltpu.VMEM(lead + (rows + 2, SUBS, size_z), jnp.float32)
    plain = lambda *lead: pltpu.VMEM(lead + (rows, SUBS, size_z), jnp.float32)
    natural = lambda *lead: pltpu.VMEM((tiles,) + lead + (height, LANES), jnp.float32)
    hbm = pl.BlockSpec(memory_space=pl.ANY)
    smem = pl.BlockSpec(memory_space=pltpu.SMEM)
    vmem = pl.BlockSpec(memory_space=pltpu.VMEM)
    shape = [(piece, to) for _, piece, to in sources]
    operands = [own, potential, added, *mates, table] + [m for msgs, _, _ in sources for m in msgs]
    aliases = {}
    if b is not None:
        operands.append(b)
        aliases = {2 + len(operands) - 1: 0}
    return pl.pallas_call(
        functools.partial(taylor_kernel, span, shape, planes, b is None),
        out_shape=(
            jax.ShapeDtypeStruct(own.shape, jnp.float32),
            jax.ShapeDtypeStruct((planes, out_rows[1] - out_rows[0], size_z), jnp.float32),
        ),
        in_specs=[smem, smem] + [hbm] * 6 + [vmem] + [hbm] * (len(operands) - 7),
        out_specs=(hbm, hbm),
        input_output_aliases=aliases,
        scratch_shapes=[
            natural(n_fields, planes + 8),
            natural(2, planes + 6),
            natural(n_fields, planes),
            natural(planes),
            held(2, planes + 8),
            held(4, planes + 6),
            held(4, planes + 4),
            held(4, planes + 2),
            plain(2, planes + 6),
            plain(planes),
            pltpu.SemaphoreType.DMA((tiles * (2 + 4 * len(sources)),)),
            pltpu.SemaphoreType.DMA((tiles * n_fields * (1 + 2 * len(sources)),)),
            pltpu.SemaphoreType.DMA((tiles * (n_fields // 2 + 1),)),
        ],
        cost_estimate=pl.CostEstimate(
            flops=rows * SUBS * size_z * planes * 120000, transcendentals=0, bytes_accessed=20 << 20
        ),
        name="taylor",
    )(flags, mask, *operands)


def elements_kernel(n_states, parts, last_step, rec_ref, add_ref, b_ref, q_ref, out_ref, acc):
    step = pl.program_id(0) * pl.num_programs(1) + pl.program_id(1)

    @pl.when(step == 0)
    def _():
        acc[...] = jnp.zeros_like(acc)

    field = rec_ref[0] + add_ref[0]
    group = 16
    total = acc[...]
    for g in range(field.shape[0] // group):
        at = slice(g * group, (g + 1) * group)
        weighted = [field[at] * b_ref[j, 0, at] for j in range(parts)]
        weighted = jnp.concatenate(weighted, axis=0).astype(jnp.bfloat16)
        states = q_ref[:, 0, at].reshape(n_states * group, field.shape[-1])
        total += lax.dot_general(
            weighted, states, (((1,), (1,)), ((), ())), preferred_element_type=jnp.float32
        )
    acc[...] = total

    @pl.when(step == last_step)
    def _():
        found = acc[...].reshape(parts, group, n_states * group)
        row = lax.broadcasted_iota(jnp.int32, found.shape, 1)
        col = lax.broadcasted_iota(jnp.int32, found.shape, 2)
        own = jnp.sum(jnp.where(row == col % group, found, 0.0), axis=1)
        fold_r = lax.broadcasted_iota(jnp.int32, (n_states, n_states * group), 0)
        fold_c = lax.broadcasted_iota(jnp.int32, (n_states, n_states * group), 1)
        fold = jnp.where(fold_c // group == fold_r, 1.0, 0.0)
        out_ref[...] = lax.dot_general(
            fold, own, (((1,), (1,)), ((), ())), precision=highest, preferred_element_type=jnp.float32
        )


def elements(received, added, b, states):
    n_states, planes, size_y, size_z = states.shape
    block = 64
    parts = b.shape[0]
    grid = (planes, size_y // block)
    field = pl.BlockSpec((1, block, size_z), lambda p, y: (p, y, 0))
    vec = pl.BlockSpec((parts, 1, block, size_z), lambda p, y: (0, p, y, 0))
    return pl.pallas_call(
        functools.partial(elements_kernel, n_states, parts, planes * (size_y // block) - 1),
        grid=grid,
        out_shape=jax.ShapeDtypeStruct((n_states, parts), jnp.float32),
        in_specs=[field, field]
        + [vec]
        + [pl.BlockSpec((n_states, 1, block, size_z), lambda p, y: (0, p, y, 0))],
        out_specs=pl.BlockSpec((n_states, parts), lambda p, y: (0, 0)),
        scratch_shapes=[pltpu.VMEM((parts * 16, n_states * 16), jnp.float32)],
        name="elements",
    )(received, added, b, states)


def moments_kernel(side_ref, f_ref, low_ref, high_ref, r_ref, *outs):
    planes = f_ref.shape[0]

    def step(q, carry):
        at = pl.ds(pl.multiple_of(q * SUBS, SUBS), SUBS)
        r = r_ref[at, :]
        up = low_ref[0, at, :] * f_ref[0, at, :]
        for j in range(1, planes):
            up = r * up + low_ref[j, at, :] * f_ref[j, at, :]
        down = high_ref[planes - 1, at, :] * f_ref[planes - 1, at, :]
        for j in range(planes - 2, -1, -1):
            down = r * down + high_ref[j, at, :] * f_ref[j, at, :]
        for k, out in enumerate(outs):
            out[at, :] = jnp.where(side_ref[k] > 0.5, down, up)
        return carry

    lax.fori_loop(0, f_ref.shape[1] // SUBS, step, 0, unroll=4)


def solve_kernel(n_far, side_ref, f_ref, low_ref, high_ref, r_ref, scale_ref, *refs):
    far, decay, out = refs[:n_far], refs[n_far : 2 * n_far], refs[2 * n_far]
    planes = f_ref.shape[0]

    def step(q, carry):
        at = pl.ds(pl.multiple_of(q * SUBS, SUBS), SUBS)
        r = r_ref[at, :]
        up, down = jnp.zeros_like(r), jnp.zeros_like(r)
        for k in range(n_far):
            value = decay[k][at, :] * far[k][at, :]
            up = up + side_ref[k] * value
            down = down + (1.0 - side_ref[k]) * value
        below = []
        for j in range(planes):
            up = r * up + low_ref[j, at, :] * f_ref[j, at, :]
            below.append(up)
        for j in range(planes - 1, -1, -1):
            down = r * down
            out[j, at, :] = scale_ref[at, :] * (
                high_ref[j, at, :] * below[j] + low_ref[j, at, :] * down
            )
            down = down + high_ref[j, at, :] * f_ref[j, at, :]
        return carry

    lax.fori_loop(0, f_ref.shape[1] // SUBS, step, 0, unroll=2)


class Poisson:
    def __init__(self, planes, size_y, size_z):
        self.count = lax.axis_size("grid")
        self.place = lax.axis_index("grid")
        self.chip, self.core = self.place // 2, self.place % 2
        self.first = self.core == 0
        self.planes, self.half = planes, size_z // 2
        self.table_y, self.table_z = sine_table(size_y), sine_table(size_z)
        full_x = planes * self.count
        sine_half = lambda n: jnp.sin(
            (0.5 * jnp.pi / (n + 1)) * (jnp.arange(n, dtype=jnp.int32) + 1).astype(jnp.float32)
        )
        of_y = 4.0 * sine_half(size_y) ** 2
        of_z = self.pick(4.0 * sine_half(size_z) ** 2, True)
        mu = of_y[:, None] + of_z[None, :]
        root = jnp.sqrt(mu + 0.25 * mu * mu)
        theta = jnp.log1p(0.5 * mu + root)
        self.r = jnp.exp(-theta)
        x = (2 * planes * self.chip + jnp.arange(2 * planes)).astype(jnp.float32)[:, None, None]
        self.low = -jnp.expm1(-2.0 * theta * (x + 1.0))
        self.high = -jnp.expm1(-2.0 * theta * (full_x - x))
        self.scale = four_pi / (-2.0 * root * jnp.expm1(-2.0 * (full_x + 1) * theta))
        self.hops = list(range(1, self.count // 2))
        other = [self.chip ^ k for k in self.hops]
        self.side = jnp.stack([o < self.chip for o in other]).astype(jnp.float32)
        self.decay = [
            jnp.exp(-(2.0 * planes) * theta * (jnp.abs(o - self.chip) - 1).astype(jnp.float32))
            for o in other
        ]
        self.pieces = []

    def pick(self, array, mine):
        take = self.first if mine else jnp.logical_not(self.first)
        return jnp.where(take, array[..., : self.half], array[..., self.half :])

    def swap(self, array):
        return lax.ppermute(array, "grid", [(i, i ^ 1) for i in range(self.count)])

    def add(self, piece):
        mine, got = self.pick(piece, True), self.swap(self.pick(piece, False))
        both = jnp.where(
            self.first, jnp.concatenate([mine, got]), jnp.concatenate([got, mine])
        )
        self.pieces.append(both)

    def solve(self):
        whole = jnp.concatenate(self.pieces, axis=1)
        total = jnp.einsum("xyl,yk->xkl", whole, self.table_y, precision=highest)
        shape = jax.ShapeDtypeStruct(self.r.shape, jnp.float32)
        vmem = pl.BlockSpec(memory_space=pltpu.VMEM)
        smem = pl.BlockSpec(memory_space=pltpu.SMEM)
        sums = pl.pallas_call(
            moments_kernel,
            out_shape=[shape] * len(self.hops),
            in_specs=[smem] + [vmem] * 4,
            out_specs=[vmem] * len(self.hops),
            name="moments",
        )(self.side, total, self.low, self.high, self.r)
        far = [
            lax.ppermute(sent, "grid", [(i, i ^ (2 * k)) for i in range(self.count)])
            for k, sent in zip(self.hops, sums)
        ]
        field = pl.pallas_call(
            functools.partial(solve_kernel, len(far)),
            out_shape=jax.ShapeDtypeStruct(total.shape, jnp.float32),
            in_specs=[pl.BlockSpec(memory_space=pltpu.SMEM)] + [vmem] * (5 + 2 * len(far)),
            out_specs=vmem,
            name="solve",
        )(self.side, total, self.low, self.high, self.r, self.scale, *far, *self.decay)
        field = jnp.einsum("xkl,ky->xyl", field, self.table_y, precision=highest)
        lower, upper = field[: self.planes], field[self.planes :]
        mine = jnp.where(self.first, lower, upper)
        got = self.swap(jnp.where(self.first, upper, lower))
        flip = lambda mine: self.pick(self.table_z.T, mine).T
        back = lambda part, table: jnp.einsum("xyl,lz->xyz", part, table, precision=highest)
        return back(mine, flip(True)) + back(got, flip(False))


def scatter_sum(value):
    count = lax.axis_size("grid")
    place = lax.axis_index("grid")
    blocks = value.reshape(count // 2, 2, -1, value.shape[1])
    first = place % 2 == 0
    sent = jnp.where(first, blocks[:, 1], blocks[:, 0])
    mine = jnp.where(first, blocks[:, 0], blocks[:, 1])
    mine = mine + lax.ppermute(sent, "grid", [(i, i ^ 1) for i in range(count)])
    pick = lambda k: lax.dynamic_index_in_dim(mine, (place // 2) ^ k, 0, keepdims=False)
    total = pick(0)
    for k in range(1, count // 2):
        total = total + lax.ppermute(pick(k), "grid", [(i, i ^ (2 * k)) for i in range(count)])
    return total


def on_device(vectors, potential, added_field, qp_states):
    own = vectors.reshape((-1,) + vectors.shape[3:])
    added = added_field[0]
    count = lax.axis_size("grid")
    groups = lax.axis_size("grp")
    place = lax.axis_index("grid")
    n_fields, planes, size_y, size_z = own.shape
    assert planes == ORDER and n_fields == 6
    assert count % 2 == 0
    mask = jnp.stack([place > 0, place < count - 1]).astype(jnp.float32)
    even = place % 2 == 0
    flags = jnp.stack([even, jnp.logical_not(even)]).astype(jnp.int32)
    mate_pairs = [(i, i ^ 1) for i in range(count)]
    chip_pairs = []
    for i in range(1, count - 1, 2):
        chip_pairs += [(i, i + 1), (i + 1, i)]
    relayed = count == 8
    left, right = count // 2 - 1, count // 2
    first_leg = [(left, count - 1), (right, 0)]
    second_leg = [(count - 1, right), (0, left)]
    layout = spans(size_y, SHARES)
    split = 4

    def message(lo, hi):
        edge = lambda f: jnp.where(even, f[:-1, lo:hi], f[1:, lo:hi])
        parts = [own[split:, :, lo:hi].reshape(-1, hi - lo, size_z), edge(potential), edge(added)]
        return jnp.concatenate(parts)

    ends = jnp.logical_or(place == 0, place == count - 1)

    def exchange(c, after):
        lo, hi = layout[c][1]
        held = lambda a: a if after is None else lax.optimization_barrier((a, after))[0]
        block = own[:split, :, lo:hi].reshape(-1, hi - lo, size_z)
        rest, pairs = message(lo, hi), chip_pairs
        if relayed:
            hop = lax.ppermute(rest, "grid", first_leg)
            rest = jnp.where(ends, hop, rest)
            pairs = [p for p in chip_pairs if set(p) != {left, right}] + second_leg
        direct = lax.ppermute(held(block), "grid", chip_pairs)
        return direct, lax.ppermute(held(rest), "grid", pairs)

    messages = [exchange(c, None) for c in range(AHEAD)]
    mates = [lax.ppermute(f, "grid", mate_pairs) for f in (own, potential, added)]
    poisson = Poisson(planes, size_y, size_z)
    group_pairs = [(g, g + groups // 2) for g in range(groups // 2)]
    b, arrived = None, []
    for c, span in enumerate(layout):
        _, (lo, hi), window = span
        sources = []
        if c:
            before = layout[c - 1][1]
            sources.append((messages[c - 1], (window[0] - before[0], lo - window[0]), 0))
        sources.append((messages[c], (0, hi - lo), lo - window[0]))
        if c >= 2:
            b, arrived[c - 2] = lax.optimization_barrier((b, arrived[c - 2]))
        if c == len(layout) - 1:
            b, arrived[c - 1] = lax.optimization_barrier((b, arrived[c - 1]))
        b, rho = taylor(span, flags, mask, own, potential, added, mates, poisson.table_z, sources, b)
        if c + AHEAD < len(layout):
            after = (messages[c + AHEAD - 1], rho) if c == 0 else rho
            messages.append(exchange(c + AHEAD, after))
        arrived.append(lax.ppermute(rho, "grp", group_pairs))
    for c in range(len(layout)):
        poisson.add(arrived[c])
    received = poisson.solve()
    partial = elements(received, added, b, qp_states)
    return scatter_sum(partial)[None]


def solution(mesh):
    in_specs = (
        P("grp", None, None, "grid", None, None),
        P("grid", None, None),
        P("grp", "grid", None, None),
        P(None, "grid", None, None),
    )
    out_specs = P("grp", "grid", None)
    return jax.shard_map(
        on_device, mesh=mesh, in_specs=in_specs, out_specs=out_specs, check_vma=False
    )
```
